32 devices in a mesh: beam: 2 (over y), bin: 4 (over z), chan: 4 (over x, core).
Axes of the slice: x: 2, y: 2, z: 4, core: 2. Of those that a mesh axis runs over, the one named last changes fastest.
Arguments:
- spectra: bfloat16 [2, 8192, 1024], P(None, ('beam', 'chan', 'bin')), parts along dimension 1, may hold values from -6 to 6
- dm_trials: int32 [64], replicated, may hold values from 0 to 1023
- chan_delay: int32 [4096], replicated, may hold values from 0 to 32767
- template_bank: bfloat16 [2, 256, 256], replicated, may hold values from -0.25 to 0.25
- template_ids: int32 [128], replicated, may hold values from 0 to 255
Outputs:
- powers: bfloat16 [128, 128, 1024], P(('beam', 'chan'), None, 'bin'), parts along dimension 0
The draws below stay inside these ranges and needn't reach their ends.
There are 2 independent parts, one for each index of `beam`. The reference program is written for one: setup_inputs(seed, part) draws one part's arguments, and reference() takes and returns one part's arrays. A program takes and returns all parts, laid end to end along the dimension named above; an argument that names none is the same for every part. Nothing has to cross between parts.
All inputs are finite; a program needn't handle non-finite values.
Results may differ from the reference program's by a relative error of at most 0.0095.
Values may be sent and summed in bfloat16 or wider, within the bound.
A program may use at most 64 MiB of HBM per device.

```python
import math
import jax
import jax.numpy as jnp
from jax import lax

CHANS = 4096
TRIALS = 64
TEMPLATES = 128
BANK = 256
EDGE = 128
TAPS = 256
BINS = 1024


def touch_ends(drawn, key, smallest, largest):
    longest = drawn.shape.index(max(drawn.shape))
    spots = []
    for shift in (0, 1):
        where = [jax.random.randint(jax.random.fold_in(key, axis), (), 0, length) for axis, length in enumerate(drawn.shape)]
        where[longest] = (where[longest] + shift) % drawn.shape[longest]
        spots.append(tuple(where))
    return drawn.at[spots[0]].set(smallest).at[spots[1]].set(largest)


def shard_levels(rng, shape, cuts, low, largest):
    def one(dim, parts):
        draws = jax.random.uniform(jax.random.fold_in(jax.random.fold_in(rng, 6), dim), (parts,), jnp.float32, low / len(cuts), largest / len(cuts))
        return jnp.repeat(jnp.exp(draws), shape[dim] // parts).reshape((-1,) + (1,) * (len(shape) - dim - 1))

    level = one(*cuts[0])
    for cut in cuts[1:]:
        level = level * one(*cut)
    return level


def gaussian(stream_key, extent, width, bound, shards=(), kind=jnp.bfloat16):
    result = jax.random.normal(stream_key, extent, jnp.float32) * width
    if len(shards) > 0:
        result = shard_levels(stream_key, extent, shards, -0.22, 0.18) * result
    return jnp.clip(result, min=-bound, max=bound).astype(kind)


def setup_inputs(seed: int = 0, part: int = 0) -> dict:
    key_of = jax.random.split(jax.random.key(seed), 6)
    part_splits = jax.random.split(jax.random.fold_in(key_of[5], part), 6)
    return {
        "spectra": gaussian(part_splits[0], (2, CHANS, BINS), 1.0, 6.0, ((1, 16),)),
        "dm_trials": touch_ends(jax.random.randint(key_of[1], (TRIALS,), 0, 1024), jax.random.fold_in(key_of[1], 1), 0, 1023).astype(jnp.int32),
        "chan_delay": touch_ends(jax.random.randint(key_of[2], (CHANS,), 0, 32768), jax.random.fold_in(key_of[2], 1), 0, 32767).astype(jnp.int32),
        "template_bank": gaussian(key_of[3], (2, BANK, TAPS), (2 * TAPS) ** -0.5, 0.25),
        "template_ids": touch_ends(jax.random.randint(key_of[4], (TEMPLATES,), 0, BANK), jax.random.fold_in(key_of[4], 1), 0, BANK - 1).astype(jnp.int32),
    }


def reference(spectra, dm_trials, chan_delay, template_bank, template_ids):
    samples = 2 * BINS
    block_size = math.gcd(BINS, 32)
    delays = dm_trials[:, None] * chan_delay[None, :] % samples
    starts_list = jnp.arange(BINS // block_size, dtype=jnp.int32) * block_size

    def one_block(first_bin):
        spec_part = lax.dynamic_slice_in_dim(spectra, first_bin, block_size, 2).astype(jnp.float32)
        bin_ids = first_bin + jnp.arange(block_size, dtype=jnp.int32)
        turn_counts = bin_ids[:, None, None] * delays[None, :, :] % samples
        angles = turn_counts.astype(jnp.float32) * (2.0 * math.pi / samples)
        cos_half = lax.optimization_barrier(jnp.cos(angles).astype(jnp.bfloat16))
        sin_half = lax.optimization_barrier((-jnp.sin(angles)).astype(jnp.bfloat16))
        cosine = cos_half.astype(jnp.float32)
        sine_part = sin_half.astype(jnp.float32)
        real_part = jnp.einsum('fdc,cf->df', cosine, spec_part[0]) - jnp.einsum('fdc,cf->df', sine_part, spec_part[1])
        imag_part = jnp.einsum('fdc,cf->df', cosine, spec_part[1]) + jnp.einsum('fdc,cf->df', sine_part, spec_part[0])
        return jnp.stack([real_part, imag_part], 1)
    pieces = lax.map(one_block, starts_list)
    summed = pieces.transpose(1, 2, 0, 3).reshape(TRIALS, 2, BINS)
    dedispersed = (summed * (1.0 / math.sqrt(CHANS))).astype(jnp.bfloat16)
    templates = jnp.take(template_bank, template_ids, axis=1).astype(jnp.float32)
    length = BINS + TAPS
    signal_rows = dedispersed.astype(jnp.float32)
    signal_rows = signal_rows[:, 0] + 1j * signal_rows[:, 1]
    signal_rows = jnp.pad(signal_rows, ((0, 0), (EDGE, length - BINS - EDGE)))
    tap_rows = templates[0] + 1j * templates[1]
    flipped_taps = jnp.concatenate([tap_rows[:, :1], jnp.zeros((TEMPLATES, length - TAPS), tap_rows.dtype), tap_rows[:, :0:-1]], 1)
    tap_freq = jnp.fft.fft(flipped_taps, axis=1)

    def one_trial(signal):
        response = jnp.fft.ifft(jnp.fft.fft(signal)[None, :] * tap_freq, axis=1)[:, :BINS]
        real_resp = jnp.real(response)
        imag_resp = jnp.imag(response)
        return (real_resp * real_resp + imag_resp * imag_resp).astype(jnp.bfloat16)
    return lax.map(one_trial, signal_rows)
```

```python
import functools
import math

import jax
import jax.numpy as jnp
from jax import lax
from jax.experimental import pallas as pl
from jax.experimental.pallas import tpu as pltpu
from jax.sharding import PartitionSpec as P

EDGE = 128
LANES = 128
MESH = pl.DeviceIdType.MESH


def cos_sin(turns, samples):
    eighth = samples // 8
    quadrant = (turns + eighth) // (2 * eighth)
    rest = turns - quadrant * (2 * eighth)
    x = rest.astype(jnp.float32) * (2.0 * math.pi / samples)
    y = x * x
    c = 1.0 + y * (-0.5 + y * (1.0 / 24 + y * (-1.0 / 720 + y * (1.0 / 40320))))
    s = x * (1.0 + y * (-1.0 / 6 + y * (1.0 / 120 + y * (-1.0 / 5040 + y * (1.0 / 362880)))))
    swap = (quadrant & 1) == 1
    cos = jnp.where(swap, s, c)
    sin = jnp.where(swap, c, s)
    cos = jnp.where(((quadrant + 1) & 2) == 2, -cos, cos)
    sin = jnp.where((quadrant & 2) == 2, -sin, sin)
    return cos, sin


def take_lanes(x, index):
    return jnp.take_along_axis(x, index, axis=1, mode="promise_in_bounds")


def dedisperse_kernel(
    samples, scale, spec_ref, delay_ref, dm_ref, out_ref, send_ref, sum_ref, chan_recv, bin_recv,
    table_ref, even_ref, split_ref, merge_ref, prod_a, prod_b, chan_sems, bin_sems,
):
    bin_size = lax.axis_size("bin")
    chan_size = lax.axis_size("chan")
    my_bin = lax.axis_index("bin")
    my_chan = lax.axis_index("chan")
    chans = spec_ref.shape[1]
    bins = spec_ref.shape[2]
    half = samples // 2
    group = prod_a.shape[1] // 2
    blocks = group // LANES
    all_blocks = half // LANES
    groups, rows = send_ref.shape[:2]
    width = out_ref.shape[1]
    tile = LANES
    own = bins // bin_size
    tiles = own // tile
    padded = max(chans, LANES)

    def chan_at(offset):
        return lax.rem(my_chan + offset, chan_size)

    def bin_at(offset):
        return lax.rem(my_bin + offset, bin_size)

    barrier = pltpu.get_barrier_semaphore()

    def greet_chan(offset, _):
        pl.semaphore_signal(
            barrier, inc=1, device_id={"chan": chan_at(offset)}, device_id_type=MESH
        )
        return 0

    def greet_bin(offset, _):
        pl.semaphore_signal(barrier, inc=1, device_id={"bin": bin_at(offset)}, device_id_type=MESH)
        return 0

    lax.fori_loop(1, chan_size, greet_chan, 0)
    lax.fori_loop(1, bin_size, greet_bin, 0)

    if delay_ref.shape[1] == chans:
        delay = delay_ref[...]
    else:
        rank = lax.axis_index("chan") * bin_size + lax.axis_index("bin")
        delay = delay_ref[:, pl.ds(pl.multiple_of(rank * chans, LANES), chans)]
    if chans < padded:
        delay = jnp.concatenate([delay, jnp.zeros((1, padded - chans), jnp.int32)], 1)

    def rotations(count, stride):
        turns = lax.broadcasted_iota(jnp.int32, (count, padded), 0) * stride * delay
        return cos_sin(turns & (samples - 1), samples)

    fine_cos, fine_sin = rotations(8, 1)
    mid_cos, mid_sin = rotations(LANES // 8, 8)
    low_cos = jnp.concatenate(
        [fine_cos * mid_cos[a:a + 1] - fine_sin * mid_sin[a:a + 1] for a in range(LANES // 8)], 0
    ).T[:chans]
    low_sin = jnp.concatenate(
        [fine_sin * mid_cos[a:a + 1] + fine_cos * mid_sin[a:a + 1] for a in range(LANES // 8)], 0
    ).T[:chans]
    coarse_cos, coarse_sin = rotations(all_blocks + 8, LANES)
    fill_rows = jnp.zeros((LANES - all_blocks - 8, padded), jnp.float32)
    high_cos = jnp.concatenate([coarse_cos, fill_rows], 0).T[:chans]
    high_sin = jnp.concatenate([coarse_sin, fill_rows], 0).T[:chans]
    lane_ids = lax.broadcasted_iota(jnp.int32, (chans, LANES), 1)

    def fill(block, _):
        spread = jnp.full((chans, LANES), block, jnp.int32)
        block_cos = take_lanes(high_cos, spread)
        block_sin = take_lanes(high_sin, spread)
        at = pl.multiple_of(block * LANES, LANES)
        cos = low_cos * block_cos - low_sin * block_sin
        sin = low_sin * block_cos + low_cos * block_sin
        table_ref[:, pl.ds(at, LANES)] = cos.astype(jnp.bfloat16)
        table_ref[:, pl.ds(half + at, LANES)] = sin.astype(jnp.bfloat16)
        return 0

    lax.fori_loop(0, all_blocks, fill, 0)
    parity = take_lanes(high_cos, jnp.full((chans, LANES), all_blocks, jnp.int32))
    table_ref[:, half:half + LANES] = jnp.where(lane_ids == 0, parity, low_sin).astype(jnp.bfloat16)

    paired = half == group and tiles == 2 and half % (4 * LANES) == 0
    if paired:
        even_cos = low_cos * low_cos - low_sin * low_sin
        even_sin = 2.0 * low_sin * low_cos
        for block in range(all_blocks // 2):
            spread = jnp.full((chans, LANES), 2 * block, jnp.int32)
            block_cos = take_lanes(high_cos, spread)
            block_sin = take_lanes(high_sin, spread)
            at = block * LANES
            cos = even_cos * block_cos - even_sin * block_sin
            sin = even_sin * block_cos + even_cos * block_sin
            if block == 0:
                sin = jnp.where(lane_ids == 0, parity, sin)
            even_ref[:, at:at + LANES] = cos.astype(jnp.bfloat16)
            even_ref[:, half // 2 + at:half // 2 + at + LANES] = sin.astype(jnp.bfloat16)
        near = lax.broadcasted_iota(jnp.int32, (own, own), 0)
        far = lax.broadcasted_iota(jnp.int32, (own, own), 1)

        def source(spot):
            return jnp.where(spot < tile, 2 * spot + 1, 2 * (spot - tile))

        split_ref[...] = (near == source(far)).astype(jnp.float32).astype(jnp.bfloat16)
        merge_ref[...] = (far == source(near)).astype(jnp.float32).astype(jnp.bfloat16)

    lane = lax.broadcasted_iota(jnp.int32, (8, LANES), 1)
    is_real = (lane // (rows // 2)) % 2 == 0
    dm = jnp.broadcast_to(dm_ref[...], (8, dm_ref.shape[1]))
    dm = jnp.concatenate([dm] * (LANES // dm_ref.shape[1]), 1)
    dm = take_lanes(dm, (lane // rows) * (rows // 2) + lane % (rows // 2))

    def first_of(step):
        return pl.multiple_of(step * tile, tile)

    def multiply(step, g, prod_ref):
        at = pl.ds(first_of(step), tile)
        both = jnp.concatenate([spec_ref[0, :, at], spec_ref[1, :, at]], 1)
        for part in (0, 1):
            columns = pl.ds(pl.multiple_of(part * half + g * group, group), group)
            prod_ref[:, part * group:(part + 1) * group] = lax.dot_general(
                both, table_ref[:, columns], (((0,), (0,)), ((), ())),
                preferred_element_type=jnp.float32,
            )

    def turns_of(step, r):
        bin_ids = step * tile + r * 8 + lax.broadcasted_iota(jnp.int32, (8, LANES), 0)
        return (bin_ids * dm) & (samples - 1)

    def pick(turns, half, group, g, r, prod_ref, acc):
        folded = jnp.where(turns > half, 2 * half - turns, turns)
        index = folded & (half - 1)
        spot = index & (LANES - 1)
        which = index // LANES - g * (group // LANES)
        acc = list(acc)
        for b in range(group // LANES):
            hit = which == b
            for i, (part, table) in enumerate(((0, 0), (1, 1), (1, 0), (0, 1))):
                top = part * tile + r * 8
                left = table * group + b * LANES
                piece = take_lanes(prod_ref[top:top + 8, left:left + LANES], spot)
                acc[i] = piece if acc[i] is None else jnp.where(hit, piece, acc[i])
        return acc

    def finish(turns, half, acc):
        sign = jnp.where(turns > half, -1.0, jnp.where(turns == 0, 0.0, 1.0))
        a, b, a2, b2 = acc
        real = jnp.where(turns == half, b2, a + sign * b)
        imag = jnp.where(turns == half, b, a2 - sign * b2)
        return jnp.where(is_real, real, imag)

    def split_multiply(block, even, prod_ref):
        at = pl.ds(pl.multiple_of(block * own, LANES), own)
        chosen = split_ref[:, even * tile:(even + 1) * tile]
        both = jnp.concatenate(
            [
                jnp.dot(spec_ref[part, :, at], chosen, preferred_element_type=jnp.float32)
                for part in (0, 1)
            ],
            1,
        ).astype(jnp.bfloat16)
        size = 2 * half // (1 + even)
        prod_ref[:, :size] = lax.dot_general(
            both, (even_ref if even else table_ref)[...], (((0,), (0,)), ((), ())),
            preferred_element_type=jnp.float32,
        )

    def split_gather(block, even, prod_ref):
        pieces = []
        for r in range(tile // 8):
            spots = r * 8 + lax.broadcasted_iota(jnp.int32, (8, LANES), 0)
            bin_ids = block * own + 2 * spots + (1 - even)
            turns = ((bin_ids * dm) & (samples - 1)) >> even
            size = half >> even
            acc = pick(turns, size, size, 0, r, prod_ref, [None] * 4)
            pieces.append(finish(turns, size, acc))
        return pieces

    def put(step, pieces):
        block = jnp.concatenate(pieces, 0).T
        at = pl.ds(first_of(step), tile)
        send_ref[:, :, at] = block.reshape(groups, rows, tile).astype(send_ref.dtype)

    def block_at(p):
        return bin_at(p + 1)

    def compute(p):
        base = block_at(p) * tiles

        def one_tile(t, _):
            step = base + t

            def one_group(g, accs):
                multiply(step, g, prod_a)
                new = []
                for r in range(tile // 8):
                    new += pick(
                        turns_of(step, r), half, group, g, r, prod_a, accs[4 * r:4 * r + 4]
                    )
                return tuple(new)

            zero = jnp.zeros((8, LANES), jnp.float32)
            accs = lax.fori_loop(0, half // group, one_group, (zero,) * (4 * (tile // 8)))
            put(step, [
                finish(turns_of(step, r), half, accs[4 * r:4 * r + 4]) for r in range(tile // 8)
            ])
            return 0

        if paired:
            block = block_at(p)
            split_multiply(block, 1, prod_b)
            pieces = split_gather(block, 0, prod_a)
            split_multiply(block_at(jnp.minimum(p + 1, bin_size - 1)), 0, prod_a)
            pieces += split_gather(block, 1, prod_b)
            merged = lax.dot_general(
                jnp.concatenate(pieces, 0).astype(jnp.bfloat16), merge_ref[...],
                (((0,), (0,)), ((), ())), preferred_element_type=jnp.float32,
            )
            at = pl.ds(pl.multiple_of(block * own, LANES), own)
            send_ref[:, :, at] = merged.reshape(groups, rows, own).astype(send_ref.dtype)
        else:
            lax.fori_loop(0, tiles, one_tile, 0)

    def chan_copy(p, offset):
        at = pl.ds(pl.multiple_of(block_at(p) * own, LANES), own)
        return pltpu.make_async_remote_copy(
            src_ref=send_ref.at[chan_at(offset), :, at],
            dst_ref=chan_recv.at[chan_size - offset, :, at],
            send_sem=chan_sems.at[0, offset, p],
            recv_sem=chan_sems.at[1, chan_size - offset, p],
            device_id={"chan": chan_at(offset)},
            device_id_type=MESH,
        )

    def bin_copy(block, piece):
        to = block + (0, 1, -1)[piece]
        begin, size, land = ((0, own, EDGE), (own - EDGE, EDGE, 0), (0, EDGE, EDGE + own))[piece]
        offset = lax.rem(to - my_bin + bin_size, bin_size)
        slot = lax.rem(bin_size - offset, bin_size)
        return pltpu.make_async_remote_copy(
            src_ref=sum_ref.at[:, pl.ds(pl.multiple_of(EDGE + block * own + begin, LANES), size)],
            dst_ref=bin_recv.at[slot, :, land:land + size],
            send_sem=bin_sems.at[0, piece, offset],
            recv_sem=bin_sems.at[1, piece, slot],
            device_id={"bin": to},
            device_id_type=MESH,
        )

    def each_piece(block, act):
        for piece in range(3):
            to = block + (0, 1, -1)[piece]

            @pl.when((to >= 0) & (to < bin_size) & (to != my_bin))
            def _():
                act(bin_copy(block, piece))

    def forward(p):
        block = block_at(p)
        at = pl.multiple_of(block * own, LANES)
        for offset in range(1, chan_size):
            chan_copy(p, chan_size - offset).wait_recv()
        total = send_ref[my_chan, :, pl.ds(at, own)].astype(jnp.float32)
        for offset in range(1, chan_size):
            total += chan_recv[offset, :, pl.ds(at, own)].astype(jnp.float32)
        sum_ref[:, pl.ds(pl.multiple_of(EDGE + at, LANES), own)] = total.astype(sum_ref.dtype)
        each_piece(block, lambda copy: copy.start())

    edge = jnp.zeros((rows, EDGE), sum_ref.dtype)
    sum_ref[:, :EDGE] = edge
    sum_ref[:, EDGE + bins:] = edge

    @pl.when(my_bin == 0)
    def _():
        for slot in range(1, bin_size):
            bin_recv[slot, :, :EDGE] = edge

    @pl.when(my_bin == bin_size - 1)
    def _():
        for slot in range(1, bin_size):
            bin_recv[slot, :, EDGE + own:] = edge

    if paired:
        split_multiply(block_at(0), 0, prod_a)
    pl.semaphore_wait(barrier, chan_size + bin_size - 2)

    def one_block(p, _):
        compute(p)
        for offset in range(1, chan_size):
            chan_copy(p, offset).start()

        @pl.when(p > 0)
        def _():
            forward(p - 1)

        return 0

    lax.fori_loop(0, bin_size, one_block, 0)
    forward(bin_size - 1)

    total = sum_ref[:, pl.ds(pl.multiple_of(my_bin * own, LANES), width)].astype(jnp.float32)
    for slot in range(1, bin_size):
        for piece in range(3):
            begin, size = ((EDGE, own), (0, EDGE), (EDGE + own, EDGE))[piece]
            sender = lax.rem(my_bin + slot, bin_size)
            comes = (True, my_bin > 0, my_bin < bin_size - 1)[piece]

            @pl.when(comes)
            def _():
                pltpu.make_async_remote_copy(
                    src_ref=sum_ref.at[:, begin:begin + size],
                    dst_ref=bin_recv.at[slot, :, begin:begin + size],
                    send_sem=bin_sems.at[0, piece, slot],
                    recv_sem=bin_sems.at[1, piece, slot],
                    device_id={"bin": sender},
                    device_id_type=MESH,
                ).wait_recv()

        total += bin_recv[slot].astype(jnp.float32)
    out_ref[...] = (total * scale).astype(jnp.bfloat16).astype(jnp.float32)

    def drain(p, _):
        for offset in range(1, chan_size):
            chan_copy(p, offset).wait_send()
        each_piece(block_at(p), lambda copy: copy.wait_send())
        return 0

    lax.fori_loop(0, bin_size, drain, 0)


def gather_lanes(x, index):
    return lax.gather(
        x, index[:, :, None],
        dimension_numbers=lax.GatherDimensionNumbers(
            offset_dims=(), collapsed_slice_dims=(1,), start_index_map=(1,),
            operand_batching_dims=(0,), start_indices_batching_dims=(0,),
        ),
        slice_sizes=(1, 1), mode="promise_in_bounds",
    )


def paired_kernel(
    samples, scale, spec_hbm, delay_hbm, dm_hbm, out_ref, spec_ref, delay_ref, dm_ref, send_ref,
    sum_ref, chan_recv, bin_recv, low_ref, table_ref, split_ref, odd_ref, even_ref,
    load_sems, chan_sems, bin_sems,
):
    bin_size = lax.axis_size("bin")
    chan_size = lax.axis_size("chan")
    my_bin = lax.axis_index("bin")
    my_chan = lax.axis_index("chan")
    chans = spec_ref.shape[1]
    bins = spec_ref.shape[2]
    half = samples // 2
    quarter = half // 2
    groups, rows = send_ref.shape[:2]
    width = out_ref.shape[1]
    tile = LANES
    own = bins // bin_size
    count = quarter // LANES
    pack = 16

    def chan_at(offset):
        return lax.rem(my_chan + offset, chan_size)

    def bin_at(offset):
        return lax.rem(my_bin + offset, bin_size)

    def block_at(p):
        return bin_at(p + 1)

    def spec_copy(p):
        at = pl.ds(pl.multiple_of(block_at(p) * own, LANES), own)
        return pltpu.make_async_copy(
            spec_hbm.at[:, :, at], spec_ref.at[:, :, at], load_sems.at[2 + p]
        )

    rank = my_chan * bin_size + my_bin
    mine = pl.ds(pl.multiple_of(rank * chans, LANES), chans)
    delay_copy = pltpu.make_async_copy(delay_hbm.at[:, mine], delay_ref, load_sems.at[0])
    dm_copy = pltpu.make_async_copy(dm_hbm, dm_ref, load_sems.at[1])
    delay_copy.start()
    dm_copy.start()
    for p in range(bin_size):
        spec_copy(p).start()

    barrier = pltpu.get_barrier_semaphore()

    def greet_chan(offset, _):
        pl.semaphore_signal(
            barrier, inc=1, device_id={"chan": chan_at(offset)}, device_id_type=MESH
        )
        return 0

    def greet_bin(offset, _):
        pl.semaphore_signal(barrier, inc=1, device_id={"bin": bin_at(offset)}, device_id_type=MESH)
        return 0

    lax.fori_loop(1, chan_size, greet_chan, 0)
    lax.fori_loop(1, bin_size, greet_bin, 0)

    near = lax.broadcasted_iota(jnp.int32, (own, own), 0)
    far = lax.broadcasted_iota(jnp.int32, (own, own), 1)
    source = jnp.where(near < tile, 2 * near + 1, 2 * (near - tile))
    split_ref[...] = (far == source).astype(jnp.float32).astype(jnp.bfloat16)

    edge = jnp.zeros((rows, EDGE), sum_ref.dtype)
    sum_ref[:, :EDGE] = edge
    sum_ref[:, EDGE + bins:] = edge

    @pl.when(my_bin == 0)
    def _():
        for slot in range(1, bin_size):
            bin_recv[slot, :, :EDGE] = edge

    @pl.when(my_bin == bin_size - 1)
    def _():
        for slot in range(1, bin_size):
            bin_recv[slot, :, EDGE + own:] = edge

    delay_copy.wait()
    delay = delay_ref[...]

    def rotations(factor):
        return cos_sin((factor * delay) & (samples - 1), samples)

    row = lax.broadcasted_iota(jnp.int32, (8, chans), 0)
    fine_cos, fine_sin = rotations(2 * row)
    mid_cos, mid_sin = rotations(2 * 8 * lax.broadcasted_iota(jnp.int32, (LANES // 8, chans), 0))
    high_cos, high_sin = rotations(jnp.where(row == 0, 1, 2 * LANES * row))
    one_cos, one_sin = high_cos[:1], high_sin[:1]
    for a in range(LANES // 8):
        at = slice(8 * a, 8 * a + 8)
        cos = fine_cos * mid_cos[a:a + 1] - fine_sin * mid_sin[a:a + 1]
        sin = fine_sin * mid_cos[a:a + 1] + fine_cos * mid_sin[a:a + 1]
        low_ref[0, at] = cos
        low_ref[1, at] = sin
        low_ref[2, at] = cos * one_cos - sin * one_sin
        low_ref[3, at] = sin * one_cos + cos * one_sin

    def fill(i, _):
        at = pl.ds(pl.multiple_of(i * pack, pack), pack)
        for odd in (0, 1):
            low_cos = low_ref[2 * odd, at]
            low_sin = low_ref[2 * odd + 1, at]
            for k in range(count):
                if k == 0:
                    cos, sin = low_cos, low_sin
                else:
                    block_cos, block_sin = high_cos[k:k + 1], high_sin[k:k + 1]
                    cos = low_cos * block_cos - low_sin * block_sin
                    sin = low_sin * block_cos + low_cos * block_sin
                for part, value in ((0, cos), (1, sin)):
                    first = ((2 * odd + part) * count + k) * LANES
                    to = pl.ds(pl.multiple_of(first + i * pack, pack), pack)
                    table_ref[to] = value.astype(jnp.bfloat16)
        return 0

    lax.fori_loop(0, LANES // pack, fill, 0)
    parity = (1 - 2 * (delay & 1)).astype(jnp.float32)
    top = lax.broadcasted_iota(jnp.int32, (pack, chans), 0) == 0
    table_ref[quarter:quarter + pack] = jnp.where(top, parity, low_ref[1, :pack]).astype(
        jnp.bfloat16
    )

    dm_copy.wait()
    lane = lax.broadcasted_iota(jnp.int32, (8, LANES), 1)
    dm = jnp.broadcast_to(dm_ref[...], (8, dm_ref.shape[1]))
    dm = jnp.concatenate([dm] * (LANES // dm_ref.shape[1]), 1)
    dm = take_lanes(dm, (lane // rows) * (rows // 2) + lane % (rows // 2))
    dm = jnp.concatenate([dm] * (pack // 8), 0)
    lane = lax.broadcasted_iota(jnp.int32, (pack, LANES), 1)
    is_real = (lane // (rows // 2)) % 2 == 0
    flip = jnp.where(is_real, 1.0, -1.0)

    def turned(block):
        at = pl.ds(pl.multiple_of(block * own, LANES), own)
        sides = [
            lax.dot_general(
                split_ref[...], spec_ref[part, :, at], (((1,), (1,)), ((), ())),
                preferred_element_type=jnp.float32,
            ).astype(jnp.bfloat16)
            for part in (0, 1)
        ]
        return [
            jnp.concatenate([side[n * tile:(n + 1) * tile] for side in sides], 0) for n in (0, 1)
        ]

    def multiply(left, prod_ref):
        size = prod_ref.shape[1]
        prod_ref[...] = lax.dot_general(
            left, table_ref[:size], (((1,), (1,)), ((), ())), preferred_element_type=jnp.float32
        ).astype(jnp.bfloat16)

    def collect(block, even, prod_ref):
        size = half >> even
        pieces = []
        for r in range(tile // pack):
            spots = r * pack + lax.broadcasted_iota(jnp.int32, (pack, LANES), 0)
            if even:
                turns = ((block * tile + spots) * dm) & (2 * size - 1)
            else:
                turns = ((block * own + 2 * spots + 1) * dm) & (2 * size - 1)
            index = jnp.where(turns > size, 2 * size - turns, turns) & (size - 1)
            if even:
                which, places = index // LANES, list(range(count))
            else:
                which = (index >> 1) // LANES + (index & 1) * (2 * count)
                places = list(range(count)) + list(range(2 * count, 3 * count))
                index = index >> 1
            spot = (index & (LANES - 1)).astype(jnp.int16)
            which = which.astype(jnp.int16)
            acc = [None] * 4
            for b in places:
                hit = which == b
                for i, (part, table) in enumerate(((0, 0), (1, 1), (1, 0), (0, 1))):
                    top = part * tile + r * pack
                    left = (b + table * count) * LANES
                    piece = gather_lanes(prod_ref[top:top + pack, left:left + LANES], spot)
                    acc[i] = piece if acc[i] is None else jnp.where(hit, piece, acc[i])
            a, b, a2, b2 = [value.astype(jnp.float32) for value in acc]
            sign = jnp.where(turns > size, -flip, jnp.where(turns == 0, 0.0, flip))
            sums = jnp.where(is_real, a, a2) + sign * jnp.where(is_real, b, b2)
            pieces.append(
                jnp.where(turns == size, jnp.where(is_real, b2, b), sums).astype(jnp.bfloat16)
            )
        return pieces

    def compute(p):
        block = block_at(p)
        odd, even = turned(block)
        multiply(odd, odd_ref)
        multiply(even, even_ref)
        near = collect(block, 0, odd_ref)
        far = collect(block, 1, even_ref)
        part = len(near) // 2
        for t in (0, 1):
            picked = near[t * part:(t + 1) * part] + far[t * part:(t + 1) * part]
            at = pl.ds(pl.multiple_of(block * own + t * tile, LANES), tile)
            send_ref[:, :, at] = jnp.concatenate(picked, 0).T.reshape(groups, rows, tile)

    def chan_copy(p, offset):
        at = pl.ds(pl.multiple_of(block_at(p) * own, LANES), own)
        return pltpu.make_async_remote_copy(
            src_ref=send_ref.at[chan_at(offset), :, at],
            dst_ref=chan_recv.at[chan_size - offset, :, at],
            send_sem=chan_sems.at[0, offset, p],
            recv_sem=chan_sems.at[1, chan_size - offset, p],
            device_id={"chan": chan_at(offset)},
            device_id_type=MESH,
        )

    def bin_copy(block, piece):
        to = block + (0, 1, -1)[piece]
        begin, size, land = ((0, own, EDGE), (own - EDGE, EDGE, 0), (0, EDGE, EDGE + own))[piece]
        offset = lax.rem(to - my_bin + bin_size, bin_size)
        slot = lax.rem(bin_size - offset, bin_size)
        return pltpu.make_async_remote_copy(
            src_ref=sum_ref.at[:, pl.ds(pl.multiple_of(EDGE + block * own + begin, LANES), size)],
            dst_ref=bin_recv.at[slot, :, land:land + size],
            send_sem=bin_sems.at[0, piece, offset],
            recv_sem=bin_sems.at[1, piece, slot],
            device_id={"bin": to},
            device_id_type=MESH,
        )

    def each_piece(block, act):
        for piece in range(3):
            to = block + (0, 1, -1)[piece]

            @pl.when((to >= 0) & (to < bin_size) & (to != my_bin))
            def _():
                act(bin_copy(block, piece))

    def forward(p):
        block = block_at(p)
        at = pl.multiple_of(block * own, LANES)
        for offset in range(1, chan_size):
            chan_copy(p, chan_size - offset).wait_recv()
        total = send_ref[my_chan, :, pl.ds(at, own)].astype(jnp.float32)
        for offset in range(1, chan_size):
            total += chan_recv[offset, :, pl.ds(at, own)].astype(jnp.float32)
        sum_ref[:, pl.ds(pl.multiple_of(EDGE + at, LANES), own)] = total.astype(sum_ref.dtype)
        each_piece(block, lambda copy: copy.start())

    def one_block(p, _):
        spec_copy(p).wait()
        compute(p)

        @pl.when(p == 0)
        def _():
            pl.semaphore_wait(barrier, chan_size + bin_size - 2)

        for offset in range(1, chan_size):
            chan_copy(p, offset).start()
        return 0

    lax.fori_loop(0, bin_size, one_block, 0)
    for p in range(bin_size):
        forward(p)

    total = sum_ref[:, pl.ds(pl.multiple_of(my_bin * own, LANES), width)].astype(jnp.float32)
    for slot in range(1, bin_size):
        for piece in range(3):
            begin, size = ((EDGE, own), (0, EDGE), (EDGE + own, EDGE))[piece]
            sender = lax.rem(my_bin + slot, bin_size)
            comes = (True, my_bin > 0, my_bin < bin_size - 1)[piece]

            @pl.when(comes)
            def _():
                pltpu.make_async_remote_copy(
                    src_ref=sum_ref.at[:, begin:begin + size],
                    dst_ref=bin_recv.at[slot, :, begin:begin + size],
                    send_sem=bin_sems.at[0, piece, slot],
                    recv_sem=bin_sems.at[1, piece, slot],
                    device_id={"bin": sender},
                    device_id_type=MESH,
                ).wait_recv()

        total += bin_recv[slot].astype(jnp.float32)
    signal = (total * scale).astype(jnp.bfloat16).astype(jnp.float32)
    lane = lax.broadcasted_iota(jnp.int32, (rows, tile), 1)
    back = (lane >> 1) + (tile // 2) * (1 - (lane & 1))
    for t in range(width // tile):
        at = slice(t * tile, (t + 1) * tile)
        out_ref[:, at] = take_lanes(signal[:, at], back)

    def drain(p, _):
        for offset in range(1, chan_size):
            chan_copy(p, offset).wait_send()
        each_piece(block_at(p), lambda copy: copy.wait_send())
        return 0

    lax.fori_loop(0, bin_size, drain, 0)


def correlate_kernel(trials, signal_ref, bank_ref, ids_ref, out_ref, taps_ref):
    step = pl.program_id(0)
    per_step, templates, bins = out_ref.shape
    bank_size, taps = bank_ref.shape[1:]

    @pl.when(step == 0)
    def _():
        rows = lax.broadcasted_iota(jnp.int32, (bank_size, templates), 0)
        one_hot = (ids_ref[...] == rows).astype(jnp.bfloat16)
        chosen = [
            lax.dot_general(
                one_hot, bank_ref[part], (((0,), (0,)), ((), ())),
                preferred_element_type=jnp.float32,
            )
            for part in (0, 1)
        ]
        taps_ref[:templates, :taps] = chosen[0].astype(jnp.bfloat16)
        taps_ref[:templates, taps:] = (-chosen[1]).astype(jnp.bfloat16)
        taps_ref[templates:, :taps] = chosen[1].astype(jnp.bfloat16)
        taps_ref[templates:, taps:] = chosen[0].astype(jnp.bfloat16)

    row = lax.broadcasted_iota(jnp.int32, (8, LANES), 0)
    col = lax.broadcasted_iota(jnp.int32, (8, LANES), 1)
    spot = (row + col) & (LANES - 1)
    inside = row + col < LANES
    length = bins + taps
    spans = length // LANES
    for t in range(per_step):
        trial = step * per_step + t
        hankel = []
        for part in (0, 1):
            line = signal_ref[pl.ds(part * trials + trial, 1), :]
            turned = [
                take_lanes(jnp.broadcast_to(line[:, s * LANES:(s + 1) * LANES], (8, LANES)), spot)
                for s in range(spans)
            ]
            base = jnp.concatenate(
                [jnp.where(inside, turned[s], turned[(s + 1) % spans]) for s in range(spans)], 1
            )
            rows = [base] + [
                pltpu.roll(base, length - 8 * a, 1) for a in range(1, LANES // 8)
            ]
            hankel.append(jnp.concatenate(rows, 0).astype(jnp.bfloat16))
        wide = jnp.concatenate(
            [
                hankel[part][:, u * LANES:u * LANES + bins]
                for part in (0, 1)
                for u in range(taps // LANES)
            ],
            0,
        )
        response = jnp.dot(taps_ref[...], wide, preferred_element_type=jnp.float32)
        real = response[:templates]
        imag = response[templates:]
        out_ref[t] = (real * real + imag * imag).astype(out_ref.dtype)


def local(spectra, dm_trials, chan_delay, template_bank, template_ids):
    chans, bins = spectra.shape[1:]
    samples = 2 * bins
    bin_size = lax.axis_size("bin")
    chan_size = lax.axis_size("chan")
    trials = dm_trials.shape[0] // chan_size
    templates = template_ids.shape[0]
    taps = template_bank.shape[2]
    own = bins // bin_size
    width = own + 2 * EDGE
    scale = 1.0 / math.sqrt(chan_delay.shape[0])
    per_step = math.gcd(trials, 4)
    if chans % LANES:
        rank = lax.axis_index("chan") * bin_size + lax.axis_index("bin")
        chan_delay = lax.dynamic_slice_in_dim(chan_delay, rank * chans, chans)
    vmem = pl.BlockSpec(memory_space=pltpu.VMEM)
    products = pltpu.VMEM((2 * LANES, 2 * min(bins, 1024)), jnp.float32)

    paired = (
        bins <= 1024 and bins % (4 * LANES) == 0 and own == 2 * LANES and chans % LANES == 0
        and trials * 2 * chan_size == LANES
    )
    if paired:
        hbm = pl.BlockSpec(memory_space=pltpu.HBM)
        signal = pl.pallas_call(
            functools.partial(paired_kernel, samples, scale),
            out_shape=jax.ShapeDtypeStruct((2 * trials, width), jnp.float32),
            in_specs=[hbm] * 3,
            out_specs=vmem,
            scratch_shapes=[
                pltpu.VMEM((2, chans, bins), jnp.bfloat16),
                pltpu.VMEM((1, chans), jnp.int32),
                pltpu.VMEM((1, dm_trials.shape[0]), jnp.int32),
                pltpu.VMEM((chan_size, 2 * trials, bins), jnp.bfloat16),
                pltpu.VMEM((2 * trials, bins + 2 * EDGE), jnp.bfloat16),
                pltpu.VMEM((chan_size, 2 * trials, bins), jnp.bfloat16),
                pltpu.VMEM((bin_size, 2 * trials, width), jnp.bfloat16),
                pltpu.VMEM((4, LANES, chans), jnp.float32),
                pltpu.VMEM((2 * bins, chans), jnp.bfloat16),
                pltpu.VMEM((own, own), jnp.bfloat16),
                pltpu.VMEM((2 * LANES, 2 * bins), jnp.bfloat16),
                pltpu.VMEM((2 * LANES, bins), jnp.bfloat16),
                pltpu.SemaphoreType.DMA((2 + bin_size,)),
                pltpu.SemaphoreType.DMA((2, chan_size, bin_size)),
                pltpu.SemaphoreType.DMA((2, 3, bin_size)),
            ],
            compiler_params=pltpu.CompilerParams(
                collective_id=0, has_side_effects=True, vmem_limit_bytes=24 * 2 ** 20
            ),
            name="dedisperse",
        )(*[
            pltpu.with_memory_space_constraint(x, pltpu.HBM)
            for x in (spectra, chan_delay[None, :], dm_trials[None, :])
        ])
    else:
        signal = pl.pallas_call(
            functools.partial(dedisperse_kernel, samples, scale),
            out_shape=jax.ShapeDtypeStruct((2 * trials, width), jnp.float32),
            in_specs=[vmem] * 3,
            out_specs=vmem,
            scratch_shapes=[
                pltpu.VMEM((chan_size, 2 * trials, bins), jnp.bfloat16),
                pltpu.VMEM((2 * trials, bins + 2 * EDGE), jnp.bfloat16),
                pltpu.VMEM((chan_size, 2 * trials, bins), jnp.bfloat16),
                pltpu.VMEM((bin_size, 2 * trials, width), jnp.bfloat16),
                pltpu.VMEM((chans, 2 * bins), jnp.bfloat16),
                pltpu.VMEM((chans, bins), jnp.bfloat16),
                pltpu.VMEM((own, own), jnp.bfloat16),
                pltpu.VMEM((own, own), jnp.bfloat16),
                products,
                products,
                pltpu.SemaphoreType.DMA((2, chan_size, bin_size)),
                pltpu.SemaphoreType.DMA((2, 3, bin_size)),
            ],
            compiler_params=pltpu.CompilerParams(collective_id=0, has_side_effects=True),
            name="dedisperse",
        )(spectra, chan_delay[None, :], dm_trials[None, :])

    return pl.pallas_call(
        functools.partial(correlate_kernel, trials),
        grid=(trials // per_step,),
        out_shape=jax.ShapeDtypeStruct((trials, templates, own), jnp.bfloat16),
        in_specs=[
            pl.BlockSpec((2 * trials, width), lambda t: (0, 0)),
            pl.BlockSpec(template_bank.shape, lambda t: (0, 0, 0)),
            pl.BlockSpec((1, templates), lambda t: (0, 0)),
        ],
        out_specs=pl.BlockSpec((per_step, templates, own), lambda t: (t, 0, 0)),
        scratch_shapes=[pltpu.VMEM((2 * templates, 2 * taps), jnp.bfloat16)],
        compiler_params=pltpu.CompilerParams(vmem_limit_bytes=16 * 2 ** 20),
        name="templates",
    )(signal, template_bank, template_ids[None, :])


def solution(mesh):
    in_specs = (P(None, ("beam", "chan", "bin"), None), P(), P(), P(), P())
    out_specs = P(("beam", "chan"), None, "bin")
    return jax.shard_map(local, mesh=mesh, in_specs=in_specs, out_specs=out_specs, check_vma=False)
```

```python
import functools
import math

import jax
import jax.numpy as jnp
from jax import lax
from jax.experimental import pallas as pl
from jax.experimental.pallas import tpu as pltpu
from jax.sharding import PartitionSpec as P

EDGE = 128
LANES = 128
MESH = pl.DeviceIdType.MESH


def cos_sin(turns, samples):
    eighth = samples // 8
    quadrant = (turns + eighth) // (2 * eighth)
    rest = turns - quadrant * (2 * eighth)
    x = rest.astype(jnp.float32) * (2.0 * math.pi / samples)
    y = x * x
    c = 1.0 + y * (-0.5 + y * (1.0 / 24 + y * (-1.0 / 720 + y * (1.0 / 40320))))
    s = x * (1.0 + y * (-1.0 / 6 + y * (1.0 / 120 + y * (-1.0 / 5040 + y * (1.0 / 362880)))))
    swap = (quadrant & 1) == 1
    cos = jnp.where(swap, s, c)
    sin = jnp.where(swap, c, s)
    cos = jnp.where(((quadrant + 1) & 2) == 2, -cos, cos)
    sin = jnp.where((quadrant & 2) == 2, -sin, sin)
    return cos, sin


def take_lanes(x, index):
    return jnp.take_along_axis(x, index, axis=1, mode="promise_in_bounds")


def dedisperse_kernel(
    samples, scale, spec_ref, delay_ref, dm_ref, out_ref, send_ref, sum_ref, chan_recv, bin_recv,
    table_ref, even_ref, split_ref, merge_ref, prod_a, prod_b, chan_sems, bin_sems,
):
    bin_size = lax.axis_size("bin")
    chan_size = lax.axis_size("chan")
    my_bin = lax.axis_index("bin")
    my_chan = lax.axis_index("chan")
    chans = spec_ref.shape[1]
    bins = spec_ref.shape[2]
    half = samples // 2
    group = prod_a.shape[1] // 2
    blocks = group // LANES
    all_blocks = half // LANES
    groups, rows = send_ref.shape[:2]
    width = out_ref.shape[1]
    tile = LANES
    own = bins // bin_size
    tiles = own // tile
    padded = max(chans, LANES)

    def chan_at(offset):
        return lax.rem(my_chan + offset, chan_size)

    def bin_at(offset):
        return lax.rem(my_bin + offset, bin_size)

    barrier = pltpu.get_barrier_semaphore()

    def greet_chan(offset, _):
        pl.semaphore_signal(
            barrier, inc=1, device_id={"chan": chan_at(offset)}, device_id_type=MESH
        )
        return 0

    def greet_bin(offset, _):
        pl.semaphore_signal(barrier, inc=1, device_id={"bin": bin_at(offset)}, device_id_type=MESH)
        return 0

    lax.fori_loop(1, chan_size, greet_chan, 0)
    lax.fori_loop(1, bin_size, greet_bin, 0)

    if delay_ref.shape[1] == chans:
        delay = delay_ref[...]
    else:
        rank = lax.axis_index("chan") * bin_size + lax.axis_index("bin")
        delay = delay_ref[:, pl.ds(pl.multiple_of(rank * chans, LANES), chans)]
    if chans < padded:
        delay = jnp.concatenate([delay, jnp.zeros((1, padded - chans), jnp.int32)], 1)

    def rotations(count, stride):
        turns = lax.broadcasted_iota(jnp.int32, (count, padded), 0) * stride * delay
        return cos_sin(turns & (samples - 1), samples)

    fine_cos, fine_sin = rotations(8, 1)
    mid_cos, mid_sin = rotations(LANES // 8, 8)
    low_cos = jnp.concatenate(
        [fine_cos * mid_cos[a:a + 1] - fine_sin * mid_sin[a:a + 1] for a in range(LANES // 8)], 0
    ).T[:chans]
    low_sin = jnp.concatenate(
        [fine_sin * mid_cos[a:a + 1] + fine_cos * mid_sin[a:a + 1] for a in range(LANES // 8)], 0
    ).T[:chans]
    coarse_cos, coarse_sin = rotations(all_blocks + 8, LANES)
    fill_rows = jnp.zeros((LANES - all_blocks - 8, padded), jnp.float32)
    high_cos = jnp.concatenate([coarse_cos, fill_rows], 0).T[:chans]
    high_sin = jnp.concatenate([coarse_sin, fill_rows], 0).T[:chans]
    lane_ids = lax.broadcasted_iota(jnp.int32, (chans, LANES), 1)

    def fill(block, _):
        spread = jnp.full((chans, LANES), block, jnp.int32)
        block_cos = take_lanes(high_cos, spread)
        block_sin = take_lanes(high_sin, spread)
        at = pl.multiple_of(block * LANES, LANES)
        cos = low_cos * block_cos - low_sin * block_sin
        sin = low_sin * block_cos + low_cos * block_sin
        table_ref[:, pl.ds(at, LANES)] = cos.astype(jnp.bfloat16)
        table_ref[:, pl.ds(half + at, LANES)] = sin.astype(jnp.bfloat16)
        return 0

    lax.fori_loop(0, all_blocks, fill, 0)
    parity = take_lanes(high_cos, jnp.full((chans, LANES), all_blocks, jnp.int32))
    table_ref[:, half:half + LANES] = jnp.where(lane_ids == 0, parity, low_sin).astype(jnp.bfloat16)

    paired = half == group and tiles == 2 and half % (4 * LANES) == 0
    if paired:
        even_cos = low_cos * low_cos - low_sin * low_sin
        even_sin = 2.0 * low_sin * low_cos
        for block in range(all_blocks // 2):
            spread = jnp.full((chans, LANES), 2 * block, jnp.int32)
            block_cos = take_lanes(high_cos, spread)
            block_sin = take_lanes(high_sin, spread)
            at = block * LANES
            cos = even_cos * block_cos - even_sin * block_sin
            sin = even_sin * block_cos + even_cos * block_sin
            if block == 0:
                sin = jnp.where(lane_ids == 0, parity, sin)
            even_ref[:, at:at + LANES] = cos.astype(jnp.bfloat16)
            even_ref[:, half // 2 + at:half // 2 + at + LANES] = sin.astype(jnp.bfloat16)
        near = lax.broadcasted_iota(jnp.int32, (own, own), 0)
        far = lax.broadcasted_iota(jnp.int32, (own, own), 1)

        def source(spot):
            return jnp.where(spot < tile, 2 * spot + 1, 2 * (spot - tile))

        split_ref[...] = (near == source(far)).astype(jnp.float32).astype(jnp.bfloat16)
        merge_ref[...] = (far == source(near)).astype(jnp.float32).astype(jnp.bfloat16)

    lane = lax.broadcasted_iota(jnp.int32, (8, LANES), 1)
    is_real = (lane // (rows // 2)) % 2 == 0
    dm = jnp.broadcast_to(dm_ref[...], (8, dm_ref.shape[1]))
    dm = jnp.concatenate([dm] * (LANES // dm_ref.shape[1]), 1)
    dm = take_lanes(dm, (lane // rows) * (rows // 2) + lane % (rows // 2))

    def first_of(step):
        return pl.multiple_of(step * tile, tile)

    def multiply(step, g, prod_ref):
        at = pl.ds(first_of(step), tile)
        both = jnp.concatenate([spec_ref[0, :, at], spec_ref[1, :, at]], 1)
        for part in (0, 1):
            columns = pl.ds(pl.multiple_of(part * half + g * group, group), group)
            prod_ref[:, part * group:(part + 1) * group] = lax.dot_general(
                both, table_ref[:, columns], (((0,), (0,)), ((), ())),
                preferred_element_type=jnp.float32,
            )

    def turns_of(step, r):
        bin_ids = step * tile + r * 8 + lax.broadcasted_iota(jnp.int32, (8, LANES), 0)
        return (bin_ids * dm) & (samples - 1)

    def pick(turns, half, group, g, r, prod_ref, acc):
        folded = jnp.where(turns > half, 2 * half - turns, turns)
        index = folded & (half - 1)
        spot = index & (LANES - 1)
        which = index // LANES - g * (group // LANES)
        acc = list(acc)
        for b in range(group // LANES):
            hit = which == b
            for i, (part, table) in enumerate(((0, 0), (1, 1), (1, 0), (0, 1))):
                top = part * tile + r * 8
                left = table * group + b * LANES
                piece = take_lanes(prod_ref[top:top + 8, left:left + LANES], spot)
                acc[i] = piece if acc[i] is None else jnp.where(hit, piece, acc[i])
        return acc

    def finish(turns, half, acc):
        sign = jnp.where(turns > half, -1.0, jnp.where(turns == 0, 0.0, 1.0))
        a, b, a2, b2 = acc
        real = jnp.where(turns == half, b2, a + sign * b)
        imag = jnp.where(turns == half, b, a2 - sign * b2)
        return jnp.where(is_real, real, imag)

    def split_multiply(block, even, prod_ref):
        at = pl.ds(pl.multiple_of(block * own, LANES), own)
        chosen = split_ref[:, even * tile:(even + 1) * tile]
        both = jnp.concatenate(
            [
                jnp.dot(spec_ref[part, :, at], chosen, preferred_element_type=jnp.float32)
                for part in (0, 1)
            ],
            1,
        ).astype(jnp.bfloat16)
        size = 2 * half // (1 + even)
        prod_ref[:, :size] = lax.dot_general(
            both, (even_ref if even else table_ref)[...], (((0,), (0,)), ((), ())),
            preferred_element_type=jnp.float32,
        )

    def split_gather(block, even, prod_ref):
        pieces = []
        for r in range(tile // 8):
            spots = r * 8 + lax.broadcasted_iota(jnp.int32, (8, LANES), 0)
            bin_ids = block * own + 2 * spots + (1 - even)
            turns = ((bin_ids * dm) & (samples - 1)) >> even
            size = half >> even
            acc = pick(turns, size, size, 0, r, prod_ref, [None] * 4)
            pieces.append(finish(turns, size, acc))
        return pieces

    def put(step, pieces):
        block = jnp.concatenate(pieces, 0).T
        at = pl.ds(first_of(step), tile)
        send_ref[:, :, at] = block.reshape(groups, rows, tile).astype(send_ref.dtype)

    def block_at(p):
        return bin_at(p + 1)

    def compute(p):
        base = block_at(p) * tiles

        def one_tile(t, _):
            step = base + t

            def one_group(g, accs):
                multiply(step, g, prod_a)
                new = []
                for r in range(tile // 8):
                    new += pick(
                        turns_of(step, r), half, group, g, r, prod_a, accs[4 * r:4 * r + 4]
                    )
                return tuple(new)

            zero = jnp.zeros((8, LANES), jnp.float32)
            accs = lax.fori_loop(0, half // group, one_group, (zero,) * (4 * (tile // 8)))
            put(step, [
                finish(turns_of(step, r), half, accs[4 * r:4 * r + 4]) for r in range(tile // 8)
            ])
            return 0

        if paired:
            block = block_at(p)
            split_multiply(block, 1, prod_b)
            pieces = split_gather(block, 0, prod_a)
            split_multiply(block_at(jnp.minimum(p + 1, bin_size - 1)), 0, prod_a)
            pieces += split_gather(block, 1, prod_b)
            merged = lax.dot_general(
                jnp.concatenate(pieces, 0).astype(jnp.bfloat16), merge_ref[...],
                (((0,), (0,)), ((), ())), preferred_element_type=jnp.float32,
            )
            at = pl.ds(pl.multiple_of(block * own, LANES), own)
            send_ref[:, :, at] = merged.reshape(groups, rows, own).astype(send_ref.dtype)
        else:
            lax.fori_loop(0, tiles, one_tile, 0)

    def chan_copy(p, offset):
        at = pl.ds(pl.multiple_of(block_at(p) * own, LANES), own)
        return pltpu.make_async_remote_copy(
            src_ref=send_ref.at[chan_at(offset), :, at],
            dst_ref=chan_recv.at[chan_size - offset, :, at],
            send_sem=chan_sems.at[0, offset, p],
            recv_sem=chan_sems.at[1, chan_size - offset, p],
            device_id={"chan": chan_at(offset)},
            device_id_type=MESH,
        )

    def bin_copy(block, piece):
        to = block + (0, 1, -1)[piece]
        begin, size, land = ((0, own, EDGE), (own - EDGE, EDGE, 0), (0, EDGE, EDGE + own))[piece]
        offset = lax.rem(to - my_bin + bin_size, bin_size)
        slot = lax.rem(bin_size - offset, bin_size)
        return pltpu.make_async_remote_copy(
            src_ref=sum_ref.at[:, pl.ds(pl.multiple_of(EDGE + block * own + begin, LANES), size)],
            dst_ref=bin_recv.at[slot, :, land:land + size],
            send_sem=bin_sems.at[0, piece, offset],
            recv_sem=bin_sems.at[1, piece, slot],
            device_id={"bin": to},
            device_id_type=MESH,
        )

    def each_piece(block, act):
        for piece in range(3):
            to = block + (0, 1, -1)[piece]

            @pl.when((to >= 0) & (to < bin_size) & (to != my_bin))
            def _():
                act(bin_copy(block, piece))

    def forward(p):
        block = block_at(p)
        at = pl.multiple_of(block * own, LANES)
        for offset in range(1, chan_size):
            chan_copy(p, chan_size - offset).wait_recv()
        total = send_ref[my_chan, :, pl.ds(at, own)].astype(jnp.float32)
        for offset in range(1, chan_size):
            total += chan_recv[offset, :, pl.ds(at, own)].astype(jnp.float32)
        sum_ref[:, pl.ds(pl.multiple_of(EDGE + at, LANES), own)] = total.astype(sum_ref.dtype)
        each_piece(block, lambda copy: copy.start())

    edge = jnp.zeros((rows, EDGE), sum_ref.dtype)
    sum_ref[:, :EDGE] = edge
    sum_ref[:, EDGE + bins:] = edge

    @pl.when(my_bin == 0)
    def _():
        for slot in range(1, bin_size):
            bin_recv[slot, :, :EDGE] = edge

    @pl.when(my_bin == bin_size - 1)
    def _():
        for slot in range(1, bin_size):
            bin_recv[slot, :, EDGE + own:] = edge

    if paired:
        split_multiply(block_at(0), 0, prod_a)
    pl.semaphore_wait(barrier, chan_size + bin_size - 2)

    def one_block(p, _):
        compute(p)
        for offset in range(1, chan_size):
            chan_copy(p, offset).start()

        @pl.when(p > 0)
        def _():
            forward(p - 1)

        return 0

    lax.fori_loop(0, bin_size, one_block, 0)
    forward(bin_size - 1)

    total = sum_ref[:, pl.ds(pl.multiple_of(my_bin * own, LANES), width)].astype(jnp.float32)
    for slot in range(1, bin_size):
        for piece in range(3):
            begin, size = ((EDGE, own), (0, EDGE), (EDGE + own, EDGE))[piece]
            sender = lax.rem(my_bin + slot, bin_size)
            comes = (True, my_bin > 0, my_bin < bin_size - 1)[piece]

            @pl.when(comes)
            def _():
                pltpu.make_async_remote_copy(
                    src_ref=sum_ref.at[:, begin:begin + size],
                    dst_ref=bin_recv.at[slot, :, begin:begin + size],
                    send_sem=bin_sems.at[0, piece, slot],
                    recv_sem=bin_sems.at[1, piece, slot],
                    device_id={"bin": sender},
                    device_id_type=MESH,
                ).wait_recv()

        total += bin_recv[slot].astype(jnp.float32)
    out_ref[...] = (total * scale).astype(jnp.bfloat16).astype(jnp.float32)

    def drain(p, _):
        for offset in range(1, chan_size):
            chan_copy(p, offset).wait_send()
        each_piece(block_at(p), lambda copy: copy.wait_send())
        return 0

    lax.fori_loop(0, bin_size, drain, 0)


def gather_lanes(x, index):
    return lax.gather(
        x, index[:, :, None],
        dimension_numbers=lax.GatherDimensionNumbers(
            offset_dims=(), collapsed_slice_dims=(1,), start_index_map=(1,),
            operand_batching_dims=(0,), start_indices_batching_dims=(0,),
        ),
        slice_sizes=(1, 1), mode="promise_in_bounds",
    )


def paired_kernel(
    samples, scale, spec_hbm, delay_hbm, dm_hbm, out_ref, spec_ref, delay_ref, dm_ref, send_ref,
    sum_ref, chan_recv, bin_recv, low_ref, table_ref, split_ref, odd_ref, even_ref,
    load_sems, chan_sems, bin_sems,
):
    bin_size = lax.axis_size("bin")
    chan_size = lax.axis_size("chan")
    my_bin = lax.axis_index("bin")
    my_chan = lax.axis_index("chan")
    chans = spec_ref.shape[1]
    bins = spec_ref.shape[2]
    half = samples // 2
    quarter = half // 2
    groups, rows = send_ref.shape[:2]
    width = out_ref.shape[1]
    tile = LANES
    own = bins // bin_size
    count = quarter // LANES
    pack = 16

    def chan_at(offset):
        return lax.rem(my_chan + offset, chan_size)

    def bin_at(offset):
        return lax.rem(my_bin + offset, bin_size)

    def block_at(p):
        return bin_at(p + 1)

    def spec_copy(p):
        at = pl.ds(pl.multiple_of(block_at(p) * own, LANES), own)
        return pltpu.make_async_copy(
            spec_hbm.at[:, :, at], spec_ref.at[:, :, at], load_sems.at[2 + p]
        )

    rank = my_chan * bin_size + my_bin
    mine = pl.ds(pl.multiple_of(rank * chans, LANES), chans)
    delay_copy = pltpu.make_async_copy(delay_hbm.at[:, mine], delay_ref, load_sems.at[0])
    dm_copy = pltpu.make_async_copy(dm_hbm, dm_ref, load_sems.at[1])
    delay_copy.start()
    dm_copy.start()
    for p in range(bin_size):
        spec_copy(p).start()

    barrier = pltpu.get_barrier_semaphore()

    def greet_chan(offset, _):
        pl.semaphore_signal(
            barrier, inc=1, device_id={"chan": chan_at(offset)}, device_id_type=MESH
        )
        return 0

    def greet_bin(offset, _):
        pl.semaphore_signal(barrier, inc=1, device_id={"bin": bin_at(offset)}, device_id_type=MESH)
        return 0

    lax.fori_loop(1, chan_size, greet_chan, 0)
    lax.fori_loop(1, bin_size, greet_bin, 0)

    near = lax.broadcasted_iota(jnp.int32, (own, own), 0)
    far = lax.broadcasted_iota(jnp.int32, (own, own), 1)
    source = jnp.where(near < tile, 2 * near + 1, 2 * (near - tile))
    split_ref[...] = (far == source).astype(jnp.float32).astype(jnp.bfloat16)

    edge = jnp.zeros((rows, EDGE), sum_ref.dtype)
    sum_ref[:, :EDGE] = edge
    sum_ref[:, EDGE + bins:] = edge

    @pl.when(my_bin == 0)
    def _():
        for slot in range(1, bin_size):
            bin_recv[slot, :, :EDGE] = edge

    @pl.when(my_bin == bin_size - 1)
    def _():
        for slot in range(1, bin_size):
            bin_recv[slot, :, EDGE + own:] = edge

    delay_copy.wait()
    delay = delay_ref[...]

    def rotations(factor):
        return cos_sin((factor * delay) & (samples - 1), samples)

    row = lax.broadcasted_iota(jnp.int32, (8, chans), 0)
    fine_cos, fine_sin = rotations(2 * row)
    mid_cos, mid_sin = rotations(2 * 8 * lax.broadcasted_iota(jnp.int32, (LANES // 8, chans), 0))
    high_cos, high_sin = rotations(jnp.where(row == 0, 1, 2 * LANES * row))
    one_cos, one_sin = high_cos[:1], high_sin[:1]
    for a in range(LANES // 8):
        at = slice(8 * a, 8 * a + 8)
        cos = fine_cos * mid_cos[a:a + 1] - fine_sin * mid_sin[a:a + 1]
        sin = fine_sin * mid_cos[a:a + 1] + fine_cos * mid_sin[a:a + 1]
        low_ref[0, at] = cos
        low_ref[1, at] = sin
        low_ref[2, at] = cos * one_cos - sin * one_sin
        low_ref[3, at] = sin * one_cos + cos * one_sin

    def fill(i, _):
        at = pl.ds(pl.multiple_of(i * pack, pack), pack)
        for odd in (0, 1):
            low_cos = low_ref[2 * odd, at]
            low_sin = low_ref[2 * odd + 1, at]
            for k in range(count):
                if k == 0:
                    cos, sin = low_cos, low_sin
                else:
                    block_cos, block_sin = high_cos[k:k + 1], high_sin[k:k + 1]
                    cos = low_cos * block_cos - low_sin * block_sin
                    sin = low_sin * block_cos + low_cos * block_sin
                for part, value in ((0, cos), (1, sin)):
                    first = ((2 * odd + part) * count + k) * LANES
                    to = pl.ds(pl.multiple_of(first + i * pack, pack), pack)
                    table_ref[to] = value.astype(jnp.bfloat16)
        return 0

    lax.fori_loop(0, LANES // pack, fill, 0)
    parity = (1 - 2 * (delay & 1)).astype(jnp.float32)
    top = lax.broadcasted_iota(jnp.int32, (pack, chans), 0) == 0
    table_ref[quarter:quarter + pack] = jnp.where(top, parity, low_ref[1, :pack]).astype(
        jnp.bfloat16
    )

    dm_copy.wait()
    lane = lax.broadcasted_iota(jnp.int32, (8, LANES), 1)
    dm = jnp.broadcast_to(dm_ref[...], (8, dm_ref.shape[1]))
    dm = jnp.concatenate([dm] * (LANES // dm_ref.shape[1]), 1)
    dm = take_lanes(dm, (lane // rows) * (rows // 2) + lane % (rows // 2))
    dm = jnp.concatenate([dm] * (pack // 8), 0)
    lane = lax.broadcasted_iota(jnp.int32, (pack, LANES), 1)
    is_real = (lane // (rows // 2)) % 2 == 0
    flip = jnp.where(is_real, 1.0, -1.0)

    def turned(block):
        at = pl.ds(pl.multiple_of(block * own, LANES), own)
        sides = [
            lax.dot_general(
                split_ref[...], spec_ref[part, :, at], (((1,), (1,)), ((), ())),
                preferred_element_type=jnp.float32,
            ).astype(jnp.bfloat16)
            for part in (0, 1)
        ]
        return [
            jnp.concatenate([side[n * tile:(n + 1) * tile] for side in sides], 0) for n in (0, 1)
        ]

    def multiply(left, prod_ref):
        size = prod_ref.shape[1]
        prod_ref[...] = lax.dot_general(
            left, table_ref[:size], (((1,), (1,)), ((), ())), preferred_element_type=jnp.float32
        ).astype(jnp.bfloat16)

    def collect(block, even, prod_ref):
        size = half >> even
        pieces = []
        for r in range(tile // pack):
            spots = r * pack + lax.broadcasted_iota(jnp.int32, (pack, LANES), 0)
            if even:
                turns = ((block * tile + spots) * dm) & (2 * size - 1)
            else:
                turns = ((block * own + 2 * spots + 1) * dm) & (2 * size - 1)
            index = jnp.where(turns > size, 2 * size - turns, turns) & (size - 1)
            if even:
                which, places = index // LANES, list(range(count))
            else:
                which = (index >> 1) // LANES + (index & 1) * (2 * count)
                places = list(range(count)) + list(range(2 * count, 3 * count))
                index = index >> 1
            spot = (index & (LANES - 1)).astype(jnp.int16)
            which = which.astype(jnp.int16)
            acc = [None] * 4
            for b in places:
                hit = which == b
                for i, (part, table) in enumerate(((0, 0), (1, 1), (1, 0), (0, 1))):
                    top = part * tile + r * pack
                    left = (b + table * count) * LANES
                    piece = gather_lanes(prod_ref[top:top + pack, left:left + LANES], spot)
                    acc[i] = piece if acc[i] is None else jnp.where(hit, piece, acc[i])
            a, b, a2, b2 = [value.astype(jnp.float32) for value in acc]
            sign = jnp.where(turns > size, -flip, jnp.where(turns == 0, 0.0, flip))
            sums = jnp.where(is_real, a, a2) + sign * jnp.where(is_real, b, b2)
            pieces.append(
                jnp.where(turns == size, jnp.where(is_real, b2, b), sums).astype(jnp.bfloat16)
            )
        return pieces

    def compute(p):
        block = block_at(p)
        odd, even = turned(block)
        multiply(odd, odd_ref)
        multiply(even, even_ref)
        near = collect(block, 0, odd_ref)
        far = collect(block, 1, even_ref)
        part = len(near) // 2
        for t in (0, 1):
            picked = near[t * part:(t + 1) * part] + far[t * part:(t + 1) * part]
            at = pl.ds(pl.multiple_of(block * own + t * tile, LANES), tile)
            send_ref[:, :, at] = jnp.concatenate(picked, 0).T.reshape(groups, rows, tile)

    def chan_copy(p, offset):
        at = pl.ds(pl.multiple_of(block_at(p) * own, LANES), own)
        return pltpu.make_async_remote_copy(
            src_ref=send_ref.at[chan_at(offset), :, at],
            dst_ref=chan_recv.at[chan_size - offset, :, at],
            send_sem=chan_sems.at[0, offset, p],
            recv_sem=chan_sems.at[1, chan_size - offset, p],
            device_id={"chan": chan_at(offset)},
            device_id_type=MESH,
        )

    def bin_copy(block, piece):
        to = block + (0, 1, -1)[piece]
        begin, size, land = ((0, own, EDGE), (own - EDGE, EDGE, 0), (0, EDGE, EDGE + own))[piece]
        offset = lax.rem(to - my_bin + bin_size, bin_size)
        slot = lax.rem(bin_size - offset, bin_size)
        return pltpu.make_async_remote_copy(
            src_ref=sum_ref.at[:, pl.ds(pl.multiple_of(EDGE + block * own + begin, LANES), size)],
            dst_ref=bin_recv.at[slot, :, land:land + size],
            send_sem=bin_sems.at[0, piece, offset],
            recv_sem=bin_sems.at[1, piece, slot],
            device_id={"bin": to},
            device_id_type=MESH,
        )

    def each_piece(block, act):
        for piece in range(3):
            to = block + (0, 1, -1)[piece]

            @pl.when((to >= 0) & (to < bin_size) & (to != my_bin))
            def _():
                act(bin_copy(block, piece))

    def forward(p):
        block = block_at(p)
        at = pl.multiple_of(block * own, LANES)
        for offset in range(1, chan_size):
            chan_copy(p, chan_size - offset).wait_recv()
        total = send_ref[my_chan, :, pl.ds(at, own)].astype(jnp.float32)
        for offset in range(1, chan_size):
            total += chan_recv[offset, :, pl.ds(at, own)].astype(jnp.float32)
        sum_ref[:, pl.ds(pl.multiple_of(EDGE + at, LANES), own)] = total.astype(sum_ref.dtype)
        each_piece(block, lambda copy: copy.start())

    def one_block(p, _):
        spec_copy(p).wait()
        compute(p)

        @pl.when(p == 0)
        def _():
            pl.semaphore_wait(barrier, chan_size + bin_size - 2)

        for offset in range(1, chan_size):
            chan_copy(p, offset).start()
        return 0

    lax.fori_loop(0, bin_size, one_block, 0)
    for p in range(bin_size):
        forward(p)

    total = sum_ref[:, pl.ds(pl.multiple_of(my_bin * own, LANES), width)].astype(jnp.float32)
    for slot in range(1, bin_size):
        for piece in range(3):
            begin, size = ((EDGE, own), (0, EDGE), (EDGE + own, EDGE))[piece]
            sender = lax.rem(my_bin + slot, bin_size)
            comes = (True, my_bin > 0, my_bin < bin_size - 1)[piece]

            @pl.when(comes)
            def _():
                pltpu.make_async_remote_copy(
                    src_ref=sum_ref.at[:, begin:begin + size],
                    dst_ref=bin_recv.at[slot, :, begin:begin + size],
                    send_sem=bin_sems.at[0, piece, slot],
                    recv_sem=bin_sems.at[1, piece, slot],
                    device_id={"bin": sender},
                    device_id_type=MESH,
                ).wait_recv()

        total += bin_recv[slot].astype(jnp.float32)
    signal = (total * scale).astype(jnp.bfloat16).astype(jnp.float32)
    lane = lax.broadcasted_iota(jnp.int32, (rows, tile), 1)
    back = (lane >> 1) + (tile // 2) * (1 - (lane & 1))
    for t in range(width // tile):
        at = slice(t * tile, (t + 1) * tile)
        out_ref[:, at] = take_lanes(signal[:, at], back)

    def drain(p, _):
        for offset in range(1, chan_size):
            chan_copy(p, offset).wait_send()
        each_piece(block_at(p), lambda copy: copy.wait_send())
        return 0

    lax.fori_loop(0, bin_size, drain, 0)


def correlate_kernel(trials, signal_ref, bank_ref, ids_ref, out_hbm, taps_ref, power_ref, sems):
    _, templates, bins = power_ref.shape
    bank_size, taps = bank_ref.shape[1:]
    group = math.gcd(trials, 2)

    rows = lax.broadcasted_iota(jnp.int32, (bank_size, templates), 0)
    one_hot = (ids_ref[...] == rows).astype(jnp.bfloat16)
    back = (LANES - 1 - lax.broadcasted_iota(jnp.int32, (16, LANES), 1)).astype(jnp.int16)
    back = jnp.concatenate([back] * (templates // 16), 0)
    for part in (0, 1):
        chosen = lax.dot_general(
            one_hot, bank_ref[part], (((0,), (0,)), ((), ())), preferred_element_type=jnp.float32
        ).astype(jnp.bfloat16)
        for u in range(taps // LANES):
            at = u * LANES
            turned = gather_lanes(chosen[:, at:at + LANES], back)
            taps_ref[part * templates:(part + 1) * templates, at:at + LANES] = turned
            taps_ref[
                (1 - part) * templates:(2 - part) * templates, taps + at:taps + at + LANES
            ] = turned if part == 0 else -turned

    pack = 16
    length = bins + taps

    def out_copy(g):
        at = pl.ds(g * group, group)
        return pltpu.make_async_copy(power_ref.at[at], out_hbm.at[at], sems.at[g])

    def one_group(g, _):
        for t in range(group):
            trial = g * group + t
            hankel = []
            for part in (0, 1):
                line = signal_ref[pl.ds(part * trials + trial, 1), :]
                line = jnp.broadcast_to(line, (pack, length)).astype(jnp.bfloat16)
                rows = [
                    pltpu.roll(line, length + pack * a - (LANES - 1), 1, stride=1, stride_axis=0)
                    for a in range(LANES // pack)
                ]
                hankel.append(jnp.concatenate(rows, 0))
            wide = jnp.concatenate(
                [
                    hankel[part][:, u * LANES:u * LANES + bins]
                    for part in (0, 1)
                    for u in range(taps // LANES)
                ],
                0,
            )
            response = jnp.dot(taps_ref[...], wide, preferred_element_type=jnp.float32)
            real = response[:templates]
            imag = response[templates:]
            power_ref[trial] = (real * real + imag * imag).astype(power_ref.dtype)
        out_copy(g).start()
        return 0

    for g in range(trials // group):
        one_group(g, 0)
    for g in range(trials // group):
        out_copy(g).wait()


def local(spectra, dm_trials, chan_delay, template_bank, template_ids):
    chans, bins = spectra.shape[1:]
    samples = 2 * bins
    bin_size = lax.axis_size("bin")
    chan_size = lax.axis_size("chan")
    trials = dm_trials.shape[0] // chan_size
    templates = template_ids.shape[0]
    taps = template_bank.shape[2]
    own = bins // bin_size
    width = own + 2 * EDGE
    scale = 1.0 / math.sqrt(chan_delay.shape[0])
    if chans % LANES:
        rank = lax.axis_index("chan") * bin_size + lax.axis_index("bin")
        chan_delay = lax.dynamic_slice_in_dim(chan_delay, rank * chans, chans)
    vmem = pl.BlockSpec(memory_space=pltpu.VMEM)
    products = pltpu.VMEM((2 * LANES, 2 * min(bins, 1024)), jnp.float32)

    paired = (
        bins <= 1024 and bins % (4 * LANES) == 0 and own == 2 * LANES and chans % LANES == 0
        and trials * 2 * chan_size == LANES
    )
    if paired:
        hbm = pl.BlockSpec(memory_space=pltpu.HBM)
        signal = pl.pallas_call(
            functools.partial(paired_kernel, samples, scale),
            out_shape=jax.ShapeDtypeStruct((2 * trials, width), jnp.float32),
            in_specs=[hbm] * 3,
            out_specs=vmem,
            scratch_shapes=[
                pltpu.VMEM((2, chans, bins), jnp.bfloat16),
                pltpu.VMEM((1, chans), jnp.int32),
                pltpu.VMEM((1, dm_trials.shape[0]), jnp.int32),
                pltpu.VMEM((chan_size, 2 * trials, bins), jnp.bfloat16),
                pltpu.VMEM((2 * trials, bins + 2 * EDGE), jnp.bfloat16),
                pltpu.VMEM((chan_size, 2 * trials, bins), jnp.bfloat16),
                pltpu.VMEM((bin_size, 2 * trials, width), jnp.bfloat16),
                pltpu.VMEM((4, LANES, chans), jnp.float32),
                pltpu.VMEM((2 * bins, chans), jnp.bfloat16),
                pltpu.VMEM((own, own), jnp.bfloat16),
                pltpu.VMEM((2 * LANES, 2 * bins), jnp.bfloat16),
                pltpu.VMEM((2 * LANES, bins), jnp.bfloat16),
                pltpu.SemaphoreType.DMA((2 + bin_size,)),
                pltpu.SemaphoreType.DMA((2, chan_size, bin_size)),
                pltpu.SemaphoreType.DMA((2, 3, bin_size)),
            ],
            compiler_params=pltpu.CompilerParams(
                collective_id=0, has_side_effects=True, vmem_limit_bytes=24 * 2 ** 20
            ),
            name="dedisperse",
        )(*[
            pltpu.with_memory_space_constraint(x, pltpu.HBM)
            for x in (spectra, chan_delay[None, :], dm_trials[None, :])
        ])
    else:
        signal = pl.pallas_call(
            functools.partial(dedisperse_kernel, samples, scale),
            out_shape=jax.ShapeDtypeStruct((2 * trials, width), jnp.float32),
            in_specs=[vmem] * 3,
            out_specs=vmem,
            scratch_shapes=[
                pltpu.VMEM((chan_size, 2 * trials, bins), jnp.bfloat16),
                pltpu.VMEM((2 * trials, bins + 2 * EDGE), jnp.bfloat16),
                pltpu.VMEM((chan_size, 2 * trials, bins), jnp.bfloat16),
                pltpu.VMEM((bin_size, 2 * trials, width), jnp.bfloat16),
                pltpu.VMEM((chans, 2 * bins), jnp.bfloat16),
                pltpu.VMEM((chans, bins), jnp.bfloat16),
                pltpu.VMEM((own, own), jnp.bfloat16),
                pltpu.VMEM((own, own), jnp.bfloat16),
                products,
                products,
                pltpu.SemaphoreType.DMA((2, chan_size, bin_size)),
                pltpu.SemaphoreType.DMA((2, 3, bin_size)),
            ],
            compiler_params=pltpu.CompilerParams(collective_id=0, has_side_effects=True),
            name="dedisperse",
        )(spectra, chan_delay[None, :], dm_trials[None, :])

    return pl.pallas_call(
        functools.partial(correlate_kernel, trials),
        out_shape=jax.ShapeDtypeStruct((trials, templates, own), jnp.bfloat16),
        in_specs=[vmem] * 3,
        out_specs=pl.BlockSpec(memory_space=pltpu.HBM),
        scratch_shapes=[
            pltpu.VMEM((2 * templates, 2 * taps), jnp.bfloat16),
            pltpu.VMEM((trials, templates, own), jnp.bfloat16),
            pltpu.SemaphoreType.DMA((trials,)),
        ],
        compiler_params=pltpu.CompilerParams(vmem_limit_bytes=16 * 2 ** 20),
        name="templates",
    )(signal, template_bank, template_ids[None, :])


def solution(mesh):
    in_specs = (P(None, ("beam", "chan", "bin"), None), P(), P(), P(), P())
    out_specs = P(("beam", "chan"), None, "bin")
    return jax.shard_map(local, mesh=mesh, in_specs=in_specs, out_specs=out_specs, check_vma=False)
```

```python
import functools
import math

import jax
import jax.numpy as jnp
from jax import lax
from jax.experimental import pallas as pl
from jax.experimental.pallas import tpu as pltpu
from jax.sharding import PartitionSpec as P

EDGE = 128
LANES = 128
MESH = pl.DeviceIdType.MESH


def cos_sin(turns, samples):
    eighth = samples // 8
    quadrant = lax.shift_right_logical(turns + eighth, eighth.bit_length())
    rest = turns - quadrant * (2 * eighth)
    x = rest.astype(jnp.float32) * (2.0 * math.pi / samples)
    y = x * x
    c = 1.0 + y * (-0.5 + y * (1.0 / 24 + y * (-1.0 / 720 + y * (1.0 / 40320))))
    s = x * (1.0 + y * (-1.0 / 6 + y * (1.0 / 120 + y * (-1.0 / 5040 + y * (1.0 / 362880)))))
    swap = (quadrant & 1) == 1
    cos = jnp.where(swap, s, c)
    sin = jnp.where(swap, c, s)
    cos = jnp.where(((quadrant + 1) & 2) == 2, -cos, cos)
    sin = jnp.where((quadrant & 2) == 2, -sin, sin)
    return cos, sin


def take_lanes(x, index):
    return jnp.take_along_axis(x, index, axis=1, mode="promise_in_bounds")


def dedisperse_kernel(
    samples, scale, spec_ref, delay_ref, dm_ref, out_ref, send_ref, sum_ref, chan_recv, bin_recv,
    table_ref, even_ref, split_ref, merge_ref, prod_a, prod_b, chan_sems, bin_sems,
):
    bin_size = lax.axis_size("bin")
    chan_size = lax.axis_size("chan")
    my_bin = lax.axis_index("bin")
    my_chan = lax.axis_index("chan")
    chans = spec_ref.shape[1]
    bins = spec_ref.shape[2]
    half = samples // 2
    group = prod_a.shape[1] // 2
    blocks = group // LANES
    all_blocks = half // LANES
    groups, rows = send_ref.shape[:2]
    width = out_ref.shape[1]
    tile = LANES
    own = bins // bin_size
    tiles = own // tile
    padded = max(chans, LANES)

    def chan_at(offset):
        return lax.rem(my_chan + offset, chan_size)

    def bin_at(offset):
        return lax.rem(my_bin + offset, bin_size)

    barrier = pltpu.get_barrier_semaphore()

    def greet_chan(offset, _):
        pl.semaphore_signal(
            barrier, inc=1, device_id={"chan": chan_at(offset)}, device_id_type=MESH
        )
        return 0

    def greet_bin(offset, _):
        pl.semaphore_signal(barrier, inc=1, device_id={"bin": bin_at(offset)}, device_id_type=MESH)
        return 0

    lax.fori_loop(1, chan_size, greet_chan, 0)
    lax.fori_loop(1, bin_size, greet_bin, 0)

    if delay_ref.shape[1] == chans:
        delay = delay_ref[...]
    else:
        rank = lax.axis_index("chan") * bin_size + lax.axis_index("bin")
        delay = delay_ref[:, pl.ds(pl.multiple_of(rank * chans, LANES), chans)]
    if chans < padded:
        delay = jnp.concatenate([delay, jnp.zeros((1, padded - chans), jnp.int32)], 1)

    def rotations(count, stride):
        turns = lax.broadcasted_iota(jnp.int32, (count, padded), 0) * stride * delay
        return cos_sin(turns & (samples - 1), samples)

    fine_cos, fine_sin = rotations(8, 1)
    mid_cos, mid_sin = rotations(LANES // 8, 8)
    low_cos = jnp.concatenate(
        [fine_cos * mid_cos[a:a + 1] - fine_sin * mid_sin[a:a + 1] for a in range(LANES // 8)], 0
    ).T[:chans]
    low_sin = jnp.concatenate(
        [fine_sin * mid_cos[a:a + 1] + fine_cos * mid_sin[a:a + 1] for a in range(LANES // 8)], 0
    ).T[:chans]
    coarse_cos, coarse_sin = rotations(all_blocks + 8, LANES)
    fill_rows = jnp.zeros((LANES - all_blocks - 8, padded), jnp.float32)
    high_cos = jnp.concatenate([coarse_cos, fill_rows], 0).T[:chans]
    high_sin = jnp.concatenate([coarse_sin, fill_rows], 0).T[:chans]
    lane_ids = lax.broadcasted_iota(jnp.int32, (chans, LANES), 1)

    def fill(block, _):
        spread = jnp.full((chans, LANES), block, jnp.int32)
        block_cos = take_lanes(high_cos, spread)
        block_sin = take_lanes(high_sin, spread)
        at = pl.multiple_of(block * LANES, LANES)
        cos = low_cos * block_cos - low_sin * block_sin
        sin = low_sin * block_cos + low_cos * block_sin
        table_ref[:, pl.ds(at, LANES)] = cos.astype(jnp.bfloat16)
        table_ref[:, pl.ds(half + at, LANES)] = sin.astype(jnp.bfloat16)
        return 0

    lax.fori_loop(0, all_blocks, fill, 0)
    parity = take_lanes(high_cos, jnp.full((chans, LANES), all_blocks, jnp.int32))
    table_ref[:, half:half + LANES] = jnp.where(lane_ids == 0, parity, low_sin).astype(jnp.bfloat16)

    paired = half == group and tiles == 2 and half % (4 * LANES) == 0
    if paired:
        even_cos = low_cos * low_cos - low_sin * low_sin
        even_sin = 2.0 * low_sin * low_cos
        for block in range(all_blocks // 2):
            spread = jnp.full((chans, LANES), 2 * block, jnp.int32)
            block_cos = take_lanes(high_cos, spread)
            block_sin = take_lanes(high_sin, spread)
            at = block * LANES
            cos = even_cos * block_cos - even_sin * block_sin
            sin = even_sin * block_cos + even_cos * block_sin
            if block == 0:
                sin = jnp.where(lane_ids == 0, parity, sin)
            even_ref[:, at:at + LANES] = cos.astype(jnp.bfloat16)
            even_ref[:, half // 2 + at:half // 2 + at + LANES] = sin.astype(jnp.bfloat16)
        near = lax.broadcasted_iota(jnp.int32, (own, own), 0)
        far = lax.broadcasted_iota(jnp.int32, (own, own), 1)

        def source(spot):
            return jnp.where(spot < tile, 2 * spot + 1, 2 * (spot - tile))

        split_ref[...] = (near == source(far)).astype(jnp.float32).astype(jnp.bfloat16)
        merge_ref[...] = (far == source(near)).astype(jnp.float32).astype(jnp.bfloat16)

    lane = lax.broadcasted_iota(jnp.int32, (8, LANES), 1)
    is_real = (lane // (rows // 2)) % 2 == 0
    dm = jnp.broadcast_to(dm_ref[...], (8, dm_ref.shape[1]))
    dm = jnp.concatenate([dm] * (LANES // dm_ref.shape[1]), 1)
    dm = take_lanes(dm, (lane // rows) * (rows // 2) + lane % (rows // 2))

    def first_of(step):
        return pl.multiple_of(step * tile, tile)

    def multiply(step, g, prod_ref):
        at = pl.ds(first_of(step), tile)
        both = jnp.concatenate([spec_ref[0, :, at], spec_ref[1, :, at]], 1)
        for part in (0, 1):
            columns = pl.ds(pl.multiple_of(part * half + g * group, group), group)
            prod_ref[:, part * group:(part + 1) * group] = lax.dot_general(
                both, table_ref[:, columns], (((0,), (0,)), ((), ())),
                preferred_element_type=jnp.float32,
            )

    def turns_of(step, r):
        bin_ids = step * tile + r * 8 + lax.broadcasted_iota(jnp.int32, (8, LANES), 0)
        return (bin_ids * dm) & (samples - 1)

    def pick(turns, half, group, g, r, prod_ref, acc):
        folded = jnp.where(turns > half, 2 * half - turns, turns)
        index = folded & (half - 1)
        spot = index & (LANES - 1)
        which = index // LANES - g * (group // LANES)
        acc = list(acc)
        for b in range(group // LANES):
            hit = which == b
            for i, (part, table) in enumerate(((0, 0), (1, 1), (1, 0), (0, 1))):
                top = part * tile + r * 8
                left = table * group + b * LANES
                piece = take_lanes(prod_ref[top:top + 8, left:left + LANES], spot)
                acc[i] = piece if acc[i] is None else jnp.where(hit, piece, acc[i])
        return acc

    def finish(turns, half, acc):
        sign = jnp.where(turns > half, -1.0, jnp.where(turns == 0, 0.0, 1.0))
        a, b, a2, b2 = acc
        real = jnp.where(turns == half, b2, a + sign * b)
        imag = jnp.where(turns == half, b, a2 - sign * b2)
        return jnp.where(is_real, real, imag)

    def split_multiply(block, even, prod_ref):
        at = pl.ds(pl.multiple_of(block * own, LANES), own)
        chosen = split_ref[:, even * tile:(even + 1) * tile]
        both = jnp.concatenate(
            [
                jnp.dot(spec_ref[part, :, at], chosen, preferred_element_type=jnp.float32)
                for part in (0, 1)
            ],
            1,
        ).astype(jnp.bfloat16)
        size = 2 * half // (1 + even)
        prod_ref[:, :size] = lax.dot_general(
            both, (even_ref if even else table_ref)[...], (((0,), (0,)), ((), ())),
            preferred_element_type=jnp.float32,
        )

    def split_gather(block, even, prod_ref):
        pieces = []
        for r in range(tile // 8):
            spots = r * 8 + lax.broadcasted_iota(jnp.int32, (8, LANES), 0)
            bin_ids = block * own + 2 * spots + (1 - even)
            turns = ((bin_ids * dm) & (samples - 1)) >> even
            size = half >> even
            acc = pick(turns, size, size, 0, r, prod_ref, [None] * 4)
            pieces.append(finish(turns, size, acc))
        return pieces

    def put(step, pieces):
        block = jnp.concatenate(pieces, 0).T
        at = pl.ds(first_of(step), tile)
        send_ref[:, :, at] = block.reshape(groups, rows, tile).astype(send_ref.dtype)

    def block_at(p):
        return bin_at(p + 1)

    def compute(p):
        base = block_at(p) * tiles

        def one_tile(t, _):
            step = base + t

            def one_group(g, accs):
                multiply(step, g, prod_a)
                new = []
                for r in range(tile // 8):
                    new += pick(
                        turns_of(step, r), half, group, g, r, prod_a, accs[4 * r:4 * r + 4]
                    )
                return tuple(new)

            zero = jnp.zeros((8, LANES), jnp.float32)
            accs = lax.fori_loop(0, half // group, one_group, (zero,) * (4 * (tile // 8)))
            put(step, [
                finish(turns_of(step, r), half, accs[4 * r:4 * r + 4]) for r in range(tile // 8)
            ])
            return 0

        if paired:
            block = block_at(p)
            split_multiply(block, 1, prod_b)
            pieces = split_gather(block, 0, prod_a)
            split_multiply(block_at(jnp.minimum(p + 1, bin_size - 1)), 0, prod_a)
            pieces += split_gather(block, 1, prod_b)
            merged = lax.dot_general(
                jnp.concatenate(pieces, 0).astype(jnp.bfloat16), merge_ref[...],
                (((0,), (0,)), ((), ())), preferred_element_type=jnp.float32,
            )
            at = pl.ds(pl.multiple_of(block * own, LANES), own)
            send_ref[:, :, at] = merged.reshape(groups, rows, own).astype(send_ref.dtype)
        else:
            lax.fori_loop(0, tiles, one_tile, 0)

    def chan_copy(p, offset):
        at = pl.ds(pl.multiple_of(block_at(p) * own, LANES), own)
        return pltpu.make_async_remote_copy(
            src_ref=send_ref.at[chan_at(offset), :, at],
            dst_ref=chan_recv.at[chan_size - offset, :, at],
            send_sem=chan_sems.at[0, offset, p],
            recv_sem=chan_sems.at[1, chan_size - offset, p],
            device_id={"chan": chan_at(offset)},
            device_id_type=MESH,
        )

    def bin_copy(block, piece):
        to = block + (0, 1, -1)[piece]
        begin, size, land = ((0, own, EDGE), (own - EDGE, EDGE, 0), (0, EDGE, EDGE + own))[piece]
        offset = lax.rem(to - my_bin + bin_size, bin_size)
        slot = lax.rem(bin_size - offset, bin_size)
        return pltpu.make_async_remote_copy(
            src_ref=sum_ref.at[:, pl.ds(pl.multiple_of(EDGE + block * own + begin, LANES), size)],
            dst_ref=bin_recv.at[slot, :, land:land + size],
            send_sem=bin_sems.at[0, piece, offset],
            recv_sem=bin_sems.at[1, piece, slot],
            device_id={"bin": to},
            device_id_type=MESH,
        )

    def each_piece(block, act):
        for piece in range(3):
            to = block + (0, 1, -1)[piece]

            @pl.when((to >= 0) & (to < bin_size) & (to != my_bin))
            def _():
                act(bin_copy(block, piece))

    def forward(p):
        block = block_at(p)
        at = pl.multiple_of(block * own, LANES)
        for offset in range(1, chan_size):
            chan_copy(p, chan_size - offset).wait_recv()
        total = send_ref[my_chan, :, pl.ds(at, own)].astype(jnp.float32)
        for offset in range(1, chan_size):
            total += chan_recv[offset, :, pl.ds(at, own)].astype(jnp.float32)
        sum_ref[:, pl.ds(pl.multiple_of(EDGE + at, LANES), own)] = total.astype(sum_ref.dtype)
        each_piece(block, lambda copy: copy.start())

    edge = jnp.zeros((rows, EDGE), sum_ref.dtype)
    sum_ref[:, :EDGE] = edge
    sum_ref[:, EDGE + bins:] = edge

    @pl.when(my_bin == 0)
    def _():
        for slot in range(1, bin_size):
            bin_recv[slot, :, :EDGE] = edge

    @pl.when(my_bin == bin_size - 1)
    def _():
        for slot in range(1, bin_size):
            bin_recv[slot, :, EDGE + own:] = edge

    if paired:
        split_multiply(block_at(0), 0, prod_a)
    pl.semaphore_wait(barrier, chan_size + bin_size - 2)

    def one_block(p, _):
        compute(p)
        for offset in range(1, chan_size):
            chan_copy(p, offset).start()

        @pl.when(p > 0)
        def _():
            forward(p - 1)

        return 0

    lax.fori_loop(0, bin_size, one_block, 0)
    forward(bin_size - 1)

    total = sum_ref[:, pl.ds(pl.multiple_of(my_bin * own, LANES), width)].astype(jnp.float32)
    for slot in range(1, bin_size):
        for piece in range(3):
            begin, size = ((EDGE, own), (0, EDGE), (EDGE + own, EDGE))[piece]
            sender = lax.rem(my_bin + slot, bin_size)
            comes = (True, my_bin > 0, my_bin < bin_size - 1)[piece]

            @pl.when(comes)
            def _():
                pltpu.make_async_remote_copy(
                    src_ref=sum_ref.at[:, begin:begin + size],
                    dst_ref=bin_recv.at[slot, :, begin:begin + size],
                    send_sem=bin_sems.at[0, piece, slot],
                    recv_sem=bin_sems.at[1, piece, slot],
                    device_id={"bin": sender},
                    device_id_type=MESH,
                ).wait_recv()

        total += bin_recv[slot].astype(jnp.float32)
    out_ref[...] = (total * scale).astype(jnp.bfloat16).astype(jnp.float32)

    def drain(p, _):
        for offset in range(1, chan_size):
            chan_copy(p, offset).wait_send()
        each_piece(block_at(p), lambda copy: copy.wait_send())
        return 0

    lax.fori_loop(0, bin_size, drain, 0)


def gather_lanes(x, index):
    return lax.gather(
        x, index[:, :, None],
        dimension_numbers=lax.GatherDimensionNumbers(
            offset_dims=(), collapsed_slice_dims=(1,), start_index_map=(1,),
            operand_batching_dims=(0,), start_indices_batching_dims=(0,),
        ),
        slice_sizes=(1, 1), mode="promise_in_bounds",
    )


def paired_kernel(
    samples, scale, spec_hbm, delay_hbm, dm_hbm, out_ref, spec_ref, delay_ref, dm_ref, send_ref,
    sum_ref, chan_recv, bin_recv, low_ref, table_ref, split_ref, odd_ref, even_ref,
    load_sems, chan_sems, bin_sems,
):
    bin_size = lax.axis_size("bin")
    chan_size = lax.axis_size("chan")
    my_bin = lax.axis_index("bin")
    my_chan = lax.axis_index("chan")
    chans = spec_ref.shape[1]
    bins = spec_ref.shape[2]
    half = samples // 2
    quarter = half // 2
    groups, _, rows, _ = send_ref.shape
    width = out_ref.shape[1]
    tile = LANES
    own = bins // bin_size
    cut = own // tile
    spans = width // tile
    count = quarter // LANES
    pack = 16

    pairs = chan_size // 2
    partners = list(range(2, chan_size)) + [1]

    def chan_at(offset):
        return (my_chan // 2 + offset // 2) % pairs * 2 + (my_chan + offset) % 2

    def mirror(offset):
        return (pairs - offset // 2) % pairs * 2 + offset % 2

    def bin_at(offset):
        return lax.rem(my_bin + offset, bin_size)

    def block_at(p):
        return bin_at(p + 1)

    def spec_copy(p):
        at = pl.ds(pl.multiple_of(block_at(p) * own, LANES), own)
        return pltpu.make_async_copy(
            spec_hbm.at[:, :, at], spec_ref.at[:, :, at], load_sems.at[2 + p]
        )

    rank = my_chan * bin_size + my_bin
    mine = pl.ds(pl.multiple_of(rank * chans, LANES), chans)
    delay_copy = pltpu.make_async_copy(delay_hbm.at[:, mine], delay_ref, load_sems.at[0])
    dm_copy = pltpu.make_async_copy(dm_hbm, dm_ref, load_sems.at[1])
    delay_copy.start()
    dm_copy.start()
    for p in range(bin_size):
        spec_copy(p).start()

    barrier = pltpu.get_barrier_semaphore()

    def greet_chan(offset, _):
        pl.semaphore_signal(
            barrier, inc=1, device_id={"chan": chan_at(offset)}, device_id_type=MESH
        )
        return 0

    def greet_bin(offset, _):
        pl.semaphore_signal(barrier, inc=1, device_id={"bin": bin_at(offset)}, device_id_type=MESH)
        return 0

    for offset in range(1, bin_size):
        greet_bin(offset, 0)
    for offset in partners:
        greet_chan(offset, 0)

    near = lax.broadcasted_iota(jnp.int32, (own, own), 0)
    far = lax.broadcasted_iota(jnp.int32, (own, own), 1)
    source = jnp.where(near < tile, 2 * near + 1, 2 * (near - tile))
    split_ref[...] = (far == source).astype(jnp.float32).astype(jnp.bfloat16)

    edge = jnp.zeros((rows, tile), sum_ref.dtype)
    sum_ref[0] = edge
    sum_ref[sum_ref.shape[0] - 1] = edge

    @pl.when(my_bin == 0)
    def _():
        for slot in range(1, bin_size):
            bin_recv[slot, 0] = edge

    @pl.when(my_bin == bin_size - 1)
    def _():
        for slot in range(1, bin_size):
            bin_recv[slot, spans - 1] = edge

    delay_copy.wait()
    delay = delay_ref[...]

    def rotations(factor):
        return cos_sin((factor * delay) & (samples - 1), samples)

    row = lax.broadcasted_iota(jnp.int32, (8, chans), 0)
    fine_cos, fine_sin = rotations(2 * row)
    mid_cos, mid_sin = rotations(2 * 8 * lax.broadcasted_iota(jnp.int32, (LANES // 8, chans), 0))
    high_cos, high_sin = rotations(jnp.where(row == 0, 1, 2 * LANES * row))
    one_cos, one_sin = high_cos[:1], high_sin[:1]
    for a in range(LANES // 8):
        at = slice(8 * a, 8 * a + 8)
        cos = fine_cos * mid_cos[a:a + 1] - fine_sin * mid_sin[a:a + 1]
        sin = fine_sin * mid_cos[a:a + 1] + fine_cos * mid_sin[a:a + 1]
        low_ref[0, at] = cos
        low_ref[1, at] = sin
        low_ref[2, at] = cos * one_cos - sin * one_sin
        low_ref[3, at] = sin * one_cos + cos * one_sin

    def fill(i, _):
        at = pl.ds(pl.multiple_of(i * pack, pack), pack)
        for odd in (0, 1):
            low_cos = low_ref[2 * odd, at]
            low_sin = low_ref[2 * odd + 1, at]
            for k in range(count):
                if k == 0:
                    cos, sin = low_cos, low_sin
                else:
                    block_cos, block_sin = high_cos[k:k + 1], high_sin[k:k + 1]
                    cos = low_cos * block_cos - low_sin * block_sin
                    sin = low_sin * block_cos + low_cos * block_sin
                for part, value in ((0, cos), (1, sin)):
                    first = ((2 * odd + part) * count + k) * LANES
                    to = pl.ds(pl.multiple_of(first + i * pack, pack), pack)
                    table_ref[to] = value.astype(jnp.bfloat16)
        return 0

    lax.fori_loop(0, LANES // pack, fill, 0)
    parity = (1 - 2 * (delay & 1)).astype(jnp.float32)
    top = lax.broadcasted_iota(jnp.int32, (pack, chans), 0) == 0
    table_ref[quarter:quarter + pack] = jnp.where(top, parity, low_ref[1, :pack]).astype(
        jnp.bfloat16
    )

    dm_copy.wait()
    lane = lax.broadcasted_iota(jnp.int32, (8, LANES), 1)
    dm = jnp.broadcast_to(dm_ref[...], (8, dm_ref.shape[1]))
    dm = jnp.concatenate([dm] * (LANES // dm_ref.shape[1]), 1)
    dm = take_lanes(dm, (lane // rows) * (rows // 2) + lane % (rows // 2))
    dm = jnp.concatenate([dm] * (pack // 8), 0)
    lane = lax.broadcasted_iota(jnp.int32, (pack, LANES), 1)
    real = 1 - (lane // (rows // 2)) % 2
    is_real = real.astype(jnp.int16) == 1
    flip = (2 * real - 1).astype(jnp.float32)

    def turned(block):
        at = pl.ds(pl.multiple_of(block * own, LANES), own)
        sides = [
            lax.dot_general(
                split_ref[...], spec_ref[part, :, at], (((1,), (1,)), ((), ())),
                preferred_element_type=jnp.float32,
            ).astype(jnp.bfloat16)
            for part in (0, 1)
        ]
        return [
            jnp.concatenate([side[n * tile:(n + 1) * tile] for side in sides], 0) for n in (0, 1)
        ]

    def multiply(left, prod_ref):
        size = prod_ref.shape[1]
        prod_ref[...] = lax.dot_general(
            left, table_ref[:size], (((1,), (1,)), ((), ())), preferred_element_type=jnp.float32
        ).astype(jnp.bfloat16)

    spots = lax.broadcasted_iota(jnp.int32, (pack, LANES), 0)
    steps = [[(spots * factor + shift) * dm for factor, shift in ((2, 1), (1, 0))],
             [factor * pack * dm for factor in (2, 1)]]
    flip = flip.astype(jnp.bfloat16)
    zero = jnp.zeros((pack, LANES), jnp.bfloat16)

    def collect(block, even, prod_ref):
        size = half >> even
        start = steps[0][even] + (block * (own >> even)) * dm
        places = list(range(count))
        if not even:
            places += list(range(2 * count, 3 * count))
        pieces = []
        for r in range(tile // pack):
            turns = (start + r * steps[1][even]) & (2 * size - 1)
            index = jnp.minimum(turns, 2 * size - turns) & (size - 1)
            if even:
                which = index >> 7
            else:
                which = (index >> 8) + (index & 1) * (2 * count)
                index = index >> 1
            spot = (index & (LANES - 1)).astype(jnp.int16)
            which = which.astype(jnp.int16)
            turns = turns.astype(jnp.int16)
            acc = [None] * 4
            for b in places:
                hit = which == b
                for i, (part, table) in enumerate(((0, 0), (1, 1), (1, 0), (0, 1))):
                    top = part * tile + r * pack
                    left = (b + table * count) * LANES
                    piece = gather_lanes(prod_ref[top:top + pack, left:left + LANES], spot)
                    acc[i] = piece if acc[i] is None else jnp.where(hit, piece, acc[i])
            a, b, a2, b2 = acc
            sign = jnp.where(turns > size, -flip, flip)
            side = jnp.where(turns == 0, zero, jnp.where(is_real, b, b2) * sign)
            sums = jnp.where(is_real, a, a2) + side
            pieces.append(jnp.where(turns == size, jnp.where(is_real, b2, b), sums))
        return pieces

    def compute(p):
        block = block_at(p)
        odd, even = turned(block)
        multiply(odd, odd_ref)
        multiply(even, even_ref)
        near = collect(block, 0, odd_ref)
        far = collect(block, 1, even_ref)
        part = len(near) // 2
        for t in (0, 1):
            picked = near[t * part:(t + 1) * part] + far[t * part:(t + 1) * part]
            send_ref[:, block * cut + t] = jnp.concatenate(picked, 0).T.reshape(groups, rows, tile)

    def chan_copy(p, offset):
        at = pl.ds(block_at(p) * cut, cut)
        return pltpu.make_async_remote_copy(
            src_ref=send_ref.at[chan_at(offset), at],
            dst_ref=chan_recv.at[mirror(offset), at],
            send_sem=chan_sems.at[0, offset, p],
            recv_sem=chan_sems.at[1, mirror(offset), p],
            device_id={"chan": chan_at(offset)},
            device_id_type=MESH,
        )

    def bin_copy(block, piece):
        to = block + (0, 1, -1)[piece]
        begin, size, land = ((0, cut, 1), (cut - 1, 1, 0), (0, 1, spans - 1))[piece]
        offset = lax.rem(to - my_bin + bin_size, bin_size)
        slot = lax.rem(bin_size - offset, bin_size)
        return pltpu.make_async_remote_copy(
            src_ref=sum_ref.at[pl.ds(1 + block * cut + begin, size)],
            dst_ref=bin_recv.at[slot, land:land + size],
            send_sem=bin_sems.at[0, piece, offset],
            recv_sem=bin_sems.at[1, piece, slot],
            device_id={"bin": to},
            device_id_type=MESH,
        )

    def each_piece(block, act):
        for piece in range(3):
            to = block + (0, 1, -1)[piece]

            @pl.when((to >= 0) & (to < bin_size) & (to != my_bin))
            def _():
                act(bin_copy(block, piece))

    def forward(p):
        block = block_at(p)
        at = pl.ds(block * cut, cut)
        for offset in range(1, chan_size):
            chan_copy(p, mirror(offset)).wait_recv()
        total = send_ref[my_chan, at].astype(jnp.float32)
        for offset in range(1, chan_size):
            total += chan_recv[offset, at].astype(jnp.float32)
        sum_ref[pl.ds(1 + block * cut, cut)] = total.astype(sum_ref.dtype)
        each_piece(block, lambda copy: copy.start())

    def one_block(p, _):
        spec_copy(p).wait()
        compute(p)

        @pl.when(p == 0)
        def _():
            pl.semaphore_wait(barrier, chan_size + bin_size - 2)

        for offset in partners:
            chan_copy(p, offset).start()
        return 0

    lax.fori_loop(0, bin_size, one_block, 0)
    for p in range(bin_size):
        forward(p)

    total = sum_ref[pl.ds(my_bin * cut, spans)].astype(jnp.float32)
    for slot in range(1, bin_size):
        for piece in range(3):
            begin, size = ((1, cut), (0, 1), (spans - 1, 1))[piece]
            sender = lax.rem(my_bin + slot, bin_size)
            comes = (True, my_bin > 0, my_bin < bin_size - 1)[piece]

            @pl.when(comes)
            def _():
                pltpu.make_async_remote_copy(
                    src_ref=sum_ref.at[begin:begin + size],
                    dst_ref=bin_recv.at[slot, begin:begin + size],
                    send_sem=bin_sems.at[0, piece, slot],
                    recv_sem=bin_sems.at[1, piece, slot],
                    device_id={"bin": sender},
                    device_id_type=MESH,
                ).wait_recv()

        total += bin_recv[slot].astype(jnp.float32)
    signal = (total * scale).astype(jnp.bfloat16).astype(jnp.float32)
    lane = lax.broadcasted_iota(jnp.int32, (rows, tile), 1)
    back = (lane >> 1) + (tile // 2) * (1 - (lane & 1))
    for t in range(spans):
        out_ref[:, t * tile:(t + 1) * tile] = take_lanes(signal[t], back)

    def drain(p, _):
        for offset in range(1, chan_size):
            chan_copy(p, offset).wait_send()
        each_piece(block_at(p), lambda copy: copy.wait_send())
        return 0

    lax.fori_loop(0, bin_size, drain, 0)


def correlate_kernel(trials, signal_ref, bank_ref, ids_ref, out_hbm, taps_ref, power_ref, sems):
    _, templates, bins = power_ref.shape
    bank_size, taps = bank_ref.shape[1:]
    group = math.gcd(trials, 2)

    rows = lax.broadcasted_iota(jnp.int32, (bank_size, templates), 0)
    one_hot = (ids_ref[...] == rows).astype(jnp.bfloat16)
    back = (LANES - 1 - lax.broadcasted_iota(jnp.int32, (16, LANES), 1)).astype(jnp.int16)
    back = jnp.concatenate([back] * (templates // 16), 0)
    for part in (0, 1):
        chosen = lax.dot_general(
            one_hot, bank_ref[part], (((0,), (0,)), ((), ())), preferred_element_type=jnp.float32
        ).astype(jnp.bfloat16)
        for u in range(taps // LANES):
            at = u * LANES
            turned = gather_lanes(chosen[:, at:at + LANES], back)
            taps_ref[part * templates:(part + 1) * templates, at:at + LANES] = turned
            taps_ref[
                (1 - part) * templates:(2 - part) * templates, taps + at:taps + at + LANES
            ] = turned if part == 0 else -turned

    pack = 16
    length = bins + taps

    def out_copy(g):
        at = pl.ds(g * group, group)
        return pltpu.make_async_copy(power_ref.at[at], out_hbm.at[at], sems.at[g])

    def one_group(g, _):
        for t in range(group):
            trial = g * group + t
            hankel = []
            for part in (0, 1):
                line = signal_ref[pl.ds(part * trials + trial, 1), :]
                line = jnp.broadcast_to(line, (pack, length)).astype(jnp.bfloat16)
                rows = [
                    pltpu.roll(line, length + pack * a - (LANES - 1), 1, stride=1, stride_axis=0)
                    for a in range(LANES // pack)
                ]
                hankel.append(jnp.concatenate(rows, 0))
            wide = jnp.concatenate(
                [
                    hankel[part][:, u * LANES:u * LANES + bins]
                    for part in (0, 1)
                    for u in range(taps // LANES)
                ],
                0,
            )
            response = jnp.dot(taps_ref[...], wide, preferred_element_type=jnp.float32)
            real = response[:templates]
            imag = response[templates:]
            power_ref[trial] = (real * real + imag * imag).astype(power_ref.dtype)
        out_copy(g).start()
        return 0

    for g in range(trials // group):
        one_group(g, 0)
    for g in range(trials // group):
        out_copy(g).wait()


def local(spectra, dm_trials, chan_delay, template_bank, template_ids):
    chans, bins = spectra.shape[1:]
    samples = 2 * bins
    bin_size = lax.axis_size("bin")
    chan_size = lax.axis_size("chan")
    trials = dm_trials.shape[0] // chan_size
    templates = template_ids.shape[0]
    taps = template_bank.shape[2]
    own = bins // bin_size
    width = own + 2 * EDGE
    scale = 1.0 / math.sqrt(chan_delay.shape[0])
    if chans % LANES:
        rank = lax.axis_index("chan") * bin_size + lax.axis_index("bin")
        chan_delay = lax.dynamic_slice_in_dim(chan_delay, rank * chans, chans)
    vmem = pl.BlockSpec(memory_space=pltpu.VMEM)
    products = pltpu.VMEM((2 * LANES, 2 * min(bins, 1024)), jnp.float32)

    paired = (
        bins <= 1024 and bins % (4 * LANES) == 0 and own == 2 * LANES and chans % LANES == 0
        and trials * 2 * chan_size == LANES and chan_size % 2 == 0
    )
    if paired:
        hbm = pl.BlockSpec(memory_space=pltpu.HBM)
        signal = pl.pallas_call(
            functools.partial(paired_kernel, samples, scale),
            out_shape=jax.ShapeDtypeStruct((2 * trials, width), jnp.float32),
            in_specs=[hbm] * 3,
            out_specs=vmem,
            scratch_shapes=[
                pltpu.VMEM((2, chans, bins), jnp.bfloat16),
                pltpu.VMEM((1, chans), jnp.int32),
                pltpu.VMEM((1, dm_trials.shape[0]), jnp.int32),
                pltpu.VMEM((chan_size, bins // LANES, 2 * trials, LANES), jnp.bfloat16),
                pltpu.VMEM((bins // LANES + 2, 2 * trials, LANES), jnp.bfloat16),
                pltpu.VMEM((chan_size, bins // LANES, 2 * trials, LANES), jnp.bfloat16),
                pltpu.VMEM((bin_size, width // LANES, 2 * trials, LANES), jnp.bfloat16),
                pltpu.VMEM((4, LANES, chans), jnp.float32),
                pltpu.VMEM((2 * bins, chans), jnp.bfloat16),
                pltpu.VMEM((own, own), jnp.bfloat16),
                pltpu.VMEM((2 * LANES, 2 * bins), jnp.bfloat16),
                pltpu.VMEM((2 * LANES, bins), jnp.bfloat16),
                pltpu.SemaphoreType.DMA((2 + bin_size,)),
                pltpu.SemaphoreType.DMA((2, chan_size, bin_size)),
                pltpu.SemaphoreType.DMA((2, 3, bin_size)),
            ],
            compiler_params=pltpu.CompilerParams(
                collective_id=0, has_side_effects=True, vmem_limit_bytes=24 * 2 ** 20
            ),
            name="dedisperse",
        )(*[
            pltpu.with_memory_space_constraint(x, pltpu.HBM)
            for x in (spectra, chan_delay[None, :], dm_trials[None, :])
        ])
    else:
        signal = pl.pallas_call(
            functools.partial(dedisperse_kernel, samples, scale),
            out_shape=jax.ShapeDtypeStruct((2 * trials, width), jnp.float32),
            in_specs=[vmem] * 3,
            out_specs=vmem,
            scratch_shapes=[
                pltpu.VMEM((chan_size, 2 * trials, bins), jnp.bfloat16),
                pltpu.VMEM((2 * trials, bins + 2 * EDGE), jnp.bfloat16),
                pltpu.VMEM((chan_size, 2 * trials, bins), jnp.bfloat16),
                pltpu.VMEM((bin_size, 2 * trials, width), jnp.bfloat16),
                pltpu.VMEM((chans, 2 * bins), jnp.bfloat16),
                pltpu.VMEM((chans, bins), jnp.bfloat16),
                pltpu.VMEM((own, own), jnp.bfloat16),
                pltpu.VMEM((own, own), jnp.bfloat16),
                products,
                products,
                pltpu.SemaphoreType.DMA((2, chan_size, bin_size)),
                pltpu.SemaphoreType.DMA((2, 3, bin_size)),
            ],
            compiler_params=pltpu.CompilerParams(collective_id=0, has_side_effects=True),
            name="dedisperse",
        )(spectra, chan_delay[None, :], dm_trials[None, :])

    return pl.pallas_call(
        functools.partial(correlate_kernel, trials),
        out_shape=jax.ShapeDtypeStruct((trials, templates, own), jnp.bfloat16),
        in_specs=[vmem] * 3,
        out_specs=pl.BlockSpec(memory_space=pltpu.HBM),
        scratch_shapes=[
            pltpu.VMEM((2 * templates, 2 * taps), jnp.bfloat16),
            pltpu.VMEM((trials, templates, own), jnp.bfloat16),
            pltpu.SemaphoreType.DMA((trials,)),
        ],
        compiler_params=pltpu.CompilerParams(vmem_limit_bytes=16 * 2 ** 20),
        name="templates",
    )(signal, template_bank, template_ids[None, :])


def solution(mesh):
    in_specs = (P(None, ("beam", "chan", "bin"), None), P(), P(), P(), P())
    out_specs = P(("beam", "chan"), None, "bin")
    return jax.shard_map(local, mesh=mesh, in_specs=in_specs, out_specs=out_specs, check_vma=False)
```

```python
import functools
import math

import jax
import jax.numpy as jnp
from jax import lax
from jax.experimental import pallas as pl
from jax.experimental.pallas import tpu as pltpu
from jax.sharding import PartitionSpec as P

EDGE = 128
LANES = 128
MESH = pl.DeviceIdType.MESH


def cos_sin(turns, samples):
    eighth = samples // 8
    quadrant = lax.shift_right_logical(turns + eighth, eighth.bit_length())
    rest = turns - quadrant * (2 * eighth)
    x = rest.astype(jnp.float32) * (2.0 * math.pi / samples)
    y = x * x
    c = 1.0 + y * (-0.5 + y * (1.0 / 24 + y * (-1.0 / 720 + y * (1.0 / 40320))))
    s = x * (1.0 + y * (-1.0 / 6 + y * (1.0 / 120 + y * (-1.0 / 5040 + y * (1.0 / 362880)))))
    swap = (quadrant & 1) == 1
    cos = jnp.where(swap, s, c)
    sin = jnp.where(swap, c, s)
    cos = jnp.where(((quadrant + 1) & 2) == 2, -cos, cos)
    sin = jnp.where((quadrant & 2) == 2, -sin, sin)
    return cos, sin


def take_lanes(x, index):
    return jnp.take_along_axis(x, index, axis=1, mode="promise_in_bounds")


def dedisperse_kernel(
    samples, scale, spec_ref, delay_ref, dm_ref, out_ref, send_ref, sum_ref, chan_recv, bin_recv,
    table_ref, even_ref, split_ref, merge_ref, prod_a, prod_b, chan_sems, bin_sems,
):
    bin_size = lax.axis_size("bin")
    chan_size = lax.axis_size("chan")
    my_bin = lax.axis_index("bin")
    my_chan = lax.axis_index("chan")
    chans = spec_ref.shape[1]
    bins = spec_ref.shape[2]
    half = samples // 2
    group = prod_a.shape[1] // 2
    blocks = group // LANES
    all_blocks = half // LANES
    groups, rows = send_ref.shape[:2]
    width = out_ref.shape[1]
    tile = LANES
    own = bins // bin_size
    tiles = own // tile
    padded = max(chans, LANES)

    def chan_at(offset):
        return lax.rem(my_chan + offset, chan_size)

    def bin_at(offset):
        return lax.rem(my_bin + offset, bin_size)

    barrier = pltpu.get_barrier_semaphore()

    def greet_chan(offset, _):
        pl.semaphore_signal(
            barrier, inc=1, device_id={"chan": chan_at(offset)}, device_id_type=MESH
        )
        return 0

    def greet_bin(offset, _):
        pl.semaphore_signal(barrier, inc=1, device_id={"bin": bin_at(offset)}, device_id_type=MESH)
        return 0

    lax.fori_loop(1, chan_size, greet_chan, 0)
    lax.fori_loop(1, bin_size, greet_bin, 0)

    if delay_ref.shape[1] == chans:
        delay = delay_ref[...]
    else:
        rank = lax.axis_index("chan") * bin_size + lax.axis_index("bin")
        delay = delay_ref[:, pl.ds(pl.multiple_of(rank * chans, LANES), chans)]
    if chans < padded:
        delay = jnp.concatenate([delay, jnp.zeros((1, padded - chans), jnp.int32)], 1)

    def rotations(count, stride):
        turns = lax.broadcasted_iota(jnp.int32, (count, padded), 0) * stride * delay
        return cos_sin(turns & (samples - 1), samples)

    fine_cos, fine_sin = rotations(8, 1)
    mid_cos, mid_sin = rotations(LANES // 8, 8)
    low_cos = jnp.concatenate(
        [fine_cos * mid_cos[a:a + 1] - fine_sin * mid_sin[a:a + 1] for a in range(LANES // 8)], 0
    ).T[:chans]
    low_sin = jnp.concatenate(
        [fine_sin * mid_cos[a:a + 1] + fine_cos * mid_sin[a:a + 1] for a in range(LANES // 8)], 0
    ).T[:chans]
    coarse_cos, coarse_sin = rotations(all_blocks + 8, LANES)
    fill_rows = jnp.zeros((LANES - all_blocks - 8, padded), jnp.float32)
    high_cos = jnp.concatenate([coarse_cos, fill_rows], 0).T[:chans]
    high_sin = jnp.concatenate([coarse_sin, fill_rows], 0).T[:chans]
    lane_ids = lax.broadcasted_iota(jnp.int32, (chans, LANES), 1)

    def fill(block, _):
        spread = jnp.full((chans, LANES), block, jnp.int32)
        block_cos = take_lanes(high_cos, spread)
        block_sin = take_lanes(high_sin, spread)
        at = pl.multiple_of(block * LANES, LANES)
        cos = low_cos * block_cos - low_sin * block_sin
        sin = low_sin * block_cos + low_cos * block_sin
        table_ref[:, pl.ds(at, LANES)] = cos.astype(jnp.bfloat16)
        table_ref[:, pl.ds(half + at, LANES)] = sin.astype(jnp.bfloat16)
        return 0

    lax.fori_loop(0, all_blocks, fill, 0)
    parity = take_lanes(high_cos, jnp.full((chans, LANES), all_blocks, jnp.int32))
    table_ref[:, half:half + LANES] = jnp.where(lane_ids == 0, parity, low_sin).astype(jnp.bfloat16)

    paired = half == group and tiles == 2 and half % (4 * LANES) == 0
    if paired:
        even_cos = low_cos * low_cos - low_sin * low_sin
        even_sin = 2.0 * low_sin * low_cos
        for block in range(all_blocks // 2):
            spread = jnp.full((chans, LANES), 2 * block, jnp.int32)
            block_cos = take_lanes(high_cos, spread)
            block_sin = take_lanes(high_sin, spread)
            at = block * LANES
            cos = even_cos * block_cos - even_sin * block_sin
            sin = even_sin * block_cos + even_cos * block_sin
            if block == 0:
                sin = jnp.where(lane_ids == 0, parity, sin)
            even_ref[:, at:at + LANES] = cos.astype(jnp.bfloat16)
            even_ref[:, half // 2 + at:half // 2 + at + LANES] = sin.astype(jnp.bfloat16)
        near = lax.broadcasted_iota(jnp.int32, (own, own), 0)
        far = lax.broadcasted_iota(jnp.int32, (own, own), 1)

        def source(spot):
            return jnp.where(spot < tile, 2 * spot + 1, 2 * (spot - tile))

        split_ref[...] = (near == source(far)).astype(jnp.float32).astype(jnp.bfloat16)
        merge_ref[...] = (far == source(near)).astype(jnp.float32).astype(jnp.bfloat16)

    lane = lax.broadcasted_iota(jnp.int32, (8, LANES), 1)
    is_real = (lane // (rows // 2)) % 2 == 0
    dm = jnp.broadcast_to(dm_ref[...], (8, dm_ref.shape[1]))
    dm = jnp.concatenate([dm] * (LANES // dm_ref.shape[1]), 1)
    dm = take_lanes(dm, (lane // rows) * (rows // 2) + lane % (rows // 2))

    def first_of(step):
        return pl.multiple_of(step * tile, tile)

    def multiply(step, g, prod_ref):
        at = pl.ds(first_of(step), tile)
        both = jnp.concatenate([spec_ref[0, :, at], spec_ref[1, :, at]], 1)
        for part in (0, 1):
            columns = pl.ds(pl.multiple_of(part * half + g * group, group), group)
            prod_ref[:, part * group:(part + 1) * group] = lax.dot_general(
                both, table_ref[:, columns], (((0,), (0,)), ((), ())),
                preferred_element_type=jnp.float32,
            )

    def turns_of(step, r):
        bin_ids = step * tile + r * 8 + lax.broadcasted_iota(jnp.int32, (8, LANES), 0)
        return (bin_ids * dm) & (samples - 1)

    def pick(turns, half, group, g, r, prod_ref, acc):
        folded = jnp.where(turns > half, 2 * half - turns, turns)
        index = folded & (half - 1)
        spot = index & (LANES - 1)
        which = index // LANES - g * (group // LANES)
        acc = list(acc)
        for b in range(group // LANES):
            hit = which == b
            for i, (part, table) in enumerate(((0, 0), (1, 1), (1, 0), (0, 1))):
                top = part * tile + r * 8
                left = table * group + b * LANES
                piece = take_lanes(prod_ref[top:top + 8, left:left + LANES], spot)
                acc[i] = piece if acc[i] is None else jnp.where(hit, piece, acc[i])
        return acc

    def finish(turns, half, acc):
        sign = jnp.where(turns > half, -1.0, jnp.where(turns == 0, 0.0, 1.0))
        a, b, a2, b2 = acc
        real = jnp.where(turns == half, b2, a + sign * b)
        imag = jnp.where(turns == half, b, a2 - sign * b2)
        return jnp.where(is_real, real, imag)

    def split_multiply(block, even, prod_ref):
        at = pl.ds(pl.multiple_of(block * own, LANES), own)
        chosen = split_ref[:, even * tile:(even + 1) * tile]
        both = jnp.concatenate(
            [
                jnp.dot(spec_ref[part, :, at], chosen, preferred_element_type=jnp.float32)
                for part in (0, 1)
            ],
            1,
        ).astype(jnp.bfloat16)
        size = 2 * half // (1 + even)
        prod_ref[:, :size] = lax.dot_general(
            both, (even_ref if even else table_ref)[...], (((0,), (0,)), ((), ())),
            preferred_element_type=jnp.float32,
        )

    def split_gather(block, even, prod_ref):
        pieces = []
        for r in range(tile // 8):
            spots = r * 8 + lax.broadcasted_iota(jnp.int32, (8, LANES), 0)
            bin_ids = block * own + 2 * spots + (1 - even)
            turns = ((bin_ids * dm) & (samples - 1)) >> even
            size = half >> even
            acc = pick(turns, size, size, 0, r, prod_ref, [None] * 4)
            pieces.append(finish(turns, size, acc))
        return pieces

    def put(step, pieces):
        block = jnp.concatenate(pieces, 0).T
        at = pl.ds(first_of(step), tile)
        send_ref[:, :, at] = block.reshape(groups, rows, tile).astype(send_ref.dtype)

    def block_at(p):
        return bin_at(p + 1)

    def compute(p):
        base = block_at(p) * tiles

        def one_tile(t, _):
            step = base + t

            def one_group(g, accs):
                multiply(step, g, prod_a)
                new = []
                for r in range(tile // 8):
                    new += pick(
                        turns_of(step, r), half, group, g, r, prod_a, accs[4 * r:4 * r + 4]
                    )
                return tuple(new)

            zero = jnp.zeros((8, LANES), jnp.float32)
            accs = lax.fori_loop(0, half // group, one_group, (zero,) * (4 * (tile // 8)))
            put(step, [
                finish(turns_of(step, r), half, accs[4 * r:4 * r + 4]) for r in range(tile // 8)
            ])
            return 0

        if paired:
            block = block_at(p)
            split_multiply(block, 1, prod_b)
            pieces = split_gather(block, 0, prod_a)
            split_multiply(block_at(jnp.minimum(p + 1, bin_size - 1)), 0, prod_a)
            pieces += split_gather(block, 1, prod_b)
            merged = lax.dot_general(
                jnp.concatenate(pieces, 0).astype(jnp.bfloat16), merge_ref[...],
                (((0,), (0,)), ((), ())), preferred_element_type=jnp.float32,
            )
            at = pl.ds(pl.multiple_of(block * own, LANES), own)
            send_ref[:, :, at] = merged.reshape(groups, rows, own).astype(send_ref.dtype)
        else:
            lax.fori_loop(0, tiles, one_tile, 0)

    def chan_copy(p, offset):
        at = pl.ds(pl.multiple_of(block_at(p) * own, LANES), own)
        return pltpu.make_async_remote_copy(
            src_ref=send_ref.at[chan_at(offset), :, at],
            dst_ref=chan_recv.at[chan_size - offset, :, at],
            send_sem=chan_sems.at[0, offset, p],
            recv_sem=chan_sems.at[1, chan_size - offset, p],
            device_id={"chan": chan_at(offset)},
            device_id_type=MESH,
        )

    def bin_copy(block, piece):
        to = block + (0, 1, -1)[piece]
        begin, size, land = ((0, own, EDGE), (own - EDGE, EDGE, 0), (0, EDGE, EDGE + own))[piece]
        offset = lax.rem(to - my_bin + bin_size, bin_size)
        slot = lax.rem(bin_size - offset, bin_size)
        return pltpu.make_async_remote_copy(
            src_ref=sum_ref.at[:, pl.ds(pl.multiple_of(EDGE + block * own + begin, LANES), size)],
            dst_ref=bin_recv.at[slot, :, land:land + size],
            send_sem=bin_sems.at[0, piece, offset],
            recv_sem=bin_sems.at[1, piece, slot],
            device_id={"bin": to},
            device_id_type=MESH,
        )

    def each_piece(block, act):
        for piece in range(3):
            to = block + (0, 1, -1)[piece]

            @pl.when((to >= 0) & (to < bin_size) & (to != my_bin))
            def _():
                act(bin_copy(block, piece))

    def forward(p):
        block = block_at(p)
        at = pl.multiple_of(block * own, LANES)
        for offset in range(1, chan_size):
            chan_copy(p, chan_size - offset).wait_recv()
        total = send_ref[my_chan, :, pl.ds(at, own)].astype(jnp.float32)
        for offset in range(1, chan_size):
            total += chan_recv[offset, :, pl.ds(at, own)].astype(jnp.float32)
        sum_ref[:, pl.ds(pl.multiple_of(EDGE + at, LANES), own)] = total.astype(sum_ref.dtype)
        each_piece(block, lambda copy: copy.start())

    edge = jnp.zeros((rows, EDGE), sum_ref.dtype)
    sum_ref[:, :EDGE] = edge
    sum_ref[:, EDGE + bins:] = edge

    @pl.when(my_bin == 0)
    def _():
        for slot in range(1, bin_size):
            bin_recv[slot, :, :EDGE] = edge

    @pl.when(my_bin == bin_size - 1)
    def _():
        for slot in range(1, bin_size):
            bin_recv[slot, :, EDGE + own:] = edge

    if paired:
        split_multiply(block_at(0), 0, prod_a)
    pl.semaphore_wait(barrier, chan_size + bin_size - 2)

    def one_block(p, _):
        compute(p)
        for offset in range(1, chan_size):
            chan_copy(p, offset).start()

        @pl.when(p > 0)
        def _():
            forward(p - 1)

        return 0

    lax.fori_loop(0, bin_size, one_block, 0)
    forward(bin_size - 1)

    total = sum_ref[:, pl.ds(pl.multiple_of(my_bin * own, LANES), width)].astype(jnp.float32)
    for slot in range(1, bin_size):
        for piece in range(3):
            begin, size = ((EDGE, own), (0, EDGE), (EDGE + own, EDGE))[piece]
            sender = lax.rem(my_bin + slot, bin_size)
            comes = (True, my_bin > 0, my_bin < bin_size - 1)[piece]

            @pl.when(comes)
            def _():
                pltpu.make_async_remote_copy(
                    src_ref=sum_ref.at[:, begin:begin + size],
                    dst_ref=bin_recv.at[slot, :, begin:begin + size],
                    send_sem=bin_sems.at[0, piece, slot],
                    recv_sem=bin_sems.at[1, piece, slot],
                    device_id={"bin": sender},
                    device_id_type=MESH,
                ).wait_recv()

        total += bin_recv[slot].astype(jnp.float32)
    out_ref[...] = (total * scale).astype(jnp.bfloat16).astype(jnp.float32)

    def drain(p, _):
        for offset in range(1, chan_size):
            chan_copy(p, offset).wait_send()
        each_piece(block_at(p), lambda copy: copy.wait_send())
        return 0

    lax.fori_loop(0, bin_size, drain, 0)


def gather_lanes(x, index):
    return lax.gather(
        x, index[:, :, None],
        dimension_numbers=lax.GatherDimensionNumbers(
            offset_dims=(), collapsed_slice_dims=(1,), start_index_map=(1,),
            operand_batching_dims=(0,), start_indices_batching_dims=(0,),
        ),
        slice_sizes=(1, 1), mode="promise_in_bounds",
    )


def build_taps(bank_ref, ids_ref, taps_ref):
    bank_size, taps = bank_ref.shape[1:]
    templates = ids_ref.shape[1]
    rows = lax.broadcasted_iota(jnp.int32, (bank_size, templates), 0)
    one_hot = (ids_ref[...] == rows).astype(jnp.bfloat16)
    back = (LANES - 1 - lax.broadcasted_iota(jnp.int32, (16, LANES), 1)).astype(jnp.int16)
    back = jnp.concatenate([back] * (templates // 16), 0)
    for part in (0, 1):
        chosen = lax.dot_general(
            one_hot, bank_ref[part], (((0,), (0,)), ((), ())), preferred_element_type=jnp.float32
        ).astype(jnp.bfloat16)
        for u in range(taps // LANES):
            at = u * LANES
            turned = gather_lanes(chosen[:, at:at + LANES], back)
            taps_ref[part * templates:(part + 1) * templates, at:at + LANES] = turned
            taps_ref[
                (1 - part) * templates:(2 - part) * templates, taps + at:taps + at + LANES
            ] = turned if part == 0 else -turned


def paired_kernel(
    samples, scale, spec_hbm, delay_hbm, dm_hbm, bank_hbm, ids_hbm, out_ref, taps_ref, spec_ref,
    delay_ref, dm_ref, bank_ref, ids_ref, send_ref,
    sum_ref, chan_recv, bin_recv, low_ref, table_ref, split_ref, odd_ref, even_ref,
    load_sems, chan_sems, bin_sems,
):
    bin_size = lax.axis_size("bin")
    chan_size = lax.axis_size("chan")
    my_bin = lax.axis_index("bin")
    my_chan = lax.axis_index("chan")
    chans = spec_ref.shape[1]
    bins = spec_ref.shape[2]
    half = samples // 2
    quarter = half // 2
    groups, _, rows, _ = send_ref.shape
    width = out_ref.shape[1]
    tile = LANES
    own = bins // bin_size
    cut = own // tile
    spans = width // tile
    count = quarter // LANES
    pack = 16

    pairs = chan_size // 2
    partners = list(range(2, chan_size)) + [1]

    def chan_at(offset):
        return (my_chan // 2 + offset // 2) % pairs * 2 + (my_chan + offset) % 2

    def mirror(offset):
        return (pairs - offset // 2) % pairs * 2 + offset % 2

    def bin_at(offset):
        return lax.rem(my_bin + offset, bin_size)

    def block_at(p):
        return bin_at(p + 1)

    def spec_copy(p):
        at = pl.ds(pl.multiple_of(block_at(p) * own, LANES), own)
        return pltpu.make_async_copy(
            spec_hbm.at[:, :, at], spec_ref.at[:, :, at], load_sems.at[2 + p]
        )

    rank = my_chan * bin_size + my_bin
    mine = pl.ds(pl.multiple_of(rank * chans, LANES), chans)
    delay_copy = pltpu.make_async_copy(delay_hbm.at[:, mine], delay_ref, load_sems.at[0])
    dm_copy = pltpu.make_async_copy(dm_hbm, dm_ref, load_sems.at[1])
    delay_copy.start()
    dm_copy.start()
    for p in range(bin_size):
        spec_copy(p).start()
    bank_copy = pltpu.make_async_copy(bank_hbm, bank_ref, load_sems.at[2 + bin_size])
    ids_copy = pltpu.make_async_copy(ids_hbm, ids_ref, load_sems.at[3 + bin_size])
    bank_copy.start()
    ids_copy.start()

    barrier = pltpu.get_barrier_semaphore()

    def greet_chan(offset, _):
        pl.semaphore_signal(
            barrier, inc=1, device_id={"chan": chan_at(offset)}, device_id_type=MESH
        )
        return 0

    def greet_bin(offset, _):
        pl.semaphore_signal(barrier, inc=1, device_id={"bin": bin_at(offset)}, device_id_type=MESH)
        return 0

    for offset in range(1, bin_size):
        greet_bin(offset, 0)
    for offset in partners:
        greet_chan(offset, 0)

    near = lax.broadcasted_iota(jnp.int32, (own, own), 0)
    far = lax.broadcasted_iota(jnp.int32, (own, own), 1)
    source = jnp.where(near < tile, 2 * near + 1, 2 * (near - tile))
    split_ref[...] = (far == source).astype(jnp.float32).astype(jnp.bfloat16)

    edge = jnp.zeros((rows, tile), sum_ref.dtype)
    sum_ref[0] = edge
    sum_ref[sum_ref.shape[0] - 1] = edge

    @pl.when(my_bin == 0)
    def _():
        for slot in range(1, bin_size):
            bin_recv[slot, 0] = edge

    @pl.when(my_bin == bin_size - 1)
    def _():
        for slot in range(1, bin_size):
            bin_recv[slot, spans - 1] = edge

    delay_copy.wait()
    delay = delay_ref[...]

    def rotations(factor):
        return cos_sin((factor * delay) & (samples - 1), samples)

    row = lax.broadcasted_iota(jnp.int32, (8, chans), 0)
    fine_cos, fine_sin = rotations(2 * row)
    mid_cos, mid_sin = rotations(2 * 8 * lax.broadcasted_iota(jnp.int32, (LANES // 8, chans), 0))
    high_cos, high_sin = rotations(jnp.where(row == 0, 1, 2 * LANES * row))
    one_cos, one_sin = high_cos[:1], high_sin[:1]
    for a in range(LANES // 8):
        at = slice(8 * a, 8 * a + 8)
        cos = fine_cos * mid_cos[a:a + 1] - fine_sin * mid_sin[a:a + 1]
        sin = fine_sin * mid_cos[a:a + 1] + fine_cos * mid_sin[a:a + 1]
        low_ref[0, at] = cos
        low_ref[1, at] = sin
        low_ref[2, at] = cos * one_cos - sin * one_sin
        low_ref[3, at] = sin * one_cos + cos * one_sin

    def fill(i, _):
        at = pl.ds(pl.multiple_of(i * pack, pack), pack)
        for odd in (0, 1):
            low_cos = low_ref[2 * odd, at]
            low_sin = low_ref[2 * odd + 1, at]
            for k in range(count):
                if k == 0:
                    cos, sin = low_cos, low_sin
                else:
                    block_cos, block_sin = high_cos[k:k + 1], high_sin[k:k + 1]
                    cos = low_cos * block_cos - low_sin * block_sin
                    sin = low_sin * block_cos + low_cos * block_sin
                for part, value in ((0, cos), (1, sin)):
                    first = ((2 * odd + part) * count + k) * LANES
                    to = pl.ds(pl.multiple_of(first + i * pack, pack), pack)
                    table_ref[to] = value.astype(jnp.bfloat16)
        return 0

    lax.fori_loop(0, LANES // pack, fill, 0)
    parity = (1 - 2 * (delay & 1)).astype(jnp.float32)
    top = lax.broadcasted_iota(jnp.int32, (pack, chans), 0) == 0
    table_ref[quarter:quarter + pack] = jnp.where(top, parity, low_ref[1, :pack]).astype(
        jnp.bfloat16
    )

    dm_copy.wait()
    lane = lax.broadcasted_iota(jnp.int32, (8, LANES), 1)
    dm = jnp.broadcast_to(dm_ref[...], (8, dm_ref.shape[1]))
    dm = jnp.concatenate([dm] * (LANES // dm_ref.shape[1]), 1)
    dm = take_lanes(dm, (lane // rows) * (rows // 2) + lane % (rows // 2))
    dm = jnp.concatenate([dm] * (pack // 8), 0)
    lane = lax.broadcasted_iota(jnp.int32, (pack, LANES), 1)
    real = 1 - (lane // (rows // 2)) % 2
    is_real = real.astype(jnp.int16) == 1
    flip = (2 * real - 1).astype(jnp.float32)

    def turned(block):
        at = pl.ds(pl.multiple_of(block * own, LANES), own)
        sides = [
            lax.dot_general(
                split_ref[...], spec_ref[part, :, at], (((1,), (1,)), ((), ())),
                preferred_element_type=jnp.float32,
            ).astype(jnp.bfloat16)
            for part in (0, 1)
        ]
        return [
            jnp.concatenate([side[n * tile:(n + 1) * tile] for side in sides], 0) for n in (0, 1)
        ]

    def multiply(left, prod_ref):
        size = prod_ref.shape[1]
        prod_ref[...] = lax.dot_general(
            left, table_ref[:size], (((1,), (1,)), ((), ())), preferred_element_type=jnp.float32
        ).astype(jnp.bfloat16)

    spots = lax.broadcasted_iota(jnp.int32, (pack, LANES), 0)
    steps = [[(spots * factor + shift) * dm for factor, shift in ((2, 1), (1, 0))],
             [factor * pack * dm for factor in (2, 1)]]
    flip = flip.astype(jnp.bfloat16)
    zero = jnp.zeros((pack, LANES), jnp.bfloat16)

    def collect(block, even, prod_ref):
        size = half >> even
        start = steps[0][even] + (block * (own >> even)) * dm
        places = list(range(count))
        if not even:
            places += list(range(2 * count, 3 * count))
        pieces = []
        for r in range(tile // pack):
            turns = (start + r * steps[1][even]) & (2 * size - 1)
            index = jnp.minimum(turns, 2 * size - turns) & (size - 1)
            if even:
                which = index >> 7
            else:
                which = (index >> 8) + (index & 1) * (2 * count)
                index = index >> 1
            spot = (index & (LANES - 1)).astype(jnp.int16)
            which = which.astype(jnp.int16)
            turns = turns.astype(jnp.int16)
            acc = [None] * 4
            for b in places:
                hit = which == b
                for i, (part, table) in enumerate(((0, 0), (1, 1), (1, 0), (0, 1))):
                    top = part * tile + r * pack
                    left = (b + table * count) * LANES
                    piece = gather_lanes(prod_ref[top:top + pack, left:left + LANES], spot)
                    acc[i] = piece if acc[i] is None else jnp.where(hit, piece, acc[i])
            a, b, a2, b2 = acc
            sign = jnp.where(turns > size, -flip, flip)
            side = jnp.where(turns == 0, zero, jnp.where(is_real, b, b2) * sign)
            sums = jnp.where(is_real, a, a2) + side
            pieces.append(jnp.where(turns == size, jnp.where(is_real, b2, b), sums))
        return pieces

    def compute(p):
        block = block_at(p)
        odd, even = turned(block)
        multiply(odd, odd_ref)
        multiply(even, even_ref)
        near = collect(block, 0, odd_ref)
        far = collect(block, 1, even_ref)
        part = len(near) // 2
        for t in (0, 1):
            picked = near[t * part:(t + 1) * part] + far[t * part:(t + 1) * part]
            send_ref[:, block * cut + t] = jnp.concatenate(picked, 0).T.reshape(groups, rows, tile)

    def chan_copy(p, offset):
        at = pl.ds(block_at(p) * cut, cut)
        return pltpu.make_async_remote_copy(
            src_ref=send_ref.at[chan_at(offset), at],
            dst_ref=chan_recv.at[mirror(offset), at],
            send_sem=chan_sems.at[0, offset, p],
            recv_sem=chan_sems.at[1, mirror(offset), p],
            device_id={"chan": chan_at(offset)},
            device_id_type=MESH,
        )

    def bin_copy(block, piece):
        to = block + (0, 1, -1)[piece]
        begin, size, land = ((0, cut, 1), (cut - 1, 1, 0), (0, 1, spans - 1))[piece]
        offset = lax.rem(to - my_bin + bin_size, bin_size)
        slot = lax.rem(bin_size - offset, bin_size)
        return pltpu.make_async_remote_copy(
            src_ref=sum_ref.at[pl.ds(1 + block * cut + begin, size)],
            dst_ref=bin_recv.at[slot, land:land + size],
            send_sem=bin_sems.at[0, piece, offset],
            recv_sem=bin_sems.at[1, piece, slot],
            device_id={"bin": to},
            device_id_type=MESH,
        )

    def each_piece(block, act):
        for piece in range(3):
            to = block + (0, 1, -1)[piece]

            @pl.when((to >= 0) & (to < bin_size) & (to != my_bin))
            def _():
                act(bin_copy(block, piece))

    def forward(p):
        block = block_at(p)
        at = pl.ds(block * cut, cut)
        for offset in range(1, chan_size):
            chan_copy(p, mirror(offset)).wait_recv()
        total = send_ref[my_chan, at].astype(jnp.float32)
        for offset in range(1, chan_size):
            total += chan_recv[offset, at].astype(jnp.float32)
        sum_ref[pl.ds(1 + block * cut, cut)] = total.astype(sum_ref.dtype)
        each_piece(block, lambda copy: copy.start())

    def one_block(p, _):
        spec_copy(p).wait()
        compute(p)

        @pl.when(p == 0)
        def _():
            pl.semaphore_wait(barrier, chan_size + bin_size - 2)

        for offset in partners:
            chan_copy(p, offset).start()
        return 0

    lax.fori_loop(0, bin_size, one_block, 0)
    bank_copy.wait()
    ids_copy.wait()
    build_taps(bank_ref, ids_ref, taps_ref)
    for p in range(bin_size):
        forward(p)

    total = sum_ref[pl.ds(my_bin * cut, spans)].astype(jnp.float32)
    for slot in range(1, bin_size):
        for piece in range(3):
            begin, size = ((1, cut), (0, 1), (spans - 1, 1))[piece]
            sender = lax.rem(my_bin + slot, bin_size)
            comes = (True, my_bin > 0, my_bin < bin_size - 1)[piece]

            @pl.when(comes)
            def _():
                pltpu.make_async_remote_copy(
                    src_ref=sum_ref.at[begin:begin + size],
                    dst_ref=bin_recv.at[slot, begin:begin + size],
                    send_sem=bin_sems.at[0, piece, slot],
                    recv_sem=bin_sems.at[1, piece, slot],
                    device_id={"bin": sender},
                    device_id_type=MESH,
                ).wait_recv()

        total += bin_recv[slot].astype(jnp.float32)
    signal = (total * scale).astype(jnp.bfloat16).astype(jnp.float32)
    lane = lax.broadcasted_iota(jnp.int32, (rows, tile), 1)
    back = (lane >> 1) + (tile // 2) * (1 - (lane & 1))
    for t in range(spans):
        out_ref[:, t * tile:(t + 1) * tile] = take_lanes(signal[t], back)

    def drain(p, _):
        for offset in range(1, chan_size):
            chan_copy(p, offset).wait_send()
        each_piece(block_at(p), lambda copy: copy.wait_send())
        return 0

    lax.fori_loop(0, bin_size, drain, 0)


def correlate_kernel(trials, signal_ref, taps_ref, out_hbm, power_ref, sems):
    _, templates, bins = power_ref.shape
    taps = taps_ref.shape[1] // 2
    group = math.gcd(trials, 2)

    pack = 16
    length = bins + taps

    def out_copy(g):
        at = pl.ds(g * group, group)
        return pltpu.make_async_copy(power_ref.at[at], out_hbm.at[at], sems.at[g])

    def one_group(g, _):
        for t in range(group):
            trial = g * group + t
            hankel = []
            for part in (0, 1):
                line = signal_ref[pl.ds(part * trials + trial, 1), :]
                line = jnp.broadcast_to(line, (pack, length)).astype(jnp.bfloat16)
                rows = [
                    pltpu.roll(line, length + pack * a - (LANES - 1), 1, stride=1, stride_axis=0)
                    for a in range(LANES // pack)
                ]
                hankel.append(jnp.concatenate(rows, 0))
            wide = jnp.concatenate(
                [
                    hankel[part][:, u * LANES:u * LANES + bins]
                    for part in (0, 1)
                    for u in range(taps // LANES)
                ],
                0,
            )
            response = jnp.dot(taps_ref[...], wide, preferred_element_type=jnp.float32)
            real = response[:templates]
            imag = response[templates:]
            power_ref[trial] = (real * real + imag * imag).astype(power_ref.dtype)
        out_copy(g).start()
        return 0

    for g in range(trials // group):
        one_group(g, 0)
    for g in range(trials // group):
        out_copy(g).wait()


def local(spectra, dm_trials, chan_delay, template_bank, template_ids):
    chans, bins = spectra.shape[1:]
    samples = 2 * bins
    bin_size = lax.axis_size("bin")
    chan_size = lax.axis_size("chan")
    trials = dm_trials.shape[0] // chan_size
    templates = template_ids.shape[0]
    taps = template_bank.shape[2]
    own = bins // bin_size
    width = own + 2 * EDGE
    scale = 1.0 / math.sqrt(chan_delay.shape[0])
    if chans % LANES:
        rank = lax.axis_index("chan") * bin_size + lax.axis_index("bin")
        chan_delay = lax.dynamic_slice_in_dim(chan_delay, rank * chans, chans)
    vmem = pl.BlockSpec(memory_space=pltpu.VMEM)
    products = pltpu.VMEM((2 * LANES, 2 * min(bins, 1024)), jnp.float32)

    paired = (
        bins <= 1024 and bins % (4 * LANES) == 0 and own == 2 * LANES and chans % LANES == 0
        and trials * 2 * chan_size == LANES and chan_size % 2 == 0
    )
    if paired:
        hbm = pl.BlockSpec(memory_space=pltpu.HBM)
        signal, chosen = pl.pallas_call(
            functools.partial(paired_kernel, samples, scale),
            out_shape=[
                jax.ShapeDtypeStruct((2 * trials, width), jnp.float32),
                jax.ShapeDtypeStruct((2 * templates, 2 * taps), jnp.bfloat16),
            ],
            in_specs=[hbm] * 5,
            out_specs=[vmem] * 2,
            scratch_shapes=[
                pltpu.VMEM((2, chans, bins), jnp.bfloat16),
                pltpu.VMEM((1, chans), jnp.int32),
                pltpu.VMEM((1, dm_trials.shape[0]), jnp.int32),
                pltpu.VMEM(template_bank.shape, jnp.bfloat16),
                pltpu.VMEM((1, templates), jnp.int32),
                pltpu.VMEM((chan_size, bins // LANES, 2 * trials, LANES), jnp.bfloat16),
                pltpu.VMEM((bins // LANES + 2, 2 * trials, LANES), jnp.bfloat16),
                pltpu.VMEM((chan_size, bins // LANES, 2 * trials, LANES), jnp.bfloat16),
                pltpu.VMEM((bin_size, width // LANES, 2 * trials, LANES), jnp.bfloat16),
                pltpu.VMEM((4, LANES, chans), jnp.float32),
                pltpu.VMEM((2 * bins, chans), jnp.bfloat16),
                pltpu.VMEM((own, own), jnp.bfloat16),
                pltpu.VMEM((2 * LANES, 2 * bins), jnp.bfloat16),
                pltpu.VMEM((2 * LANES, bins), jnp.bfloat16),
                pltpu.SemaphoreType.DMA((4 + bin_size,)),
                pltpu.SemaphoreType.DMA((2, chan_size, bin_size)),
                pltpu.SemaphoreType.DMA((2, 3, bin_size)),
            ],
            compiler_params=pltpu.CompilerParams(
                collective_id=0, has_side_effects=True, vmem_limit_bytes=24 * 2 ** 20
            ),
            name="dedisperse",
        )(*[
            pltpu.with_memory_space_constraint(x, pltpu.HBM)
            for x in (
                spectra, chan_delay[None, :], dm_trials[None, :], template_bank,
                template_ids[None, :],
            )
        ])
    else:
        signal = pl.pallas_call(
            functools.partial(dedisperse_kernel, samples, scale),
            out_shape=jax.ShapeDtypeStruct((2 * trials, width), jnp.float32),
            in_specs=[vmem] * 3,
            out_specs=vmem,
            scratch_shapes=[
                pltpu.VMEM((chan_size, 2 * trials, bins), jnp.bfloat16),
                pltpu.VMEM((2 * trials, bins + 2 * EDGE), jnp.bfloat16),
                pltpu.VMEM((chan_size, 2 * trials, bins), jnp.bfloat16),
                pltpu.VMEM((bin_size, 2 * trials, width), jnp.bfloat16),
                pltpu.VMEM((chans, 2 * bins), jnp.bfloat16),
                pltpu.VMEM((chans, bins), jnp.bfloat16),
                pltpu.VMEM((own, own), jnp.bfloat16),
                pltpu.VMEM((own, own), jnp.bfloat16),
                products,
                products,
                pltpu.SemaphoreType.DMA((2, chan_size, bin_size)),
                pltpu.SemaphoreType.DMA((2, 3, bin_size)),
            ],
            compiler_params=pltpu.CompilerParams(collective_id=0, has_side_effects=True),
            name="dedisperse",
        )(spectra, chan_delay[None, :], dm_trials[None, :])

        chosen = pl.pallas_call(
            build_taps,
            out_shape=jax.ShapeDtypeStruct((2 * templates, 2 * taps), jnp.bfloat16),
            in_specs=[vmem] * 2,
            out_specs=vmem,
            name="taps",
        )(template_bank, template_ids[None, :])

    return pl.pallas_call(
        functools.partial(correlate_kernel, trials),
        out_shape=jax.ShapeDtypeStruct((trials, templates, own), jnp.bfloat16),
        in_specs=[vmem] * 2,
        out_specs=pl.BlockSpec(memory_space=pltpu.HBM),
        scratch_shapes=[
            pltpu.VMEM((trials, templates, own), jnp.bfloat16),
            pltpu.SemaphoreType.DMA((trials,)),
        ],
        compiler_params=pltpu.CompilerParams(vmem_limit_bytes=16 * 2 ** 20),
        name="templates",
    )(signal, chosen)


def solution(mesh):
    in_specs = (P(None, ("beam", "chan", "bin"), None), P(), P(), P(), P())
    out_specs = P(("beam", "chan"), None, "bin")
    return jax.shard_map(local, mesh=mesh, in_specs=in_specs, out_specs=out_specs, check_vma=False)
```

```python
import functools
import math

import jax
import jax.numpy as jnp
from jax import lax
from jax.experimental import pallas as pl
from jax.experimental.pallas import tpu as pltpu
from jax.sharding import PartitionSpec as P

EDGE = 128
LANES = 128
MESH = pl.DeviceIdType.MESH


def cos_sin(turns, samples):
    eighth = samples // 8
    quadrant = lax.shift_right_logical(turns + eighth, eighth.bit_length())
    rest = turns - quadrant * (2 * eighth)
    x = rest.astype(jnp.float32) * (2.0 * math.pi / samples)
    y = x * x
    c = 1.0 + y * (-0.5 + y * (1.0 / 24 + y * (-1.0 / 720 + y * (1.0 / 40320))))
    s = x * (1.0 + y * (-1.0 / 6 + y * (1.0 / 120 + y * (-1.0 / 5040 + y * (1.0 / 362880)))))
    swap = (quadrant & 1) == 1
    cos = jnp.where(swap, s, c)
    sin = jnp.where(swap, c, s)
    cos = jnp.where(((quadrant + 1) & 2) == 2, -cos, cos)
    sin = jnp.where((quadrant & 2) == 2, -sin, sin)
    return cos, sin


def take_lanes(x, index):
    return jnp.take_along_axis(x, index, axis=1, mode="promise_in_bounds")


def dedisperse_kernel(
    samples, scale, spec_ref, delay_ref, dm_ref, out_ref, send_ref, sum_ref, chan_recv, bin_recv,
    table_ref, even_ref, split_ref, merge_ref, prod_a, prod_b, chan_sems, bin_sems,
):
    bin_size = lax.axis_size("bin")
    chan_size = lax.axis_size("chan")
    my_bin = lax.axis_index("bin")
    my_chan = lax.axis_index("chan")
    chans = spec_ref.shape[1]
    bins = spec_ref.shape[2]
    half = samples // 2
    group = prod_a.shape[1] // 2
    blocks = group // LANES
    all_blocks = half // LANES
    groups, rows = send_ref.shape[:2]
    width = out_ref.shape[1]
    tile = LANES
    own = bins // bin_size
    tiles = own // tile
    padded = max(chans, LANES)

    def chan_at(offset):
        return lax.rem(my_chan + offset, chan_size)

    def bin_at(offset):
        return lax.rem(my_bin + offset, bin_size)

    barrier = pltpu.get_barrier_semaphore()

    def greet_chan(offset, _):
        pl.semaphore_signal(
            barrier, inc=1, device_id={"chan": chan_at(offset)}, device_id_type=MESH
        )
        return 0

    def greet_bin(offset, _):
        pl.semaphore_signal(barrier, inc=1, device_id={"bin": bin_at(offset)}, device_id_type=MESH)
        return 0

    lax.fori_loop(1, chan_size, greet_chan, 0)
    lax.fori_loop(1, bin_size, greet_bin, 0)

    if delay_ref.shape[1] == chans:
        delay = delay_ref[...]
    else:
        rank = lax.axis_index("chan") * bin_size + lax.axis_index("bin")
        delay = delay_ref[:, pl.ds(pl.multiple_of(rank * chans, LANES), chans)]
    if chans < padded:
        delay = jnp.concatenate([delay, jnp.zeros((1, padded - chans), jnp.int32)], 1)

    def rotations(count, stride):
        turns = lax.broadcasted_iota(jnp.int32, (count, padded), 0) * stride * delay
        return cos_sin(turns & (samples - 1), samples)

    fine_cos, fine_sin = rotations(8, 1)
    mid_cos, mid_sin = rotations(LANES // 8, 8)
    low_cos = jnp.concatenate(
        [fine_cos * mid_cos[a:a + 1] - fine_sin * mid_sin[a:a + 1] for a in range(LANES // 8)], 0
    ).T[:chans]
    low_sin = jnp.concatenate(
        [fine_sin * mid_cos[a:a + 1] + fine_cos * mid_sin[a:a + 1] for a in range(LANES // 8)], 0
    ).T[:chans]
    coarse_cos, coarse_sin = rotations(all_blocks + 8, LANES)
    fill_rows = jnp.zeros((LANES - all_blocks - 8, padded), jnp.float32)
    high_cos = jnp.concatenate([coarse_cos, fill_rows], 0).T[:chans]
    high_sin = jnp.concatenate([coarse_sin, fill_rows], 0).T[:chans]
    lane_ids = lax.broadcasted_iota(jnp.int32, (chans, LANES), 1)

    def fill(block, _):
        spread = jnp.full((chans, LANES), block, jnp.int32)
        block_cos = take_lanes(high_cos, spread)
        block_sin = take_lanes(high_sin, spread)
        at = pl.multiple_of(block * LANES, LANES)
        cos = low_cos * block_cos - low_sin * block_sin
        sin = low_sin * block_cos + low_cos * block_sin
        table_ref[:, pl.ds(at, LANES)] = cos.astype(jnp.bfloat16)
        table_ref[:, pl.ds(half + at, LANES)] = sin.astype(jnp.bfloat16)
        return 0

    lax.fori_loop(0, all_blocks, fill, 0)
    parity = take_lanes(high_cos, jnp.full((chans, LANES), all_blocks, jnp.int32))
    table_ref[:, half:half + LANES] = jnp.where(lane_ids == 0, parity, low_sin).astype(jnp.bfloat16)

    paired = half == group and tiles == 2 and half % (4 * LANES) == 0
    if paired:
        even_cos = low_cos * low_cos - low_sin * low_sin
        even_sin = 2.0 * low_sin * low_cos
        for block in range(all_blocks // 2):
            spread = jnp.full((chans, LANES), 2 * block, jnp.int32)
            block_cos = take_lanes(high_cos, spread)
            block_sin = take_lanes(high_sin, spread)
            at = block * LANES
            cos = even_cos * block_cos - even_sin * block_sin
            sin = even_sin * block_cos + even_cos * block_sin
            if block == 0:
                sin = jnp.where(lane_ids == 0, parity, sin)
            even_ref[:, at:at + LANES] = cos.astype(jnp.bfloat16)
            even_ref[:, half // 2 + at:half // 2 + at + LANES] = sin.astype(jnp.bfloat16)
        near = lax.broadcasted_iota(jnp.int32, (own, own), 0)
        far = lax.broadcasted_iota(jnp.int32, (own, own), 1)

        def source(spot):
            return jnp.where(spot < tile, 2 * spot + 1, 2 * (spot - tile))

        split_ref[...] = (near == source(far)).astype(jnp.float32).astype(jnp.bfloat16)
        merge_ref[...] = (far == source(near)).astype(jnp.float32).astype(jnp.bfloat16)

    lane = lax.broadcasted_iota(jnp.int32, (8, LANES), 1)
    is_real = (lane // (rows // 2)) % 2 == 0
    dm = jnp.broadcast_to(dm_ref[...], (8, dm_ref.shape[1]))
    dm = jnp.concatenate([dm] * (LANES // dm_ref.shape[1]), 1)
    dm = take_lanes(dm, (lane // rows) * (rows // 2) + lane % (rows // 2))

    def first_of(step):
        return pl.multiple_of(step * tile, tile)

    def multiply(step, g, prod_ref):
        at = pl.ds(first_of(step), tile)
        both = jnp.concatenate([spec_ref[0, :, at], spec_ref[1, :, at]], 1)
        for part in (0, 1):
            columns = pl.ds(pl.multiple_of(part * half + g * group, group), group)
            prod_ref[:, part * group:(part + 1) * group] = lax.dot_general(
                both, table_ref[:, columns], (((0,), (0,)), ((), ())),
                preferred_element_type=jnp.float32,
            )

    def turns_of(step, r):
        bin_ids = step * tile + r * 8 + lax.broadcasted_iota(jnp.int32, (8, LANES), 0)
        return (bin_ids * dm) & (samples - 1)

    def pick(turns, half, group, g, r, prod_ref, acc):
        folded = jnp.where(turns > half, 2 * half - turns, turns)
        index = folded & (half - 1)
        spot = index & (LANES - 1)
        which = index // LANES - g * (group // LANES)
        acc = list(acc)
        for b in range(group // LANES):
            hit = which == b
            for i, (part, table) in enumerate(((0, 0), (1, 1), (1, 0), (0, 1))):
                top = part * tile + r * 8
                left = table * group + b * LANES
                piece = take_lanes(prod_ref[top:top + 8, left:left + LANES], spot)
                acc[i] = piece if acc[i] is None else jnp.where(hit, piece, acc[i])
        return acc

    def finish(turns, half, acc):
        sign = jnp.where(turns > half, -1.0, jnp.where(turns == 0, 0.0, 1.0))
        a, b, a2, b2 = acc
        real = jnp.where(turns == half, b2, a + sign * b)
        imag = jnp.where(turns == half, b, a2 - sign * b2)
        return jnp.where(is_real, real, imag)

    def split_multiply(block, even, prod_ref):
        at = pl.ds(pl.multiple_of(block * own, LANES), own)
        chosen = split_ref[:, even * tile:(even + 1) * tile]
        both = jnp.concatenate(
            [
                jnp.dot(spec_ref[part, :, at], chosen, preferred_element_type=jnp.float32)
                for part in (0, 1)
            ],
            1,
        ).astype(jnp.bfloat16)
        size = 2 * half // (1 + even)
        prod_ref[:, :size] = lax.dot_general(
            both, (even_ref if even else table_ref)[...], (((0,), (0,)), ((), ())),
            preferred_element_type=jnp.float32,
        )

    def split_gather(block, even, prod_ref):
        pieces = []
        for r in range(tile // 8):
            spots = r * 8 + lax.broadcasted_iota(jnp.int32, (8, LANES), 0)
            bin_ids = block * own + 2 * spots + (1 - even)
            turns = ((bin_ids * dm) & (samples - 1)) >> even
            size = half >> even
            acc = pick(turns, size, size, 0, r, prod_ref, [None] * 4)
            pieces.append(finish(turns, size, acc))
        return pieces

    def put(step, pieces):
        block = jnp.concatenate(pieces, 0).T
        at = pl.ds(first_of(step), tile)
        send_ref[:, :, at] = block.reshape(groups, rows, tile).astype(send_ref.dtype)

    def block_at(p):
        return bin_at(p + 1)

    def compute(p):
        base = block_at(p) * tiles

        def one_tile(t, _):
            step = base + t

            def one_group(g, accs):
                multiply(step, g, prod_a)
                new = []
                for r in range(tile // 8):
                    new += pick(
                        turns_of(step, r), half, group, g, r, prod_a, accs[4 * r:4 * r + 4]
                    )
                return tuple(new)

            zero = jnp.zeros((8, LANES), jnp.float32)
            accs = lax.fori_loop(0, half // group, one_group, (zero,) * (4 * (tile // 8)))
            put(step, [
                finish(turns_of(step, r), half, accs[4 * r:4 * r + 4]) for r in range(tile // 8)
            ])
            return 0

        if paired:
            block = block_at(p)
            split_multiply(block, 1, prod_b)
            pieces = split_gather(block, 0, prod_a)
            split_multiply(block_at(jnp.minimum(p + 1, bin_size - 1)), 0, prod_a)
            pieces += split_gather(block, 1, prod_b)
            merged = lax.dot_general(
                jnp.concatenate(pieces, 0).astype(jnp.bfloat16), merge_ref[...],
                (((0,), (0,)), ((), ())), preferred_element_type=jnp.float32,
            )
            at = pl.ds(pl.multiple_of(block * own, LANES), own)
            send_ref[:, :, at] = merged.reshape(groups, rows, own).astype(send_ref.dtype)
        else:
            lax.fori_loop(0, tiles, one_tile, 0)

    def chan_copy(p, offset):
        at = pl.ds(pl.multiple_of(block_at(p) * own, LANES), own)
        return pltpu.make_async_remote_copy(
            src_ref=send_ref.at[chan_at(offset), :, at],
            dst_ref=chan_recv.at[chan_size - offset, :, at],
            send_sem=chan_sems.at[0, offset, p],
            recv_sem=chan_sems.at[1, chan_size - offset, p],
            device_id={"chan": chan_at(offset)},
            device_id_type=MESH,
        )

    def bin_copy(block, piece):
        to = block + (0, 1, -1)[piece]
        begin, size, land = ((0, own, EDGE), (own - EDGE, EDGE, 0), (0, EDGE, EDGE + own))[piece]
        offset = lax.rem(to - my_bin + bin_size, bin_size)
        slot = lax.rem(bin_size - offset, bin_size)
        return pltpu.make_async_remote_copy(
            src_ref=sum_ref.at[:, pl.ds(pl.multiple_of(EDGE + block * own + begin, LANES), size)],
            dst_ref=bin_recv.at[slot, :, land:land + size],
            send_sem=bin_sems.at[0, piece, offset],
            recv_sem=bin_sems.at[1, piece, slot],
            device_id={"bin": to},
            device_id_type=MESH,
        )

    def each_piece(block, act):
        for piece in range(3):
            to = block + (0, 1, -1)[piece]

            @pl.when((to >= 0) & (to < bin_size) & (to != my_bin))
            def _():
                act(bin_copy(block, piece))

    def forward(p):
        block = block_at(p)
        at = pl.multiple_of(block * own, LANES)
        for offset in range(1, chan_size):
            chan_copy(p, chan_size - offset).wait_recv()
        total = send_ref[my_chan, :, pl.ds(at, own)].astype(jnp.float32)
        for offset in range(1, chan_size):
            total += chan_recv[offset, :, pl.ds(at, own)].astype(jnp.float32)
        sum_ref[:, pl.ds(pl.multiple_of(EDGE + at, LANES), own)] = total.astype(sum_ref.dtype)
        each_piece(block, lambda copy: copy.start())

    edge = jnp.zeros((rows, EDGE), sum_ref.dtype)
    sum_ref[:, :EDGE] = edge
    sum_ref[:, EDGE + bins:] = edge

    @pl.when(my_bin == 0)
    def _():
        for slot in range(1, bin_size):
            bin_recv[slot, :, :EDGE] = edge

    @pl.when(my_bin == bin_size - 1)
    def _():
        for slot in range(1, bin_size):
            bin_recv[slot, :, EDGE + own:] = edge

    if paired:
        split_multiply(block_at(0), 0, prod_a)
    pl.semaphore_wait(barrier, chan_size + bin_size - 2)

    def one_block(p, _):
        compute(p)
        for offset in range(1, chan_size):
            chan_copy(p, offset).start()

        @pl.when(p > 0)
        def _():
            forward(p - 1)

        return 0

    lax.fori_loop(0, bin_size, one_block, 0)
    forward(bin_size - 1)

    total = sum_ref[:, pl.ds(pl.multiple_of(my_bin * own, LANES), width)].astype(jnp.float32)
    for slot in range(1, bin_size):
        for piece in range(3):
            begin, size = ((EDGE, own), (0, EDGE), (EDGE + own, EDGE))[piece]
            sender = lax.rem(my_bin + slot, bin_size)
            comes = (True, my_bin > 0, my_bin < bin_size - 1)[piece]

            @pl.when(comes)
            def _():
                pltpu.make_async_remote_copy(
                    src_ref=sum_ref.at[:, begin:begin + size],
                    dst_ref=bin_recv.at[slot, :, begin:begin + size],
                    send_sem=bin_sems.at[0, piece, slot],
                    recv_sem=bin_sems.at[1, piece, slot],
                    device_id={"bin": sender},
                    device_id_type=MESH,
                ).wait_recv()

        total += bin_recv[slot].astype(jnp.float32)
    out_ref[...] = (total * scale).astype(jnp.bfloat16).astype(jnp.float32)

    def drain(p, _):
        for offset in range(1, chan_size):
            chan_copy(p, offset).wait_send()
        each_piece(block_at(p), lambda copy: copy.wait_send())
        return 0

    lax.fori_loop(0, bin_size, drain, 0)


def gather_lanes(x, index):
    return lax.gather(
        x, index[:, :, None],
        dimension_numbers=lax.GatherDimensionNumbers(
            offset_dims=(), collapsed_slice_dims=(1,), start_index_map=(1,),
            operand_batching_dims=(0,), start_indices_batching_dims=(0,),
        ),
        slice_sizes=(1, 1), mode="promise_in_bounds",
    )


def build_taps(bank_ref, ids_ref, taps_ref):
    bank_size, taps = bank_ref.shape[1:]
    templates = ids_ref.shape[1]
    rows = lax.broadcasted_iota(jnp.int32, (bank_size, templates), 0)
    one_hot = (ids_ref[...] == rows).astype(jnp.bfloat16)
    back = (LANES - 1 - lax.broadcasted_iota(jnp.int32, (16, LANES), 1)).astype(jnp.int16)
    back = jnp.concatenate([back] * (templates // 16), 0)
    for part in (0, 1):
        chosen = lax.dot_general(
            one_hot, bank_ref[part], (((0,), (0,)), ((), ())), preferred_element_type=jnp.float32
        ).astype(jnp.bfloat16)
        for u in range(taps // LANES):
            at = u * LANES
            turned = gather_lanes(chosen[:, at:at + LANES], back)
            taps_ref[part * templates:(part + 1) * templates, at:at + LANES] = turned
            taps_ref[
                (1 - part) * templates:(2 - part) * templates, taps + at:taps + at + LANES
            ] = turned if part == 0 else -turned


def paired_kernel(
    samples, scale, spec_hbm, delay_hbm, dm_hbm, bank_hbm, ids_hbm, out_ref, taps_ref, spec_ref,
    delay_ref, dm_ref, bank_ref, ids_ref, send_ref,
    sum_ref, chan_recv, bin_recv, low_ref, table_ref, split_ref, odd_ref, even_ref,
    load_sems, chan_sems, bin_sems,
):
    bin_size = lax.axis_size("bin")
    chan_size = lax.axis_size("chan")
    my_bin = lax.axis_index("bin")
    my_chan = lax.axis_index("chan")
    chans = spec_ref.shape[1]
    bins = spec_ref.shape[2]
    half = samples // 2
    quarter = half // 2
    groups, _, rows, _ = send_ref.shape
    width = out_ref.shape[1]
    tile = LANES
    own = bins // bin_size
    cut = own // tile
    spans = width // tile
    count = quarter // LANES
    pack = 16

    pairs = chan_size // 2
    partners = list(range(2, chan_size)) + [1]

    def chan_at(offset):
        return (my_chan // 2 + offset // 2) % pairs * 2 + (my_chan + offset) % 2

    def mirror(offset):
        return (pairs - offset // 2) % pairs * 2 + offset % 2

    def bin_at(offset):
        return lax.rem(my_bin + offset, bin_size)

    def block_at(p):
        return bin_at(p + 1)

    def spec_copy(p):
        at = pl.ds(pl.multiple_of(block_at(p) * own, LANES), own)
        return pltpu.make_async_copy(
            spec_hbm.at[:, :, at], spec_ref.at[:, :, at], load_sems.at[2 + p]
        )

    rank = my_chan * bin_size + my_bin
    mine = pl.ds(pl.multiple_of(rank * chans, LANES), chans)
    delay_copy = pltpu.make_async_copy(delay_hbm.at[:, mine], delay_ref, load_sems.at[0])
    dm_copy = pltpu.make_async_copy(dm_hbm, dm_ref, load_sems.at[1])
    delay_copy.start()
    dm_copy.start()

    barrier = pltpu.get_barrier_semaphore()

    def greet_chan(offset, _):
        pl.semaphore_signal(
            barrier, inc=1, device_id={"chan": chan_at(offset)}, device_id_type=MESH
        )
        return 0

    def greet_bin(offset, _):
        pl.semaphore_signal(barrier, inc=1, device_id={"bin": bin_at(offset)}, device_id_type=MESH)
        return 0

    for offset in range(1, bin_size):
        greet_bin(offset, 0)
    for offset in partners:
        greet_chan(offset, 0)
    for p in range(bin_size):
        spec_copy(p).start()
    bank_copy = pltpu.make_async_copy(bank_hbm, bank_ref, load_sems.at[2 + bin_size])
    ids_copy = pltpu.make_async_copy(ids_hbm, ids_ref, load_sems.at[3 + bin_size])
    bank_copy.start()
    ids_copy.start()

    near = lax.broadcasted_iota(jnp.int32, (own, own), 0)
    far = lax.broadcasted_iota(jnp.int32, (own, own), 1)
    source = jnp.where(near < tile, 2 * near + 1, 2 * (near - tile))
    split_ref[...] = (far == source).astype(jnp.float32).astype(jnp.bfloat16)

    edge = jnp.zeros((rows, tile), sum_ref.dtype)
    sum_ref[0] = edge
    sum_ref[sum_ref.shape[0] - 1] = edge

    @pl.when(my_bin == 0)
    def _():
        for slot in range(1, bin_size):
            bin_recv[slot, 0] = edge

    @pl.when(my_bin == bin_size - 1)
    def _():
        for slot in range(1, bin_size):
            bin_recv[slot, spans - 1] = edge

    delay_copy.wait()
    delay = delay_ref[...]

    def rotations(factor):
        return cos_sin((factor * delay) & (samples - 1), samples)

    row = lax.broadcasted_iota(jnp.int32, (8, chans), 0)
    fine_cos, fine_sin = rotations(2 * row)
    mid_cos, mid_sin = rotations(2 * 8 * lax.broadcasted_iota(jnp.int32, (LANES // 8, chans), 0))
    high_cos, high_sin = rotations(jnp.where(row == 0, 1, 2 * LANES * row))
    one_cos, one_sin = high_cos[:1], high_sin[:1]
    for a in range(LANES // 8):
        at = slice(8 * a, 8 * a + 8)
        cos = fine_cos * mid_cos[a:a + 1] - fine_sin * mid_sin[a:a + 1]
        sin = fine_sin * mid_cos[a:a + 1] + fine_cos * mid_sin[a:a + 1]
        low_ref[0, at] = cos
        low_ref[1, at] = sin
        low_ref[2, at] = cos * one_cos - sin * one_sin
        low_ref[3, at] = sin * one_cos + cos * one_sin

    def fill(i, _):
        at = pl.ds(pl.multiple_of(i * pack, pack), pack)
        for odd in (0, 1):
            low_cos = low_ref[2 * odd, at]
            low_sin = low_ref[2 * odd + 1, at]
            for k in range(count):
                if k == 0:
                    cos, sin = low_cos, low_sin
                else:
                    block_cos, block_sin = high_cos[k:k + 1], high_sin[k:k + 1]
                    cos = low_cos * block_cos - low_sin * block_sin
                    sin = low_sin * block_cos + low_cos * block_sin
                for part, value in ((0, cos), (1, sin)):
                    first = ((2 * odd + part) * count + k) * LANES
                    to = pl.ds(pl.multiple_of(first + i * pack, pack), pack)
                    table_ref[to] = value.astype(jnp.bfloat16)
        return 0

    lax.fori_loop(0, LANES // pack, fill, 0)
    parity = (1 - 2 * (delay & 1)).astype(jnp.float32)
    top = lax.broadcasted_iota(jnp.int32, (pack, chans), 0) == 0
    table_ref[quarter:quarter + pack] = jnp.where(top, parity, low_ref[1, :pack]).astype(
        jnp.bfloat16
    )

    dm_copy.wait()
    lane = lax.broadcasted_iota(jnp.int32, (8, LANES), 1)
    dm = jnp.broadcast_to(dm_ref[...], (8, dm_ref.shape[1]))
    dm = jnp.concatenate([dm] * (LANES // dm_ref.shape[1]), 1)
    dm = take_lanes(dm, (lane // rows) * (rows // 2) + lane % (rows // 2))
    dm = jnp.concatenate([dm] * (pack // 8), 0)
    lane = lax.broadcasted_iota(jnp.int32, (pack, LANES), 1)
    real = 1 - (lane // (rows // 2)) % 2
    is_real = real.astype(jnp.int16) == 1
    flip = (2 * real - 1).astype(jnp.float32)

    def turned(block):
        at = pl.ds(pl.multiple_of(block * own, LANES), own)
        sides = [
            lax.dot_general(
                split_ref[...], spec_ref[part, :, at], (((1,), (1,)), ((), ())),
                preferred_element_type=jnp.float32,
            ).astype(jnp.bfloat16)
            for part in (0, 1)
        ]
        return [
            jnp.concatenate([side[n * tile:(n + 1) * tile] for side in sides], 0) for n in (0, 1)
        ]

    def multiply(left, prod_ref):
        size = prod_ref.shape[1]
        prod_ref[...] = lax.dot_general(
            left, table_ref[:size], (((1,), (1,)), ((), ())), preferred_element_type=jnp.float32
        ).astype(jnp.bfloat16)

    spots = lax.broadcasted_iota(jnp.int32, (pack, LANES), 0)
    steps = [[(spots * factor + shift) * dm for factor, shift in ((2, 1), (1, 0))],
             [factor * pack * dm for factor in (2, 1)]]
    flip = flip.astype(jnp.bfloat16)
    zero = jnp.zeros((pack, LANES), jnp.bfloat16)

    def collect(block, even, prod_ref):
        size = half >> even
        start = steps[0][even] + (block * (own >> even)) * dm
        places = list(range(count))
        if not even:
            places += list(range(2 * count, 3 * count))
        pieces = []
        for r in range(tile // pack):
            turns = (start + r * steps[1][even]) & (2 * size - 1)
            index = jnp.minimum(turns, 2 * size - turns) & (size - 1)
            if even:
                which = index >> 7
            else:
                which = (index >> 8) + (index & 1) * (2 * count)
                index = index >> 1
            spot = (index & (LANES - 1)).astype(jnp.int16)
            which = which.astype(jnp.int16)
            turns = turns.astype(jnp.int16)
            acc = [None] * 4
            for b in places:
                hit = which == b
                for i, (part, table) in enumerate(((0, 0), (1, 1), (1, 0), (0, 1))):
                    top = part * tile + r * pack
                    left = (b + table * count) * LANES
                    piece = gather_lanes(prod_ref[top:top + pack, left:left + LANES], spot)
                    acc[i] = piece if acc[i] is None else jnp.where(hit, piece, acc[i])
            a, b, a2, b2 = acc
            sign = jnp.where(turns > size, -flip, flip)
            side = jnp.where(turns == 0, zero, jnp.where(is_real, b, b2) * sign)
            sums = jnp.where(is_real, a, a2) + side
            pieces.append(jnp.where(turns == size, jnp.where(is_real, b2, b), sums))
        return pieces

    def compute(p):
        block = block_at(p)
        odd, even = turned(block)
        multiply(odd, odd_ref)
        multiply(even, even_ref)
        near = collect(block, 0, odd_ref)
        far = collect(block, 1, even_ref)
        part = len(near) // 2
        for t in (0, 1):
            picked = near[t * part:(t + 1) * part] + far[t * part:(t + 1) * part]
            send_ref[:, block * cut + t] = jnp.concatenate(picked, 0).T.reshape(groups, rows, tile)

    def chan_copy(p, offset):
        at = pl.ds(block_at(p) * cut, cut)
        return pltpu.make_async_remote_copy(
            src_ref=send_ref.at[chan_at(offset), at],
            dst_ref=chan_recv.at[mirror(offset), at],
            send_sem=chan_sems.at[0, offset, p],
            recv_sem=chan_sems.at[1, mirror(offset), p],
            device_id={"chan": chan_at(offset)},
            device_id_type=MESH,
        )

    def bin_copy(block, piece):
        to = block + (0, 1, -1)[piece]
        begin, size, land = ((0, cut, 1), (cut - 1, 1, 0), (0, 1, spans - 1))[piece]
        offset = lax.rem(to - my_bin + bin_size, bin_size)
        slot = lax.rem(bin_size - offset, bin_size)
        return pltpu.make_async_remote_copy(
            src_ref=sum_ref.at[pl.ds(1 + block * cut + begin, size)],
            dst_ref=bin_recv.at[slot, land:land + size],
            send_sem=bin_sems.at[0, piece, offset],
            recv_sem=bin_sems.at[1, piece, slot],
            device_id={"bin": to},
            device_id_type=MESH,
        )

    def each_piece(block, act):
        for piece in range(3):
            to = block + (0, 1, -1)[piece]

            @pl.when((to >= 0) & (to < bin_size) & (to != my_bin))
            def _():
                act(bin_copy(block, piece))

    def forward(p):
        block = block_at(p)
        at = pl.ds(block * cut, cut)
        for offset in range(1, chan_size):
            chan_copy(p, mirror(offset)).wait_recv()
        total = send_ref[my_chan, at].astype(jnp.float32)
        for offset in range(1, chan_size):
            total += chan_recv[offset, at].astype(jnp.float32)
        sum_ref[pl.ds(1 + block * cut, cut)] = total.astype(sum_ref.dtype)
        each_piece(block, lambda copy: copy.start())

    def one_block(p, _):
        spec_copy(p).wait()
        compute(p)

        @pl.when(p == 0)
        def _():
            pl.semaphore_wait(barrier, chan_size + bin_size - 2)

        for offset in partners:
            chan_copy(p, offset).start()
        return 0

    lax.fori_loop(0, bin_size, one_block, 0)
    for p in range(bin_size - 1):
        forward(p)
    bank_copy.wait()
    ids_copy.wait()
    build_taps(bank_ref, ids_ref, taps_ref)
    forward(bin_size - 1)

    def drain(p, _):
        for offset in range(1, chan_size):
            chan_copy(p, offset).wait_send()

        @pl.when(p + 1 < bin_size)
        def _():
            each_piece(block_at(p), lambda copy: copy.wait_send())

        return 0

    lax.fori_loop(0, bin_size, drain, 0)

    total = sum_ref[pl.ds(my_bin * cut, spans)].astype(jnp.float32)
    for slot in range(1, bin_size):
        for piece in range(3):
            begin, size = ((1, cut), (0, 1), (spans - 1, 1))[piece]
            sender = lax.rem(my_bin + slot, bin_size)
            comes = (True, my_bin > 0, my_bin < bin_size - 1)[piece]

            @pl.when(comes)
            def _():
                pltpu.make_async_remote_copy(
                    src_ref=sum_ref.at[begin:begin + size],
                    dst_ref=bin_recv.at[slot, begin:begin + size],
                    send_sem=bin_sems.at[0, piece, slot],
                    recv_sem=bin_sems.at[1, piece, slot],
                    device_id={"bin": sender},
                    device_id_type=MESH,
                ).wait_recv()

        total += bin_recv[slot].astype(jnp.float32)
    signal = (total * scale).astype(jnp.bfloat16).astype(jnp.float32)
    lane = lax.broadcasted_iota(jnp.int32, (rows, tile), 1)
    back = (lane >> 1) + (tile // 2) * (1 - (lane & 1))
    for t in range(spans):
        out_ref[:, t * tile:(t + 1) * tile] = take_lanes(signal[t], back)

    each_piece(block_at(bin_size - 1), lambda copy: copy.wait_send())


def correlate_kernel(trials, signal_ref, taps_ref, out_hbm, power_ref, sems):
    _, templates, bins = power_ref.shape
    taps = taps_ref.shape[1] // 2
    group = math.gcd(trials, 2)

    pack = 16
    length = bins + taps

    def out_copy(g):
        at = pl.ds(g * group, group)
        return pltpu.make_async_copy(power_ref.at[at], out_hbm.at[at], sems.at[g])

    def one_group(g, _):
        for t in range(group):
            trial = g * group + t
            hankel = []
            for part in (0, 1):
                line = signal_ref[pl.ds(part * trials + trial, 1), :]
                line = jnp.broadcast_to(line, (pack, length)).astype(jnp.bfloat16)
                rows = [
                    pltpu.roll(line, length + pack * a - (LANES - 1), 1, stride=1, stride_axis=0)
                    for a in range(LANES // pack)
                ]
                hankel.append(jnp.concatenate(rows, 0))
            wide = jnp.concatenate(
                [
                    hankel[part][:, u * LANES:u * LANES + bins]
                    for part in (0, 1)
                    for u in range(taps // LANES)
                ],
                0,
            )
            response = jnp.dot(taps_ref[...], wide, preferred_element_type=jnp.float32)
            real = response[:templates]
            imag = response[templates:]
            power_ref[trial] = (real * real + imag * imag).astype(power_ref.dtype)
        out_copy(g).start()
        return 0

    for g in range(trials // group):
        one_group(g, 0)
    for g in range(trials // group):
        out_copy(g).wait()


def local(spectra, dm_trials, chan_delay, template_bank, template_ids):
    chans, bins = spectra.shape[1:]
    samples = 2 * bins
    bin_size = lax.axis_size("bin")
    chan_size = lax.axis_size("chan")
    trials = dm_trials.shape[0] // chan_size
    templates = template_ids.shape[0]
    taps = template_bank.shape[2]
    own = bins // bin_size
    width = own + 2 * EDGE
    scale = 1.0 / math.sqrt(chan_delay.shape[0])
    if chans % LANES:
        rank = lax.axis_index("chan") * bin_size + lax.axis_index("bin")
        chan_delay = lax.dynamic_slice_in_dim(chan_delay, rank * chans, chans)
    vmem = pl.BlockSpec(memory_space=pltpu.VMEM)
    products = pltpu.VMEM((2 * LANES, 2 * min(bins, 1024)), jnp.float32)

    paired = (
        bins <= 1024 and bins % (4 * LANES) == 0 and own == 2 * LANES and chans % LANES == 0
        and trials * 2 * chan_size == LANES and chan_size % 2 == 0
    )
    if paired:
        hbm = pl.BlockSpec(memory_space=pltpu.HBM)
        signal, chosen = pl.pallas_call(
            functools.partial(paired_kernel, samples, scale),
            out_shape=[
                jax.ShapeDtypeStruct((2 * trials, width), jnp.float32),
                jax.ShapeDtypeStruct((2 * templates, 2 * taps), jnp.bfloat16),
            ],
            in_specs=[hbm] * 5,
            out_specs=[vmem] * 2,
            scratch_shapes=[
                pltpu.VMEM((2, chans, bins), jnp.bfloat16),
                pltpu.VMEM((1, chans), jnp.int32),
                pltpu.VMEM((1, dm_trials.shape[0]), jnp.int32),
                pltpu.VMEM(template_bank.shape, jnp.bfloat16),
                pltpu.VMEM((1, templates), jnp.int32),
                pltpu.VMEM((chan_size, bins // LANES, 2 * trials, LANES), jnp.bfloat16),
                pltpu.VMEM((bins // LANES + 2, 2 * trials, LANES), jnp.bfloat16),
                pltpu.VMEM((chan_size, bins // LANES, 2 * trials, LANES), jnp.bfloat16),
                pltpu.VMEM((bin_size, width // LANES, 2 * trials, LANES), jnp.bfloat16),
                pltpu.VMEM((4, LANES, chans), jnp.float32),
                pltpu.VMEM((2 * bins, chans), jnp.bfloat16),
                pltpu.VMEM((own, own), jnp.bfloat16),
                pltpu.VMEM((2 * LANES, 2 * bins), jnp.bfloat16),
                pltpu.VMEM((2 * LANES, bins), jnp.bfloat16),
                pltpu.SemaphoreType.DMA((4 + bin_size,)),
                pltpu.SemaphoreType.DMA((2, chan_size, bin_size)),
                pltpu.SemaphoreType.DMA((2, 3, bin_size)),
            ],
            compiler_params=pltpu.CompilerParams(
                collective_id=0, has_side_effects=True, vmem_limit_bytes=24 * 2 ** 20
            ),
            name="dedisperse",
        )(*[
            pltpu.with_memory_space_constraint(x, pltpu.HBM)
            for x in (
                spectra, chan_delay[None, :], dm_trials[None, :], template_bank,
                template_ids[None, :],
            )
        ])
    else:
        signal = pl.pallas_call(
            functools.partial(dedisperse_kernel, samples, scale),
            out_shape=jax.ShapeDtypeStruct((2 * trials, width), jnp.float32),
            in_specs=[vmem] * 3,
            out_specs=vmem,
            scratch_shapes=[
                pltpu.VMEM((chan_size, 2 * trials, bins), jnp.bfloat16),
                pltpu.VMEM((2 * trials, bins + 2 * EDGE), jnp.bfloat16),
                pltpu.VMEM((chan_size, 2 * trials, bins), jnp.bfloat16),
                pltpu.VMEM((bin_size, 2 * trials, width), jnp.bfloat16),
                pltpu.VMEM((chans, 2 * bins), jnp.bfloat16),
                pltpu.VMEM((chans, bins), jnp.bfloat16),
                pltpu.VMEM((own, own), jnp.bfloat16),
                pltpu.VMEM((own, own), jnp.bfloat16),
                products,
                products,
                pltpu.SemaphoreType.DMA((2, chan_size, bin_size)),
                pltpu.SemaphoreType.DMA((2, 3, bin_size)),
            ],
            compiler_params=pltpu.CompilerParams(collective_id=0, has_side_effects=True),
            name="dedisperse",
        )(spectra, chan_delay[None, :], dm_trials[None, :])

        chosen = pl.pallas_call(
            build_taps,
            out_shape=jax.ShapeDtypeStruct((2 * templates, 2 * taps), jnp.bfloat16),
            in_specs=[vmem] * 2,
            out_specs=vmem,
            name="taps",
        )(template_bank, template_ids[None, :])

    return pl.pallas_call(
        functools.partial(correlate_kernel, trials),
        out_shape=jax.ShapeDtypeStruct((trials, templates, own), jnp.bfloat16),
        in_specs=[vmem] * 2,
        out_specs=pl.BlockSpec(memory_space=pltpu.HBM),
        scratch_shapes=[
            pltpu.VMEM((trials, templates, own), jnp.bfloat16),
            pltpu.SemaphoreType.DMA((trials,)),
        ],
        compiler_params=pltpu.CompilerParams(vmem_limit_bytes=16 * 2 ** 20),
        name="templates",
    )(signal, chosen)


def solution(mesh):
    in_specs = (P(None, ("beam", "chan", "bin"), None), P(), P(), P(), P())
    out_specs = P(("beam", "chan"), None, "bin")
    return jax.shard_map(local, mesh=mesh, in_specs=in_specs, out_specs=out_specs, check_vma=False)
```

```python
import functools
import math

import jax
import jax.numpy as jnp
from jax import lax
from jax.experimental import pallas as pl
from jax.experimental.pallas import tpu as pltpu
from jax.sharding import PartitionSpec as P

EDGE = 128
LANES = 128
MESH = pl.DeviceIdType.MESH


def cos_sin(turns, samples):
    eighth = samples // 8
    quadrant = lax.shift_right_logical(turns + eighth, eighth.bit_length())
    rest = turns - quadrant * (2 * eighth)
    x = rest.astype(jnp.float32) * (2.0 * math.pi / samples)
    y = x * x
    c = 1.0 + y * (-0.5 + y * (1.0 / 24 + y * (-1.0 / 720 + y * (1.0 / 40320))))
    s = x * (1.0 + y * (-1.0 / 6 + y * (1.0 / 120 + y * (-1.0 / 5040 + y * (1.0 / 362880)))))
    swap = (quadrant & 1) == 1
    cos = jnp.where(swap, s, c)
    sin = jnp.where(swap, c, s)
    cos = jnp.where(((quadrant + 1) & 2) == 2, -cos, cos)
    sin = jnp.where((quadrant & 2) == 2, -sin, sin)
    return cos, sin


def take_lanes(x, index):
    return jnp.take_along_axis(x, index, axis=1, mode="promise_in_bounds")


def dedisperse_kernel(
    samples, scale, spec_ref, delay_ref, dm_ref, out_ref, send_ref, sum_ref, chan_recv, bin_recv,
    table_ref, even_ref, split_ref, merge_ref, prod_a, prod_b, chan_sems, bin_sems,
):
    bin_size = lax.axis_size("bin")
    chan_size = lax.axis_size("chan")
    my_bin = lax.axis_index("bin")
    my_chan = lax.axis_index("chan")
    chans = spec_ref.shape[1]
    bins = spec_ref.shape[2]
    half = samples // 2
    group = prod_a.shape[1] // 2
    blocks = group // LANES
    all_blocks = half // LANES
    groups, rows = send_ref.shape[:2]
    width = out_ref.shape[1]
    tile = LANES
    own = bins // bin_size
    tiles = own // tile
    padded = max(chans, LANES)

    def chan_at(offset):
        return lax.rem(my_chan + offset, chan_size)

    def bin_at(offset):
        return lax.rem(my_bin + offset, bin_size)

    barrier = pltpu.get_barrier_semaphore()

    def greet_chan(offset, _):
        pl.semaphore_signal(
            barrier, inc=1, device_id={"chan": chan_at(offset)}, device_id_type=MESH
        )
        return 0

    def greet_bin(offset, _):
        pl.semaphore_signal(barrier, inc=1, device_id={"bin": bin_at(offset)}, device_id_type=MESH)
        return 0

    lax.fori_loop(1, chan_size, greet_chan, 0)
    lax.fori_loop(1, bin_size, greet_bin, 0)

    if delay_ref.shape[1] == chans:
        delay = delay_ref[...]
    else:
        rank = lax.axis_index("chan") * bin_size + lax.axis_index("bin")
        delay = delay_ref[:, pl.ds(pl.multiple_of(rank * chans, LANES), chans)]
    if chans < padded:
        delay = jnp.concatenate([delay, jnp.zeros((1, padded - chans), jnp.int32)], 1)

    def rotations(count, stride):
        turns = lax.broadcasted_iota(jnp.int32, (count, padded), 0) * stride * delay
        return cos_sin(turns & (samples - 1), samples)

    fine_cos, fine_sin = rotations(8, 1)
    mid_cos, mid_sin = rotations(LANES // 8, 8)
    low_cos = jnp.concatenate(
        [fine_cos * mid_cos[a:a + 1] - fine_sin * mid_sin[a:a + 1] for a in range(LANES // 8)], 0
    ).T[:chans]
    low_sin = jnp.concatenate(
        [fine_sin * mid_cos[a:a + 1] + fine_cos * mid_sin[a:a + 1] for a in range(LANES // 8)], 0
    ).T[:chans]
    coarse_cos, coarse_sin = rotations(all_blocks + 8, LANES)
    fill_rows = jnp.zeros((LANES - all_blocks - 8, padded), jnp.float32)
    high_cos = jnp.concatenate([coarse_cos, fill_rows], 0).T[:chans]
    high_sin = jnp.concatenate([coarse_sin, fill_rows], 0).T[:chans]
    lane_ids = lax.broadcasted_iota(jnp.int32, (chans, LANES), 1)

    def fill(block, _):
        spread = jnp.full((chans, LANES), block, jnp.int32)
        block_cos = take_lanes(high_cos, spread)
        block_sin = take_lanes(high_sin, spread)
        at = pl.multiple_of(block * LANES, LANES)
        cos = low_cos * block_cos - low_sin * block_sin
        sin = low_sin * block_cos + low_cos * block_sin
        table_ref[:, pl.ds(at, LANES)] = cos.astype(jnp.bfloat16)
        table_ref[:, pl.ds(half + at, LANES)] = sin.astype(jnp.bfloat16)
        return 0

    lax.fori_loop(0, all_blocks, fill, 0)
    parity = take_lanes(high_cos, jnp.full((chans, LANES), all_blocks, jnp.int32))
    table_ref[:, half:half + LANES] = jnp.where(lane_ids == 0, parity, low_sin).astype(jnp.bfloat16)

    paired = half == group and tiles == 2 and half % (4 * LANES) == 0
    if paired:
        even_cos = low_cos * low_cos - low_sin * low_sin
        even_sin = 2.0 * low_sin * low_cos
        for block in range(all_blocks // 2):
            spread = jnp.full((chans, LANES), 2 * block, jnp.int32)
            block_cos = take_lanes(high_cos, spread)
            block_sin = take_lanes(high_sin, spread)
            at = block * LANES
            cos = even_cos * block_cos - even_sin * block_sin
            sin = even_sin * block_cos + even_cos * block_sin
            if block == 0:
                sin = jnp.where(lane_ids == 0, parity, sin)
            even_ref[:, at:at + LANES] = cos.astype(jnp.bfloat16)
            even_ref[:, half // 2 + at:half // 2 + at + LANES] = sin.astype(jnp.bfloat16)
        near = lax.broadcasted_iota(jnp.int32, (own, own), 0)
        far = lax.broadcasted_iota(jnp.int32, (own, own), 1)

        def source(spot):
            return jnp.where(spot < tile, 2 * spot + 1, 2 * (spot - tile))

        split_ref[...] = (near == source(far)).astype(jnp.float32).astype(jnp.bfloat16)
        merge_ref[...] = (far == source(near)).astype(jnp.float32).astype(jnp.bfloat16)

    lane = lax.broadcasted_iota(jnp.int32, (8, LANES), 1)
    is_real = (lane // (rows // 2)) % 2 == 0
    dm = jnp.broadcast_to(dm_ref[...], (8, dm_ref.shape[1]))
    dm = jnp.concatenate([dm] * (LANES // dm_ref.shape[1]), 1)
    dm = take_lanes(dm, (lane // rows) * (rows // 2) + lane % (rows // 2))

    def first_of(step):
        return pl.multiple_of(step * tile, tile)

    def multiply(step, g, prod_ref):
        at = pl.ds(first_of(step), tile)
        both = jnp.concatenate([spec_ref[0, :, at], spec_ref[1, :, at]], 1)
        for part in (0, 1):
            columns = pl.ds(pl.multiple_of(part * half + g * group, group), group)
            prod_ref[:, part * group:(part + 1) * group] = lax.dot_general(
                both, table_ref[:, columns], (((0,), (0,)), ((), ())),
                preferred_element_type=jnp.float32,
            )

    def turns_of(step, r):
        bin_ids = step * tile + r * 8 + lax.broadcasted_iota(jnp.int32, (8, LANES), 0)
        return (bin_ids * dm) & (samples - 1)

    def pick(turns, half, group, g, r, prod_ref, acc):
        folded = jnp.where(turns > half, 2 * half - turns, turns)
        index = folded & (half - 1)
        spot = index & (LANES - 1)
        which = index // LANES - g * (group // LANES)
        acc = list(acc)
        for b in range(group // LANES):
            hit = which == b
            for i, (part, table) in enumerate(((0, 0), (1, 1), (1, 0), (0, 1))):
                top = part * tile + r * 8
                left = table * group + b * LANES
                piece = take_lanes(prod_ref[top:top + 8, left:left + LANES], spot)
                acc[i] = piece if acc[i] is None else jnp.where(hit, piece, acc[i])
        return acc

    def finish(turns, half, acc):
        sign = jnp.where(turns > half, -1.0, jnp.where(turns == 0, 0.0, 1.0))
        a, b, a2, b2 = acc
        real = jnp.where(turns == half, b2, a + sign * b)
        imag = jnp.where(turns == half, b, a2 - sign * b2)
        return jnp.where(is_real, real, imag)

    def split_multiply(block, even, prod_ref):
        at = pl.ds(pl.multiple_of(block * own, LANES), own)
        chosen = split_ref[:, even * tile:(even + 1) * tile]
        both = jnp.concatenate(
            [
                jnp.dot(spec_ref[part, :, at], chosen, preferred_element_type=jnp.float32)
                for part in (0, 1)
            ],
            1,
        ).astype(jnp.bfloat16)
        size = 2 * half // (1 + even)
        prod_ref[:, :size] = lax.dot_general(
            both, (even_ref if even else table_ref)[...], (((0,), (0,)), ((), ())),
            preferred_element_type=jnp.float32,
        )

    def split_gather(block, even, prod_ref):
        pieces = []
        for r in range(tile // 8):
            spots = r * 8 + lax.broadcasted_iota(jnp.int32, (8, LANES), 0)
            bin_ids = block * own + 2 * spots + (1 - even)
            turns = ((bin_ids * dm) & (samples - 1)) >> even
            size = half >> even
            acc = pick(turns, size, size, 0, r, prod_ref, [None] * 4)
            pieces.append(finish(turns, size, acc))
        return pieces

    def put(step, pieces):
        block = jnp.concatenate(pieces, 0).T
        at = pl.ds(first_of(step), tile)
        send_ref[:, :, at] = block.reshape(groups, rows, tile).astype(send_ref.dtype)

    def block_at(p):
        return bin_at(p + 1)

    def compute(p):
        base = block_at(p) * tiles

        def one_tile(t, _):
            step = base + t

            def one_group(g, accs):
                multiply(step, g, prod_a)
                new = []
                for r in range(tile // 8):
                    new += pick(
                        turns_of(step, r), half, group, g, r, prod_a, accs[4 * r:4 * r + 4]
                    )
                return tuple(new)

            zero = jnp.zeros((8, LANES), jnp.float32)
            accs = lax.fori_loop(0, half // group, one_group, (zero,) * (4 * (tile // 8)))
            put(step, [
                finish(turns_of(step, r), half, accs[4 * r:4 * r + 4]) for r in range(tile // 8)
            ])
            return 0

        if paired:
            block = block_at(p)
            split_multiply(block, 1, prod_b)
            pieces = split_gather(block, 0, prod_a)
            split_multiply(block_at(jnp.minimum(p + 1, bin_size - 1)), 0, prod_a)
            pieces += split_gather(block, 1, prod_b)
            merged = lax.dot_general(
                jnp.concatenate(pieces, 0).astype(jnp.bfloat16), merge_ref[...],
                (((0,), (0,)), ((), ())), preferred_element_type=jnp.float32,
            )
            at = pl.ds(pl.multiple_of(block * own, LANES), own)
            send_ref[:, :, at] = merged.reshape(groups, rows, own).astype(send_ref.dtype)
        else:
            lax.fori_loop(0, tiles, one_tile, 0)

    def chan_copy(p, offset):
        at = pl.ds(pl.multiple_of(block_at(p) * own, LANES), own)
        return pltpu.make_async_remote_copy(
            src_ref=send_ref.at[chan_at(offset), :, at],
            dst_ref=chan_recv.at[chan_size - offset, :, at],
            send_sem=chan_sems.at[0, offset, p],
            recv_sem=chan_sems.at[1, chan_size - offset, p],
            device_id={"chan": chan_at(offset)},
            device_id_type=MESH,
        )

    def bin_copy(block, piece):
        to = block + (0, 1, -1)[piece]
        begin, size, land = ((0, own, EDGE), (own - EDGE, EDGE, 0), (0, EDGE, EDGE + own))[piece]
        offset = lax.rem(to - my_bin + bin_size, bin_size)
        slot = lax.rem(bin_size - offset, bin_size)
        return pltpu.make_async_remote_copy(
            src_ref=sum_ref.at[:, pl.ds(pl.multiple_of(EDGE + block * own + begin, LANES), size)],
            dst_ref=bin_recv.at[slot, :, land:land + size],
            send_sem=bin_sems.at[0, piece, offset],
            recv_sem=bin_sems.at[1, piece, slot],
            device_id={"bin": to},
            device_id_type=MESH,
        )

    def each_piece(block, act):
        for piece in range(3):
            to = block + (0, 1, -1)[piece]

            @pl.when((to >= 0) & (to < bin_size) & (to != my_bin))
            def _():
                act(bin_copy(block, piece))

    def forward(p):
        block = block_at(p)
        at = pl.multiple_of(block * own, LANES)
        for offset in range(1, chan_size):
            chan_copy(p, chan_size - offset).wait_recv()
        total = send_ref[my_chan, :, pl.ds(at, own)].astype(jnp.float32)
        for offset in range(1, chan_size):
            total += chan_recv[offset, :, pl.ds(at, own)].astype(jnp.float32)
        sum_ref[:, pl.ds(pl.multiple_of(EDGE + at, LANES), own)] = total.astype(sum_ref.dtype)
        each_piece(block, lambda copy: copy.start())

    edge = jnp.zeros((rows, EDGE), sum_ref.dtype)
    sum_ref[:, :EDGE] = edge
    sum_ref[:, EDGE + bins:] = edge

    @pl.when(my_bin == 0)
    def _():
        for slot in range(1, bin_size):
            bin_recv[slot, :, :EDGE] = edge

    @pl.when(my_bin == bin_size - 1)
    def _():
        for slot in range(1, bin_size):
            bin_recv[slot, :, EDGE + own:] = edge

    if paired:
        split_multiply(block_at(0), 0, prod_a)
    pl.semaphore_wait(barrier, chan_size + bin_size - 2)

    def one_block(p, _):
        compute(p)
        for offset in range(1, chan_size):
            chan_copy(p, offset).start()

        @pl.when(p > 0)
        def _():
            forward(p - 1)

        return 0

    lax.fori_loop(0, bin_size, one_block, 0)
    forward(bin_size - 1)

    total = sum_ref[:, pl.ds(pl.multiple_of(my_bin * own, LANES), width)].astype(jnp.float32)
    for slot in range(1, bin_size):
        for piece in range(3):
            begin, size = ((EDGE, own), (0, EDGE), (EDGE + own, EDGE))[piece]
            sender = lax.rem(my_bin + slot, bin_size)
            comes = (True, my_bin > 0, my_bin < bin_size - 1)[piece]

            @pl.when(comes)
            def _():
                pltpu.make_async_remote_copy(
                    src_ref=sum_ref.at[:, begin:begin + size],
                    dst_ref=bin_recv.at[slot, :, begin:begin + size],
                    send_sem=bin_sems.at[0, piece, slot],
                    recv_sem=bin_sems.at[1, piece, slot],
                    device_id={"bin": sender},
                    device_id_type=MESH,
                ).wait_recv()

        total += bin_recv[slot].astype(jnp.float32)
    out_ref[...] = (total * scale).astype(jnp.bfloat16).astype(jnp.float32)

    def drain(p, _):
        for offset in range(1, chan_size):
            chan_copy(p, offset).wait_send()
        each_piece(block_at(p), lambda copy: copy.wait_send())
        return 0

    lax.fori_loop(0, bin_size, drain, 0)


def gather_lanes(x, index):
    return lax.gather(
        x, index[:, :, None],
        dimension_numbers=lax.GatherDimensionNumbers(
            offset_dims=(), collapsed_slice_dims=(1,), start_index_map=(1,),
            operand_batching_dims=(0,), start_indices_batching_dims=(0,),
        ),
        slice_sizes=(1, 1), mode="promise_in_bounds",
    )


def build_taps(bank_ref, ids_ref, taps_ref):
    bank_size, taps = bank_ref.shape[1:]
    templates = ids_ref.shape[1]
    rows = lax.broadcasted_iota(jnp.int32, (bank_size, templates), 0)
    one_hot = (ids_ref[...] == rows).astype(jnp.bfloat16)
    back = (LANES - 1 - lax.broadcasted_iota(jnp.int32, (16, LANES), 1)).astype(jnp.int16)
    back = jnp.concatenate([back] * (templates // 16), 0)
    for part in (0, 1):
        chosen = lax.dot_general(
            one_hot, bank_ref[part], (((0,), (0,)), ((), ())), preferred_element_type=jnp.float32
        ).astype(jnp.bfloat16)
        for u in range(taps // LANES):
            at = u * LANES
            turned = gather_lanes(chosen[:, at:at + LANES], back)
            taps_ref[part * templates:(part + 1) * templates, at:at + LANES] = turned
            taps_ref[
                (1 - part) * templates:(2 - part) * templates, taps + at:taps + at + LANES
            ] = turned if part == 0 else -turned


def paired_kernel(
    samples, scale, spec_hbm, delay_hbm, dm_hbm, bank_hbm, ids_hbm, out_ref, taps_ref, spec_ref,
    delay_ref, dm_ref, bank_ref, ids_ref, send_ref,
    sum_ref, chan_recv, bin_recv, low_ref, table_ref, split_ref, odd_ref, even_ref,
    load_sems, chan_sems, bin_sems,
):
    bin_size = lax.axis_size("bin")
    chan_size = lax.axis_size("chan")
    my_bin = lax.axis_index("bin")
    my_chan = lax.axis_index("chan")
    chans = spec_ref.shape[1]
    bins = spec_ref.shape[2]
    half = samples // 2
    quarter = half // 2
    groups, _, rows, _ = send_ref.shape
    width = out_ref.shape[1]
    tile = LANES
    own = bins // bin_size
    cut = own // tile
    spans = width // tile
    count = quarter // LANES
    pack = 16

    pairs = chan_size // 2
    partners = list(range(2, chan_size)) + [1]

    def chan_at(offset):
        return (my_chan // 2 + offset // 2) % pairs * 2 + (my_chan + offset) % 2

    def mirror(offset):
        return (pairs - offset // 2) % pairs * 2 + offset % 2

    def bin_at(offset):
        return lax.rem(my_bin + offset, bin_size)

    def block_at(p):
        return bin_at(p + 1)

    def spec_copy(p):
        at = pl.ds(pl.multiple_of(block_at(p) * own, LANES), own)
        return pltpu.make_async_copy(
            spec_hbm.at[:, :, at], spec_ref.at[:, :, at], load_sems.at[2 + p]
        )

    rank = my_chan * bin_size + my_bin
    mine = pl.ds(pl.multiple_of(rank * chans, LANES), chans)
    delay_copy = pltpu.make_async_copy(delay_hbm.at[:, mine], delay_ref, load_sems.at[0])
    dm_copy = pltpu.make_async_copy(dm_hbm, dm_ref, load_sems.at[1])
    delay_copy.start()
    dm_copy.start()

    barrier = pltpu.get_barrier_semaphore()

    def greet_chan(offset, _):
        pl.semaphore_signal(
            barrier, inc=1, device_id={"chan": chan_at(offset)}, device_id_type=MESH
        )
        return 0

    def greet_bin(offset, _):
        pl.semaphore_signal(barrier, inc=1, device_id={"bin": bin_at(offset)}, device_id_type=MESH)
        return 0

    for offset in range(1, bin_size):
        greet_bin(offset, 0)
    for offset in partners:
        greet_chan(offset, 0)
    for p in range(bin_size):
        spec_copy(p).start()
    bank_copy = pltpu.make_async_copy(bank_hbm, bank_ref, load_sems.at[2 + bin_size])
    ids_copy = pltpu.make_async_copy(ids_hbm, ids_ref, load_sems.at[3 + bin_size])
    bank_copy.start()
    ids_copy.start()

    near = lax.broadcasted_iota(jnp.int32, (own, own), 0)
    far = lax.broadcasted_iota(jnp.int32, (own, own), 1)
    source = jnp.where(near < tile, 2 * near + 1, 2 * (near - tile))
    split_ref[...] = (far == source).astype(jnp.float32).astype(jnp.bfloat16)

    edge = jnp.zeros((rows, tile), sum_ref.dtype)
    sum_ref[0] = edge
    sum_ref[sum_ref.shape[0] - 1] = edge

    @pl.when(my_bin == 0)
    def _():
        for slot in range(1, bin_size):
            bin_recv[slot, 0] = edge

    @pl.when(my_bin == bin_size - 1)
    def _():
        for slot in range(1, bin_size):
            bin_recv[slot, spans - 1] = edge

    delay_copy.wait()
    delay = delay_ref[...]

    def rotations(factor):
        return cos_sin((factor * delay) & (samples - 1), samples)

    row = lax.broadcasted_iota(jnp.int32, (8, chans), 0)
    fine_cos, fine_sin = rotations(2 * row)
    mid_cos, mid_sin = rotations(2 * 8 * lax.broadcasted_iota(jnp.int32, (LANES // 8, chans), 0))
    high_cos, high_sin = rotations(jnp.where(row == 0, 1, 2 * LANES * row))
    one_cos, one_sin = high_cos[:1], high_sin[:1]
    for a in range(LANES // 8):
        at = slice(8 * a, 8 * a + 8)
        cos = fine_cos * mid_cos[a:a + 1] - fine_sin * mid_sin[a:a + 1]
        sin = fine_sin * mid_cos[a:a + 1] + fine_cos * mid_sin[a:a + 1]
        low_ref[0, at] = cos
        low_ref[1, at] = sin
        low_ref[2, at] = cos * one_cos - sin * one_sin
        low_ref[3, at] = sin * one_cos + cos * one_sin

    def fill(i, _):
        at = pl.ds(pl.multiple_of(i * pack, pack), pack)
        for odd in (0, 1):
            low_cos = low_ref[2 * odd, at]
            low_sin = low_ref[2 * odd + 1, at]
            for k in range(count):
                if k == 0:
                    cos, sin = low_cos, low_sin
                else:
                    block_cos, block_sin = high_cos[k:k + 1], high_sin[k:k + 1]
                    cos = low_cos * block_cos - low_sin * block_sin
                    sin = low_sin * block_cos + low_cos * block_sin
                for part, value in ((0, cos), (1, sin)):
                    first = ((2 * odd + part) * count + k) * LANES
                    to = pl.ds(pl.multiple_of(first + i * pack, pack), pack)
                    table_ref[to] = value.astype(jnp.bfloat16)
        return 0

    lax.fori_loop(0, LANES // pack, fill, 0)
    parity = (1 - 2 * (delay & 1)).astype(jnp.float32)
    top = lax.broadcasted_iota(jnp.int32, (pack, chans), 0) == 0
    table_ref[quarter:quarter + pack] = jnp.where(top, parity, low_ref[1, :pack]).astype(
        jnp.bfloat16
    )

    dm_copy.wait()
    lane = lax.broadcasted_iota(jnp.int32, (8, LANES), 1)
    dm = jnp.broadcast_to(dm_ref[...], (8, dm_ref.shape[1]))
    dm = jnp.concatenate([dm] * (LANES // dm_ref.shape[1]), 1)
    dm = take_lanes(dm, (lane // rows) * (rows // 2) + lane % (rows // 2))
    dm = jnp.concatenate([dm] * (pack // 8), 0)
    lane = lax.broadcasted_iota(jnp.int32, (pack, LANES), 1)
    real = 1 - (lane // (rows // 2)) % 2
    is_real = real.astype(jnp.int16) == 1
    flip = (2 * real - 1).astype(jnp.float32)

    def turned(block):
        at = pl.ds(pl.multiple_of(block * own, LANES), own)
        sides = [
            lax.dot_general(
                split_ref[...], spec_ref[part, :, at], (((1,), (1,)), ((), ())),
                preferred_element_type=jnp.float32,
            ).astype(jnp.bfloat16)
            for part in (0, 1)
        ]
        return [
            jnp.concatenate([side[n * tile:(n + 1) * tile] for side in sides], 0) for n in (0, 1)
        ]

    def multiply(left, prod_ref):
        size = prod_ref.shape[1]
        prod_ref[...] = lax.dot_general(
            left, table_ref[:size], (((1,), (1,)), ((), ())), preferred_element_type=jnp.float32
        ).astype(jnp.bfloat16)

    spots = lax.broadcasted_iota(jnp.int32, (pack, LANES), 0)
    steps = [[(spots * factor + shift) * dm for factor, shift in ((2, 1), (1, 0))],
             [factor * pack * dm for factor in (2, 1)]]
    flip = flip.astype(jnp.bfloat16)
    zero = jnp.zeros((pack, LANES), jnp.bfloat16)

    def collect(block, even, prod_ref):
        size = half >> even
        start = steps[0][even] + (block * (own >> even)) * dm
        places = list(range(count))
        if not even:
            places += list(range(2 * count, 3 * count))
        pieces = []
        for r in range(tile // pack):
            turns = (start + r * steps[1][even]) & (2 * size - 1)
            index = jnp.minimum(turns, 2 * size - turns) & (size - 1)
            if even:
                which = index >> 7
            else:
                which = (index >> 8) + (index & 1) * (2 * count)
                index = index >> 1
            spot = (index & (LANES - 1)).astype(jnp.int16)
            which = which.astype(jnp.int16)
            turns = turns.astype(jnp.int16)
            acc = [None] * 4
            for b in places:
                hit = which == b
                for i, (part, table) in enumerate(((0, 0), (1, 1), (1, 0), (0, 1))):
                    top = part * tile + r * pack
                    left = (b + table * count) * LANES
                    piece = gather_lanes(prod_ref[top:top + pack, left:left + LANES], spot)
                    acc[i] = piece if acc[i] is None else jnp.where(hit, piece, acc[i])
            a, b, a2, b2 = acc
            sign = jnp.where(turns > size, -flip, flip)
            side = jnp.where(turns == 0, zero, jnp.where(is_real, b, b2) * sign)
            sums = jnp.where(is_real, a, a2) + side
            pieces.append(jnp.where(turns == size, jnp.where(is_real, b2, b), sums))
        return pieces

    def compute(p):
        block = block_at(p)
        odd, even = turned(block)
        multiply(odd, odd_ref)
        multiply(even, even_ref)
        near = collect(block, 0, odd_ref)
        far = collect(block, 1, even_ref)
        part = len(near) // 2
        for t in (0, 1):
            picked = near[t * part:(t + 1) * part] + far[t * part:(t + 1) * part]
            send_ref[:, block * cut + t] = jnp.concatenate(picked, 0).T.reshape(groups, rows, tile)

    def chan_copy(p, offset):
        at = pl.ds(block_at(p) * cut, cut)
        return pltpu.make_async_remote_copy(
            src_ref=send_ref.at[chan_at(offset), at],
            dst_ref=chan_recv.at[mirror(offset), at],
            send_sem=chan_sems.at[0, offset, p],
            recv_sem=chan_sems.at[1, mirror(offset), p],
            device_id={"chan": chan_at(offset)},
            device_id_type=MESH,
        )

    def bin_copy(block, piece):
        to = block + (0, 1, -1)[piece]
        begin, size, land = ((0, cut, 1), (cut - 1, 1, 0), (0, 1, spans - 1))[piece]
        offset = lax.rem(to - my_bin + bin_size, bin_size)
        slot = lax.rem(bin_size - offset, bin_size)
        return pltpu.make_async_remote_copy(
            src_ref=sum_ref.at[pl.ds(1 + block * cut + begin, size)],
            dst_ref=bin_recv.at[slot, land:land + size],
            send_sem=bin_sems.at[0, piece, offset],
            recv_sem=bin_sems.at[1, piece, slot],
            device_id={"bin": to},
            device_id_type=MESH,
        )

    def each_piece(block, act):
        for piece in (2, 1, 0):
            to = block + (0, 1, -1)[piece]

            @pl.when((to >= 0) & (to < bin_size) & (to != my_bin))
            def _():
                act(bin_copy(block, piece))

    def forward(p):
        block = block_at(p)
        at = pl.ds(block * cut, cut)
        for offset in range(1, chan_size):
            chan_copy(p, mirror(offset)).wait_recv()
        total = send_ref[my_chan, at].astype(jnp.float32)
        for offset in range(1, chan_size):
            total += chan_recv[offset, at].astype(jnp.float32)
        sum_ref[pl.ds(1 + block * cut, cut)] = total.astype(sum_ref.dtype)
        each_piece(block, lambda copy: copy.start())

    def one_block(p, _):
        spec_copy(p).wait()
        compute(p)

        @pl.when(p == 0)
        def _():
            pl.semaphore_wait(barrier, chan_size + bin_size - 2)

        for offset in partners:
            chan_copy(p, offset).start()
        return 0

    lax.fori_loop(0, bin_size, one_block, 0)
    for p in range(bin_size - 1):
        forward(p)
    bank_copy.wait()
    ids_copy.wait()
    build_taps(bank_ref, ids_ref, taps_ref)
    forward(bin_size - 1)

    def drain(p, _):
        for offset in range(1, chan_size):
            chan_copy(p, offset).wait_send()

        @pl.when(p + 1 < bin_size)
        def _():
            each_piece(block_at(p), lambda copy: copy.wait_send())

        return 0

    lax.fori_loop(0, bin_size, drain, 0)

    def arrive(piece):
        begin, size = ((1, cut), (0, 1), (spans - 1, 1))[piece]
        for slot in range(1, bin_size):
            pltpu.make_async_remote_copy(
                src_ref=sum_ref.at[begin:begin + size],
                dst_ref=bin_recv.at[slot, begin:begin + size],
                send_sem=bin_sems.at[0, piece, slot],
                recv_sem=bin_sems.at[1, piece, slot],
                device_id={"bin": lax.rem(my_bin + slot, bin_size)},
                device_id_type=MESH,
            ).wait_recv()

    arrive(0)

    @pl.when(my_bin > 0)
    def _():
        arrive(1)

    @pl.when(my_bin < bin_size - 1)
    def _():
        arrive(2)

    total = sum_ref[pl.ds(my_bin * cut, spans)].astype(jnp.float32)
    for slot in range(1, bin_size):
        total += bin_recv[slot].astype(jnp.float32)
    signal = (total * scale).astype(jnp.bfloat16).astype(jnp.float32)
    lane = lax.broadcasted_iota(jnp.int32, (rows, tile), 1)
    back = (lane >> 1) + (tile // 2) * (1 - (lane & 1))
    for t in range(spans):
        out_ref[:, t * tile:(t + 1) * tile] = take_lanes(signal[t], back)

    each_piece(block_at(bin_size - 1), lambda copy: copy.wait_send())


def correlate_kernel(trials, signal_ref, taps_ref, out_hbm, power_ref, sems):
    _, templates, bins = power_ref.shape
    taps = taps_ref.shape[1] // 2
    group = math.gcd(trials, 2)

    pack = 16
    length = bins + taps

    def out_copy(g):
        at = pl.ds(g * group, group)
        return pltpu.make_async_copy(power_ref.at[at], out_hbm.at[at], sems.at[g])

    def one_group(g, _):
        for t in range(group):
            trial = g * group + t
            hankel = []
            for part in (0, 1):
                line = signal_ref[pl.ds(part * trials + trial, 1), :]
                line = jnp.broadcast_to(line, (pack, length)).astype(jnp.bfloat16)
                rows = [
                    pltpu.roll(line, length + pack * a - (LANES - 1), 1, stride=1, stride_axis=0)
                    for a in range(LANES // pack)
                ]
                hankel.append(jnp.concatenate(rows, 0))
            wide = jnp.concatenate(
                [
                    hankel[part][:, u * LANES:u * LANES + bins]
                    for part in (0, 1)
                    for u in range(taps // LANES)
                ],
                0,
            )
            response = jnp.dot(taps_ref[...], wide, preferred_element_type=jnp.float32)
            real = response[:templates]
            imag = response[templates:]
            power_ref[trial] = (real * real + imag * imag).astype(power_ref.dtype)
        out_copy(g).start()
        return 0

    for g in range(trials // group):
        one_group(g, 0)
    for g in range(trials // group):
        out_copy(g).wait()


def local(spectra, dm_trials, chan_delay, template_bank, template_ids):
    chans, bins = spectra.shape[1:]
    samples = 2 * bins
    bin_size = lax.axis_size("bin")
    chan_size = lax.axis_size("chan")
    trials = dm_trials.shape[0] // chan_size
    templates = template_ids.shape[0]
    taps = template_bank.shape[2]
    own = bins // bin_size
    width = own + 2 * EDGE
    scale = 1.0 / math.sqrt(chan_delay.shape[0])
    if chans % LANES:
        rank = lax.axis_index("chan") * bin_size + lax.axis_index("bin")
        chan_delay = lax.dynamic_slice_in_dim(chan_delay, rank * chans, chans)
    vmem = pl.BlockSpec(memory_space=pltpu.VMEM)
    products = pltpu.VMEM((2 * LANES, 2 * min(bins, 1024)), jnp.float32)

    paired = (
        bins <= 1024 and bins % (4 * LANES) == 0 and own == 2 * LANES and chans % LANES == 0
        and trials * 2 * chan_size == LANES and chan_size % 2 == 0
    )
    if paired:
        hbm = pl.BlockSpec(memory_space=pltpu.HBM)
        signal, chosen = pl.pallas_call(
            functools.partial(paired_kernel, samples, scale),
            out_shape=[
                jax.ShapeDtypeStruct((2 * trials, width), jnp.float32),
                jax.ShapeDtypeStruct((2 * templates, 2 * taps), jnp.bfloat16),
            ],
            in_specs=[hbm] * 5,
            out_specs=[vmem] * 2,
            scratch_shapes=[
                pltpu.VMEM((2, chans, bins), jnp.bfloat16),
                pltpu.VMEM((1, chans), jnp.int32),
                pltpu.VMEM((1, dm_trials.shape[0]), jnp.int32),
                pltpu.VMEM(template_bank.shape, jnp.bfloat16),
                pltpu.VMEM((1, templates), jnp.int32),
                pltpu.VMEM((chan_size, bins // LANES, 2 * trials, LANES), jnp.bfloat16),
                pltpu.VMEM((bins // LANES + 2, 2 * trials, LANES), jnp.bfloat16),
                pltpu.VMEM((chan_size, bins // LANES, 2 * trials, LANES), jnp.bfloat16),
                pltpu.VMEM((bin_size, width // LANES, 2 * trials, LANES), jnp.bfloat16),
                pltpu.VMEM((4, LANES, chans), jnp.float32),
                pltpu.VMEM((2 * bins, chans), jnp.bfloat16),
                pltpu.VMEM((own, own), jnp.bfloat16),
                pltpu.VMEM((2 * LANES, 2 * bins), jnp.bfloat16),
                pltpu.VMEM((2 * LANES, bins), jnp.bfloat16),
                pltpu.SemaphoreType.DMA((4 + bin_size,)),
                pltpu.SemaphoreType.DMA((2, chan_size, bin_size)),
                pltpu.SemaphoreType.DMA((2, 3, bin_size)),
            ],
            compiler_params=pltpu.CompilerParams(
                collective_id=0, has_side_effects=True, vmem_limit_bytes=24 * 2 ** 20
            ),
            name="dedisperse",
        )(*[
            pltpu.with_memory_space_constraint(x, pltpu.HBM)
            for x in (
                spectra, chan_delay[None, :], dm_trials[None, :], template_bank,
                template_ids[None, :],
            )
        ])
    else:
        signal = pl.pallas_call(
            functools.partial(dedisperse_kernel, samples, scale),
            out_shape=jax.ShapeDtypeStruct((2 * trials, width), jnp.float32),
            in_specs=[vmem] * 3,
            out_specs=vmem,
            scratch_shapes=[
                pltpu.VMEM((chan_size, 2 * trials, bins), jnp.bfloat16),
                pltpu.VMEM((2 * trials, bins + 2 * EDGE), jnp.bfloat16),
                pltpu.VMEM((chan_size, 2 * trials, bins), jnp.bfloat16),
                pltpu.VMEM((bin_size, 2 * trials, width), jnp.bfloat16),
                pltpu.VMEM((chans, 2 * bins), jnp.bfloat16),
                pltpu.VMEM((chans, bins), jnp.bfloat16),
                pltpu.VMEM((own, own), jnp.bfloat16),
                pltpu.VMEM((own, own), jnp.bfloat16),
                products,
                products,
                pltpu.SemaphoreType.DMA((2, chan_size, bin_size)),
                pltpu.SemaphoreType.DMA((2, 3, bin_size)),
            ],
            compiler_params=pltpu.CompilerParams(collective_id=0, has_side_effects=True),
            name="dedisperse",
        )(spectra, chan_delay[None, :], dm_trials[None, :])

        chosen = pl.pallas_call(
            build_taps,
            out_shape=jax.ShapeDtypeStruct((2 * templates, 2 * taps), jnp.bfloat16),
            in_specs=[vmem] * 2,
            out_specs=vmem,
            name="taps",
        )(template_bank, template_ids[None, :])

    return pl.pallas_call(
        functools.partial(correlate_kernel, trials),
        out_shape=jax.ShapeDtypeStruct((trials, templates, own), jnp.bfloat16),
        in_specs=[vmem] * 2,
        out_specs=pl.BlockSpec(memory_space=pltpu.HBM),
        scratch_shapes=[
            pltpu.VMEM((trials, templates, own), jnp.bfloat16),
            pltpu.SemaphoreType.DMA((trials,)),
        ],
        compiler_params=pltpu.CompilerParams(vmem_limit_bytes=16 * 2 ** 20),
        name="templates",
    )(signal, chosen)


def solution(mesh):
    in_specs = (P(None, ("beam", "chan", "bin"), None), P(), P(), P(), P())
    out_specs = P(("beam", "chan"), None, "bin")
    return jax.shard_map(local, mesh=mesh, in_specs=in_specs, out_specs=out_specs, check_vma=False)
```

```python
import functools
import math

import jax
import jax.numpy as jnp
from jax import lax
from jax.experimental import pallas as pl
from jax.experimental.pallas import tpu as pltpu
from jax.sharding import PartitionSpec as P

EDGE = 128
LANES = 128
MESH = pl.DeviceIdType.MESH


def cos_sin(turns, samples):
    eighth = samples // 8
    quadrant = lax.shift_right_logical(turns + eighth, eighth.bit_length())
    rest = turns - quadrant * (2 * eighth)
    x = rest.astype(jnp.float32) * (2.0 * math.pi / samples)
    y = x * x
    c = 1.0 + y * (-0.5 + y * (1.0 / 24 + y * (-1.0 / 720 + y * (1.0 / 40320))))
    s = x * (1.0 + y * (-1.0 / 6 + y * (1.0 / 120 + y * (-1.0 / 5040 + y * (1.0 / 362880)))))
    swap = (quadrant & 1) == 1
    cos = jnp.where(swap, s, c)
    sin = jnp.where(swap, c, s)
    cos = jnp.where(((quadrant + 1) & 2) == 2, -cos, cos)
    sin = jnp.where((quadrant & 2) == 2, -sin, sin)
    return cos, sin


def take_lanes(x, index):
    return jnp.take_along_axis(x, index, axis=1, mode="promise_in_bounds")


def dedisperse_kernel(
    samples, scale, spec_ref, delay_ref, dm_ref, out_ref, send_ref, sum_ref, chan_recv, bin_recv,
    table_ref, even_ref, split_ref, merge_ref, prod_a, prod_b, chan_sems, bin_sems,
):
    bin_size = lax.axis_size("bin")
    chan_size = lax.axis_size("chan")
    my_bin = lax.axis_index("bin")
    my_chan = lax.axis_index("chan")
    chans = spec_ref.shape[1]
    bins = spec_ref.shape[2]
    half = samples // 2
    group = prod_a.shape[1] // 2
    blocks = group // LANES
    all_blocks = half // LANES
    groups, rows = send_ref.shape[:2]
    width = out_ref.shape[1]
    tile = LANES
    own = bins // bin_size
    tiles = own // tile
    padded = max(chans, LANES)

    def chan_at(offset):
        return lax.rem(my_chan + offset, chan_size)

    def bin_at(offset):
        return lax.rem(my_bin + offset, bin_size)

    barrier = pltpu.get_barrier_semaphore()

    def greet_chan(offset, _):
        pl.semaphore_signal(
            barrier, inc=1, device_id={"chan": chan_at(offset)}, device_id_type=MESH
        )
        return 0

    def greet_bin(offset, _):
        pl.semaphore_signal(barrier, inc=1, device_id={"bin": bin_at(offset)}, device_id_type=MESH)
        return 0

    lax.fori_loop(1, chan_size, greet_chan, 0)
    lax.fori_loop(1, bin_size, greet_bin, 0)

    if delay_ref.shape[1] == chans:
        delay = delay_ref[...]
    else:
        rank = lax.axis_index("chan") * bin_size + lax.axis_index("bin")
        delay = delay_ref[:, pl.ds(pl.multiple_of(rank * chans, LANES), chans)]
    if chans < padded:
        delay = jnp.concatenate([delay, jnp.zeros((1, padded - chans), jnp.int32)], 1)

    def rotations(count, stride):
        turns = lax.broadcasted_iota(jnp.int32, (count, padded), 0) * stride * delay
        return cos_sin(turns & (samples - 1), samples)

    fine_cos, fine_sin = rotations(8, 1)
    mid_cos, mid_sin = rotations(LANES // 8, 8)
    low_cos = jnp.concatenate(
        [fine_cos * mid_cos[a:a + 1] - fine_sin * mid_sin[a:a + 1] for a in range(LANES // 8)], 0
    ).T[:chans]
    low_sin = jnp.concatenate(
        [fine_sin * mid_cos[a:a + 1] + fine_cos * mid_sin[a:a + 1] for a in range(LANES // 8)], 0
    ).T[:chans]
    coarse_cos, coarse_sin = rotations(all_blocks + 8, LANES)
    fill_rows = jnp.zeros((LANES - all_blocks - 8, padded), jnp.float32)
    high_cos = jnp.concatenate([coarse_cos, fill_rows], 0).T[:chans]
    high_sin = jnp.concatenate([coarse_sin, fill_rows], 0).T[:chans]
    lane_ids = lax.broadcasted_iota(jnp.int32, (chans, LANES), 1)

    def fill(block, _):
        spread = jnp.full((chans, LANES), block, jnp.int32)
        block_cos = take_lanes(high_cos, spread)
        block_sin = take_lanes(high_sin, spread)
        at = pl.multiple_of(block * LANES, LANES)
        cos = low_cos * block_cos - low_sin * block_sin
        sin = low_sin * block_cos + low_cos * block_sin
        table_ref[:, pl.ds(at, LANES)] = cos.astype(jnp.bfloat16)
        table_ref[:, pl.ds(half + at, LANES)] = sin.astype(jnp.bfloat16)
        return 0

    lax.fori_loop(0, all_blocks, fill, 0)
    parity = take_lanes(high_cos, jnp.full((chans, LANES), all_blocks, jnp.int32))
    table_ref[:, half:half + LANES] = jnp.where(lane_ids == 0, parity, low_sin).astype(jnp.bfloat16)

    paired = half == group and tiles == 2 and half % (4 * LANES) == 0
    if paired:
        even_cos = low_cos * low_cos - low_sin * low_sin
        even_sin = 2.0 * low_sin * low_cos
        for block in range(all_blocks // 2):
            spread = jnp.full((chans, LANES), 2 * block, jnp.int32)
            block_cos = take_lanes(high_cos, spread)
            block_sin = take_lanes(high_sin, spread)
            at = block * LANES
            cos = even_cos * block_cos - even_sin * block_sin
            sin = even_sin * block_cos + even_cos * block_sin
            if block == 0:
                sin = jnp.where(lane_ids == 0, parity, sin)
            even_ref[:, at:at + LANES] = cos.astype(jnp.bfloat16)
            even_ref[:, half // 2 + at:half // 2 + at + LANES] = sin.astype(jnp.bfloat16)
        near = lax.broadcasted_iota(jnp.int32, (own, own), 0)
        far = lax.broadcasted_iota(jnp.int32, (own, own), 1)

        def source(spot):
            return jnp.where(spot < tile, 2 * spot + 1, 2 * (spot - tile))

        split_ref[...] = (near == source(far)).astype(jnp.float32).astype(jnp.bfloat16)
        merge_ref[...] = (far == source(near)).astype(jnp.float32).astype(jnp.bfloat16)

    lane = lax.broadcasted_iota(jnp.int32, (8, LANES), 1)
    is_real = (lane // (rows // 2)) % 2 == 0
    dm = jnp.broadcast_to(dm_ref[...], (8, dm_ref.shape[1]))
    dm = jnp.concatenate([dm] * (LANES // dm_ref.shape[1]), 1)
    dm = take_lanes(dm, (lane // rows) * (rows // 2) + lane % (rows // 2))

    def first_of(step):
        return pl.multiple_of(step * tile, tile)

    def multiply(step, g, prod_ref):
        at = pl.ds(first_of(step), tile)
        both = jnp.concatenate([spec_ref[0, :, at], spec_ref[1, :, at]], 1)
        for part in (0, 1):
            columns = pl.ds(pl.multiple_of(part * half + g * group, group), group)
            prod_ref[:, part * group:(part + 1) * group] = lax.dot_general(
                both, table_ref[:, columns], (((0,), (0,)), ((), ())),
                preferred_element_type=jnp.float32,
            )

    def turns_of(step, r):
        bin_ids = step * tile + r * 8 + lax.broadcasted_iota(jnp.int32, (8, LANES), 0)
        return (bin_ids * dm) & (samples - 1)

    def pick(turns, half, group, g, r, prod_ref, acc):
        folded = jnp.where(turns > half, 2 * half - turns, turns)
        index = folded & (half - 1)
        spot = index & (LANES - 1)
        which = index // LANES - g * (group // LANES)
        acc = list(acc)
        for b in range(group // LANES):
            hit = which == b
            for i, (part, table) in enumerate(((0, 0), (1, 1), (1, 0), (0, 1))):
                top = part * tile + r * 8
                left = table * group + b * LANES
                piece = take_lanes(prod_ref[top:top + 8, left:left + LANES], spot)
                acc[i] = piece if acc[i] is None else jnp.where(hit, piece, acc[i])
        return acc

    def finish(turns, half, acc):
        sign = jnp.where(turns > half, -1.0, jnp.where(turns == 0, 0.0, 1.0))
        a, b, a2, b2 = acc
        real = jnp.where(turns == half, b2, a + sign * b)
        imag = jnp.where(turns == half, b, a2 - sign * b2)
        return jnp.where(is_real, real, imag)

    def split_multiply(block, even, prod_ref):
        at = pl.ds(pl.multiple_of(block * own, LANES), own)
        chosen = split_ref[:, even * tile:(even + 1) * tile]
        both = jnp.concatenate(
            [
                jnp.dot(spec_ref[part, :, at], chosen, preferred_element_type=jnp.float32)
                for part in (0, 1)
            ],
            1,
        ).astype(jnp.bfloat16)
        size = 2 * half // (1 + even)
        prod_ref[:, :size] = lax.dot_general(
            both, (even_ref if even else table_ref)[...], (((0,), (0,)), ((), ())),
            preferred_element_type=jnp.float32,
        )

    def split_gather(block, even, prod_ref):
        pieces = []
        for r in range(tile // 8):
            spots = r * 8 + lax.broadcasted_iota(jnp.int32, (8, LANES), 0)
            bin_ids = block * own + 2 * spots + (1 - even)
            turns = ((bin_ids * dm) & (samples - 1)) >> even
            size = half >> even
            acc = pick(turns, size, size, 0, r, prod_ref, [None] * 4)
            pieces.append(finish(turns, size, acc))
        return pieces

    def put(step, pieces):
        block = jnp.concatenate(pieces, 0).T
        at = pl.ds(first_of(step), tile)
        send_ref[:, :, at] = block.reshape(groups, rows, tile).astype(send_ref.dtype)

    def block_at(p):
        return bin_at(p + 1)

    def compute(p):
        base = block_at(p) * tiles

        def one_tile(t, _):
            step = base + t

            def one_group(g, accs):
                multiply(step, g, prod_a)
                new = []
                for r in range(tile // 8):
                    new += pick(
                        turns_of(step, r), half, group, g, r, prod_a, accs[4 * r:4 * r + 4]
                    )
                return tuple(new)

            zero = jnp.zeros((8, LANES), jnp.float32)
            accs = lax.fori_loop(0, half // group, one_group, (zero,) * (4 * (tile // 8)))
            put(step, [
                finish(turns_of(step, r), half, accs[4 * r:4 * r + 4]) for r in range(tile // 8)
            ])
            return 0

        if paired:
            block = block_at(p)
            split_multiply(block, 1, prod_b)
            pieces = split_gather(block, 0, prod_a)
            split_multiply(block_at(jnp.minimum(p + 1, bin_size - 1)), 0, prod_a)
            pieces += split_gather(block, 1, prod_b)
            merged = lax.dot_general(
                jnp.concatenate(pieces, 0).astype(jnp.bfloat16), merge_ref[...],
                (((0,), (0,)), ((), ())), preferred_element_type=jnp.float32,
            )
            at = pl.ds(pl.multiple_of(block * own, LANES), own)
            send_ref[:, :, at] = merged.reshape(groups, rows, own).astype(send_ref.dtype)
        else:
            lax.fori_loop(0, tiles, one_tile, 0)

    def chan_copy(p, offset):
        at = pl.ds(pl.multiple_of(block_at(p) * own, LANES), own)
        return pltpu.make_async_remote_copy(
            src_ref=send_ref.at[chan_at(offset), :, at],
            dst_ref=chan_recv.at[chan_size - offset, :, at],
            send_sem=chan_sems.at[0, offset, p],
            recv_sem=chan_sems.at[1, chan_size - offset, p],
            device_id={"chan": chan_at(offset)},
            device_id_type=MESH,
        )

    def bin_copy(block, piece):
        to = block + (0, 1, -1)[piece]
        begin, size, land = ((0, own, EDGE), (own - EDGE, EDGE, 0), (0, EDGE, EDGE + own))[piece]
        offset = lax.rem(to - my_bin + bin_size, bin_size)
        slot = lax.rem(bin_size - offset, bin_size)
        return pltpu.make_async_remote_copy(
            src_ref=sum_ref.at[:, pl.ds(pl.multiple_of(EDGE + block * own + begin, LANES), size)],
            dst_ref=bin_recv.at[slot, :, land:land + size],
            send_sem=bin_sems.at[0, piece, offset],
            recv_sem=bin_sems.at[1, piece, slot],
            device_id={"bin": to},
            device_id_type=MESH,
        )

    def each_piece(block, act):
        for piece in range(3):
            to = block + (0, 1, -1)[piece]

            @pl.when((to >= 0) & (to < bin_size) & (to != my_bin))
            def _():
                act(bin_copy(block, piece))

    def forward(p):
        block = block_at(p)
        at = pl.multiple_of(block * own, LANES)
        for offset in range(1, chan_size):
            chan_copy(p, chan_size - offset).wait_recv()
        total = send_ref[my_chan, :, pl.ds(at, own)].astype(jnp.float32)
        for offset in range(1, chan_size):
            total += chan_recv[offset, :, pl.ds(at, own)].astype(jnp.float32)
        sum_ref[:, pl.ds(pl.multiple_of(EDGE + at, LANES), own)] = total.astype(sum_ref.dtype)
        each_piece(block, lambda copy: copy.start())

    edge = jnp.zeros((rows, EDGE), sum_ref.dtype)
    sum_ref[:, :EDGE] = edge
    sum_ref[:, EDGE + bins:] = edge

    @pl.when(my_bin == 0)
    def _():
        for slot in range(1, bin_size):
            bin_recv[slot, :, :EDGE] = edge

    @pl.when(my_bin == bin_size - 1)
    def _():
        for slot in range(1, bin_size):
            bin_recv[slot, :, EDGE + own:] = edge

    if paired:
        split_multiply(block_at(0), 0, prod_a)
    pl.semaphore_wait(barrier, chan_size + bin_size - 2)

    def one_block(p, _):
        compute(p)
        for offset in range(1, chan_size):
            chan_copy(p, offset).start()

        @pl.when(p > 0)
        def _():
            forward(p - 1)

        return 0

    lax.fori_loop(0, bin_size, one_block, 0)
    forward(bin_size - 1)

    total = sum_ref[:, pl.ds(pl.multiple_of(my_bin * own, LANES), width)].astype(jnp.float32)
    for slot in range(1, bin_size):
        for piece in range(3):
            begin, size = ((EDGE, own), (0, EDGE), (EDGE + own, EDGE))[piece]
            sender = lax.rem(my_bin + slot, bin_size)
            comes = (True, my_bin > 0, my_bin < bin_size - 1)[piece]

            @pl.when(comes)
            def _():
                pltpu.make_async_remote_copy(
                    src_ref=sum_ref.at[:, begin:begin + size],
                    dst_ref=bin_recv.at[slot, :, begin:begin + size],
                    send_sem=bin_sems.at[0, piece, slot],
                    recv_sem=bin_sems.at[1, piece, slot],
                    device_id={"bin": sender},
                    device_id_type=MESH,
                ).wait_recv()

        total += bin_recv[slot].astype(jnp.float32)
    out_ref[...] = (total * scale).astype(jnp.bfloat16).astype(jnp.float32)

    def drain(p, _):
        for offset in range(1, chan_size):
            chan_copy(p, offset).wait_send()
        each_piece(block_at(p), lambda copy: copy.wait_send())
        return 0

    lax.fori_loop(0, bin_size, drain, 0)


def gather_lanes(x, index):
    return lax.gather(
        x, index[:, :, None],
        dimension_numbers=lax.GatherDimensionNumbers(
            offset_dims=(), collapsed_slice_dims=(1,), start_index_map=(1,),
            operand_batching_dims=(0,), start_indices_batching_dims=(0,),
        ),
        slice_sizes=(1, 1), mode="promise_in_bounds",
    )


def build_taps(bank_ref, ids_ref, taps_ref):
    bank_size, taps = bank_ref.shape[1:]
    templates = ids_ref.shape[1]
    rows = lax.broadcasted_iota(jnp.int32, (bank_size, templates), 0)
    one_hot = (ids_ref[...] == rows).astype(jnp.bfloat16)
    back = (LANES - 1 - lax.broadcasted_iota(jnp.int32, (16, LANES), 1)).astype(jnp.int16)
    back = jnp.concatenate([back] * (templates // 16), 0)
    for part in (0, 1):
        chosen = lax.dot_general(
            one_hot, bank_ref[part], (((0,), (0,)), ((), ())), preferred_element_type=jnp.float32
        ).astype(jnp.bfloat16)
        for u in range(taps // LANES):
            at = u * LANES
            turned = gather_lanes(chosen[:, at:at + LANES], back)
            taps_ref[part * templates:(part + 1) * templates, at:at + LANES] = turned
            taps_ref[
                (1 - part) * templates:(2 - part) * templates, taps + at:taps + at + LANES
            ] = turned if part == 0 else -turned


def paired_kernel(
    samples, scale, spec_hbm, delay_hbm, dm_hbm, bank_hbm, ids_hbm, out_ref, taps_ref, spec_ref,
    delay_ref, dm_ref, bank_ref, ids_ref, send_ref,
    sum_ref, chan_recv, bin_recv, low_ref, table_ref, split_ref, odd_ref, even_ref,
    load_sems, chan_sems, bin_sems,
):
    bin_size = lax.axis_size("bin")
    chan_size = lax.axis_size("chan")
    my_bin = lax.axis_index("bin")
    my_chan = lax.axis_index("chan")
    chans = spec_ref.shape[1]
    bins = spec_ref.shape[2]
    half = samples // 2
    quarter = half // 2
    groups, _, rows, _ = send_ref.shape
    width = out_ref.shape[1]
    tile = LANES
    own = bins // bin_size
    cut = own // tile
    spans = width // tile
    count = quarter // LANES
    pack = 16

    pairs = chan_size // 2
    partners = list(range(2, chan_size)) + [1]

    def chan_at(offset):
        return (my_chan // 2 + offset // 2) % pairs * 2 + (my_chan + offset) % 2

    def mirror(offset):
        return (pairs - offset // 2) % pairs * 2 + offset % 2

    def bin_at(offset):
        return lax.rem(my_bin + offset, bin_size)

    def block_at(p):
        return bin_at(p + 1)

    def spec_copy(p):
        at = pl.ds(pl.multiple_of(block_at(p) * own, LANES), own)
        return pltpu.make_async_copy(
            spec_hbm.at[:, :, at], spec_ref.at[:, :, at], load_sems.at[2 + p]
        )

    rank = my_chan * bin_size + my_bin
    mine = pl.ds(pl.multiple_of(rank * chans, LANES), chans)
    delay_copy = pltpu.make_async_copy(delay_hbm.at[:, mine], delay_ref, load_sems.at[0])
    dm_copy = pltpu.make_async_copy(dm_hbm, dm_ref, load_sems.at[1])
    delay_copy.start()
    dm_copy.start()

    barrier = pltpu.get_barrier_semaphore()

    def greet_chan(offset, _):
        pl.semaphore_signal(
            barrier, inc=1, device_id={"chan": chan_at(offset)}, device_id_type=MESH
        )
        return 0

    def greet_bin(offset, _):
        pl.semaphore_signal(barrier, inc=1, device_id={"bin": bin_at(offset)}, device_id_type=MESH)
        return 0

    for offset in range(1, bin_size):
        greet_bin(offset, 0)
    for offset in partners:
        greet_chan(offset, 0)
    for p in range(bin_size):
        spec_copy(p).start()
    bank_copy = pltpu.make_async_copy(bank_hbm, bank_ref, load_sems.at[2 + bin_size])
    ids_copy = pltpu.make_async_copy(ids_hbm, ids_ref, load_sems.at[3 + bin_size])
    bank_copy.start()
    ids_copy.start()

    near = lax.broadcasted_iota(jnp.int32, (own, own), 0)
    far = lax.broadcasted_iota(jnp.int32, (own, own), 1)
    source = jnp.where(near < tile, 2 * near + 1, 2 * (near - tile))
    split_ref[...] = (far == source).astype(jnp.float32).astype(jnp.bfloat16)

    edge = jnp.zeros((rows, tile), sum_ref.dtype)
    sum_ref[0] = edge
    sum_ref[sum_ref.shape[0] - 1] = edge

    @pl.when(my_bin == 0)
    def _():
        for slot in range(1, bin_size):
            bin_recv[slot, 0] = edge

    @pl.when(my_bin == bin_size - 1)
    def _():
        for slot in range(1, bin_size):
            bin_recv[slot, spans - 1] = edge

    delay_copy.wait()
    delay = delay_ref[...]

    def rotations(factor):
        return cos_sin((factor * delay) & (samples - 1), samples)

    row = lax.broadcasted_iota(jnp.int32, (8, chans), 0)
    fine_cos, fine_sin = rotations(2 * row)
    mid_cos, mid_sin = rotations(2 * 8 * lax.broadcasted_iota(jnp.int32, (LANES // 8, chans), 0))
    high_cos, high_sin = rotations(jnp.where(row == 0, 1, 2 * LANES * row))
    one_cos, one_sin = high_cos[:1], high_sin[:1]
    for a in range(LANES // 8):
        at = slice(8 * a, 8 * a + 8)
        cos = fine_cos * mid_cos[a:a + 1] - fine_sin * mid_sin[a:a + 1]
        sin = fine_sin * mid_cos[a:a + 1] + fine_cos * mid_sin[a:a + 1]
        low_ref[0, at] = cos
        low_ref[1, at] = sin
        low_ref[2, at] = cos * one_cos - sin * one_sin
        low_ref[3, at] = sin * one_cos + cos * one_sin

    def fill(i, _):
        at = pl.ds(pl.multiple_of(i * pack, pack), pack)
        for odd in (0, 1):
            low_cos = low_ref[2 * odd, at]
            low_sin = low_ref[2 * odd + 1, at]
            for k in range(count):
                if k == 0:
                    cos, sin = low_cos, low_sin
                else:
                    block_cos, block_sin = high_cos[k:k + 1], high_sin[k:k + 1]
                    cos = low_cos * block_cos - low_sin * block_sin
                    sin = low_sin * block_cos + low_cos * block_sin
                for part, value in ((0, cos), (1, sin)):
                    first = ((2 * odd + part) * count + k) * LANES
                    to = pl.ds(pl.multiple_of(first + i * pack, pack), pack)
                    table_ref[to] = value.astype(jnp.bfloat16)
        return 0

    lax.fori_loop(0, LANES // pack, fill, 0)
    parity = (1 - 2 * (delay & 1)).astype(jnp.float32)
    top = lax.broadcasted_iota(jnp.int32, (pack, chans), 0) == 0
    table_ref[quarter:quarter + pack] = jnp.where(top, parity, low_ref[1, :pack]).astype(
        jnp.bfloat16
    )

    dm_copy.wait()
    lane = lax.broadcasted_iota(jnp.int32, (8, LANES), 1)
    dm = jnp.broadcast_to(dm_ref[...], (8, dm_ref.shape[1]))
    dm = jnp.concatenate([dm] * (LANES // dm_ref.shape[1]), 1)
    dm = take_lanes(dm, (lane // rows) * (rows // 2) + lane % (rows // 2))
    dm = jnp.concatenate([dm] * (pack // 8), 0)
    lane = lax.broadcasted_iota(jnp.int32, (pack, LANES), 1)
    real = 1 - (lane // (rows // 2)) % 2
    is_real = real.astype(jnp.int16) == 1
    flip = (2 * real - 1).astype(jnp.float32)

    def turned(block):
        at = pl.ds(pl.multiple_of(block * own, LANES), own)
        sides = [
            lax.dot_general(
                split_ref[...], spec_ref[part, :, at], (((1,), (1,)), ((), ())),
                preferred_element_type=jnp.float32,
            ).astype(jnp.bfloat16)
            for part in (0, 1)
        ]
        return [
            jnp.concatenate([side[n * tile:(n + 1) * tile] for side in sides], 0) for n in (0, 1)
        ]

    def multiply(left, prod_ref):
        size = prod_ref.shape[1]
        prod_ref[...] = lax.dot_general(
            left, table_ref[:size], (((1,), (1,)), ((), ())), preferred_element_type=jnp.float32
        ).astype(jnp.bfloat16)

    spots = lax.broadcasted_iota(jnp.int32, (pack, LANES), 0)
    steps = [[(spots * factor + shift) * dm for factor, shift in ((2, 1), (1, 0))],
             [factor * pack * dm for factor in (2, 1)]]
    flip = flip.astype(jnp.bfloat16)
    zero = jnp.zeros((pack, LANES), jnp.bfloat16)

    def collect(block, even, prod_ref):
        size = half >> even
        start = steps[0][even] + (block * (own >> even)) * dm
        places = list(range(count))
        if not even:
            places += list(range(2 * count, 3 * count))
        pieces = []
        for r in range(tile // pack):
            turns = (start + r * steps[1][even]) & (2 * size - 1)
            index = jnp.minimum(turns, 2 * size - turns) & (size - 1)
            if even:
                which = index >> 7
            else:
                which = (index >> 8) + (index & 1) * (2 * count)
                index = index >> 1
            spot = (index & (LANES - 1)).astype(jnp.int16)
            which = which.astype(jnp.int16)
            turns = turns.astype(jnp.int16)
            acc = [None] * 4
            for b in places:
                hit = which == b
                for i, (part, table) in enumerate(((0, 0), (1, 1), (1, 0), (0, 1))):
                    top = part * tile + r * pack
                    left = (b + table * count) * LANES
                    piece = gather_lanes(prod_ref[top:top + pack, left:left + LANES], spot)
                    acc[i] = piece if acc[i] is None else jnp.where(hit, piece, acc[i])
            a, b, a2, b2 = acc
            sign = jnp.where(turns > size, -flip, flip)
            side = jnp.where(turns == 0, zero, jnp.where(is_real, b, b2) * sign)
            sums = jnp.where(is_real, a, a2) + side
            pieces.append(jnp.where(turns == size, jnp.where(is_real, b2, b), sums))
        return pieces

    def compute(p):
        block = block_at(p)
        odd, even = turned(block)
        multiply(odd, odd_ref)
        multiply(even, even_ref)
        near = collect(block, 0, odd_ref)
        far = collect(block, 1, even_ref)
        part = len(near) // 2
        for t in (0, 1):
            picked = near[t * part:(t + 1) * part] + far[t * part:(t + 1) * part]
            send_ref[:, block * cut + t] = jnp.concatenate(picked, 0).T.reshape(groups, rows, tile)

    def chan_copy(p, offset):
        at = pl.ds(block_at(p) * cut, cut)
        return pltpu.make_async_remote_copy(
            src_ref=send_ref.at[chan_at(offset), at],
            dst_ref=chan_recv.at[mirror(offset), at],
            send_sem=chan_sems.at[0, offset, p],
            recv_sem=chan_sems.at[1, mirror(offset), p],
            device_id={"chan": chan_at(offset)},
            device_id_type=MESH,
        )

    def bin_copy(block, piece):
        to = block + (0, 1, -1)[piece]
        begin, size, land = ((0, cut, 1), (cut - 1, 1, 0), (0, 1, spans - 1))[piece]
        offset = lax.rem(to - my_bin + bin_size, bin_size)
        slot = lax.rem(bin_size - offset, bin_size)
        return pltpu.make_async_remote_copy(
            src_ref=sum_ref.at[pl.ds(1 + block * cut + begin, size)],
            dst_ref=bin_recv.at[slot, land:land + size],
            send_sem=bin_sems.at[0, piece, offset],
            recv_sem=bin_sems.at[1, piece, slot],
            device_id={"bin": to},
            device_id_type=MESH,
        )

    def each_piece(block, act):
        for piece in (2, 1, 0):
            to = block + (0, 1, -1)[piece]

            @pl.when((to >= 0) & (to < bin_size) & (to != my_bin))
            def _():
                act(bin_copy(block, piece))

    def forward(p):
        block = block_at(p)
        at = pl.ds(block * cut, cut)
        for offset in range(1, chan_size):
            chan_copy(p, mirror(offset)).wait_recv()
        total = send_ref[my_chan, at].astype(jnp.float32)
        for offset in range(1, chan_size):
            total += chan_recv[offset, at].astype(jnp.float32)
        sum_ref[pl.ds(1 + block * cut, cut)] = total.astype(sum_ref.dtype)
        each_piece(block, lambda copy: copy.start())

    def one_block(p, _):
        spec_copy(p).wait()
        compute(p)

        @pl.when(p == 0)
        def _():
            pl.semaphore_wait(barrier, chan_size + bin_size - 2)

        for offset in partners:
            chan_copy(p, offset).start()
        return 0

    lax.fori_loop(0, bin_size, one_block, 0)
    for p in range(bin_size - 1):
        forward(p)
    bank_copy.wait()
    ids_copy.wait()
    build_taps(bank_ref, ids_ref, taps_ref)
    forward(bin_size - 1)

    def drain(p, _):
        for offset in range(1, chan_size):
            chan_copy(p, offset).wait_send()

        @pl.when(p + 1 < bin_size)
        def _():
            each_piece(block_at(p), lambda copy: copy.wait_send())

        return 0

    lax.fori_loop(0, bin_size, drain, 0)

    def arrive(piece):
        begin, size = ((1, cut), (0, 1), (spans - 1, 1))[piece]
        for slot in range(1, bin_size):
            pltpu.make_async_remote_copy(
                src_ref=sum_ref.at[begin:begin + size],
                dst_ref=bin_recv.at[slot, begin:begin + size],
                send_sem=bin_sems.at[0, piece, slot],
                recv_sem=bin_sems.at[1, piece, slot],
                device_id={"bin": lax.rem(my_bin + slot, bin_size)},
                device_id_type=MESH,
            ).wait_recv()

    lane = lax.broadcasted_iota(jnp.int32, (rows, tile), 1)
    back = (lane >> 1) + (tile // 2) * (1 - (lane & 1))

    def finish(t):
        total = sum_ref[my_bin * cut + t].astype(jnp.float32)
        for slot in range(1, bin_size):
            total += bin_recv[slot, t].astype(jnp.float32)
        signal = (total * scale).astype(jnp.bfloat16).astype(jnp.float32)
        out_ref[:, t * tile:(t + 1) * tile] = take_lanes(signal, back)

    arrive(0)
    for t in range(1, spans - 1):
        finish(t)

    @pl.when(my_bin > 0)
    def _():
        arrive(1)

    @pl.when(my_bin < bin_size - 1)
    def _():
        arrive(2)

    finish(0)
    finish(spans - 1)
    each_piece(block_at(bin_size - 1), lambda copy: copy.wait_send())


def correlate_kernel(trials, signal_ref, taps_ref, out_hbm, power_ref, sems):
    _, templates, bins = power_ref.shape
    taps = taps_ref.shape[1] // 2
    group = math.gcd(trials, 2)

    pack = 16
    length = bins + taps

    def out_copy(g):
        at = pl.ds(g * group, group)
        return pltpu.make_async_copy(power_ref.at[at], out_hbm.at[at], sems.at[g])

    def one_group(g, _):
        for t in range(group):
            trial = g * group + t
            hankel = []
            for part in (0, 1):
                line = signal_ref[pl.ds(part * trials + trial, 1), :]
                line = jnp.broadcast_to(line, (pack, length)).astype(jnp.bfloat16)
                rows = [
                    pltpu.roll(line, length + pack * a - (LANES - 1), 1, stride=1, stride_axis=0)
                    for a in range(LANES // pack)
                ]
                hankel.append(jnp.concatenate(rows, 0))
            wide = jnp.concatenate(
                [
                    hankel[part][:, u * LANES:u * LANES + bins]
                    for part in (0, 1)
                    for u in range(taps // LANES)
                ],
                0,
            )
            response = jnp.dot(taps_ref[...], wide, preferred_element_type=jnp.float32)
            real = response[:templates]
            imag = response[templates:]
            power_ref[trial] = (real * real + imag * imag).astype(power_ref.dtype)
        out_copy(g).start()
        return 0

    for g in range(trials // group):
        one_group(g, 0)
    for g in range(trials // group):
        out_copy(g).wait()


def local(spectra, dm_trials, chan_delay, template_bank, template_ids):
    chans, bins = spectra.shape[1:]
    samples = 2 * bins
    bin_size = lax.axis_size("bin")
    chan_size = lax.axis_size("chan")
    trials = dm_trials.shape[0] // chan_size
    templates = template_ids.shape[0]
    taps = template_bank.shape[2]
    own = bins // bin_size
    width = own + 2 * EDGE
    scale = 1.0 / math.sqrt(chan_delay.shape[0])
    if chans % LANES:
        rank = lax.axis_index("chan") * bin_size + lax.axis_index("bin")
        chan_delay = lax.dynamic_slice_in_dim(chan_delay, rank * chans, chans)
    vmem = pl.BlockSpec(memory_space=pltpu.VMEM)
    products = pltpu.VMEM((2 * LANES, 2 * min(bins, 1024)), jnp.float32)

    paired = (
        bins <= 1024 and bins % (4 * LANES) == 0 and own == 2 * LANES and chans % LANES == 0
        and trials * 2 * chan_size == LANES and chan_size % 2 == 0
    )
    if paired:
        hbm = pl.BlockSpec(memory_space=pltpu.HBM)
        signal, chosen = pl.pallas_call(
            functools.partial(paired_kernel, samples, scale),
            out_shape=[
                jax.ShapeDtypeStruct((2 * trials, width), jnp.float32),
                jax.ShapeDtypeStruct((2 * templates, 2 * taps), jnp.bfloat16),
            ],
            in_specs=[hbm] * 5,
            out_specs=[vmem] * 2,
            scratch_shapes=[
                pltpu.VMEM((2, chans, bins), jnp.bfloat16),
                pltpu.VMEM((1, chans), jnp.int32),
                pltpu.VMEM((1, dm_trials.shape[0]), jnp.int32),
                pltpu.VMEM(template_bank.shape, jnp.bfloat16),
                pltpu.VMEM((1, templates), jnp.int32),
                pltpu.VMEM((chan_size, bins // LANES, 2 * trials, LANES), jnp.bfloat16),
                pltpu.VMEM((bins // LANES + 2, 2 * trials, LANES), jnp.bfloat16),
                pltpu.VMEM((chan_size, bins // LANES, 2 * trials, LANES), jnp.bfloat16),
                pltpu.VMEM((bin_size, width // LANES, 2 * trials, LANES), jnp.bfloat16),
                pltpu.VMEM((4, LANES, chans), jnp.float32),
                pltpu.VMEM((2 * bins, chans), jnp.bfloat16),
                pltpu.VMEM((own, own), jnp.bfloat16),
                pltpu.VMEM((2 * LANES, 2 * bins), jnp.bfloat16),
                pltpu.VMEM((2 * LANES, bins), jnp.bfloat16),
                pltpu.SemaphoreType.DMA((4 + bin_size,)),
                pltpu.SemaphoreType.DMA((2, chan_size, bin_size)),
                pltpu.SemaphoreType.DMA((2, 3, bin_size)),
            ],
            compiler_params=pltpu.CompilerParams(
                collective_id=0, has_side_effects=True, vmem_limit_bytes=24 * 2 ** 20
            ),
            name="dedisperse",
        )(*[
            pltpu.with_memory_space_constraint(x, pltpu.HBM)
            for x in (
                spectra, chan_delay[None, :], dm_trials[None, :], template_bank,
                template_ids[None, :],
            )
        ])
    else:
        signal = pl.pallas_call(
            functools.partial(dedisperse_kernel, samples, scale),
            out_shape=jax.ShapeDtypeStruct((2 * trials, width), jnp.float32),
            in_specs=[vmem] * 3,
            out_specs=vmem,
            scratch_shapes=[
                pltpu.VMEM((chan_size, 2 * trials, bins), jnp.bfloat16),
                pltpu.VMEM((2 * trials, bins + 2 * EDGE), jnp.bfloat16),
                pltpu.VMEM((chan_size, 2 * trials, bins), jnp.bfloat16),
                pltpu.VMEM((bin_size, 2 * trials, width), jnp.bfloat16),
                pltpu.VMEM((chans, 2 * bins), jnp.bfloat16),
                pltpu.VMEM((chans, bins), jnp.bfloat16),
                pltpu.VMEM((own, own), jnp.bfloat16),
                pltpu.VMEM((own, own), jnp.bfloat16),
                products,
                products,
                pltpu.SemaphoreType.DMA((2, chan_size, bin_size)),
                pltpu.SemaphoreType.DMA((2, 3, bin_size)),
            ],
            compiler_params=pltpu.CompilerParams(collective_id=0, has_side_effects=True),
            name="dedisperse",
        )(spectra, chan_delay[None, :], dm_trials[None, :])

        chosen = pl.pallas_call(
            build_taps,
            out_shape=jax.ShapeDtypeStruct((2 * templates, 2 * taps), jnp.bfloat16),
            in_specs=[vmem] * 2,
            out_specs=vmem,
            name="taps",
        )(template_bank, template_ids[None, :])

    return pl.pallas_call(
        functools.partial(correlate_kernel, trials),
        out_shape=jax.ShapeDtypeStruct((trials, templates, own), jnp.bfloat16),
        in_specs=[vmem] * 2,
        out_specs=pl.BlockSpec(memory_space=pltpu.HBM),
        scratch_shapes=[
            pltpu.VMEM((trials, templates, own), jnp.bfloat16),
            pltpu.SemaphoreType.DMA((trials,)),
        ],
        compiler_params=pltpu.CompilerParams(vmem_limit_bytes=16 * 2 ** 20),
        name="templates",
    )(signal, chosen)


def solution(mesh):
    in_specs = (P(None, ("beam", "chan", "bin"), None), P(), P(), P(), P())
    out_specs = P(("beam", "chan"), None, "bin")
    return jax.shard_map(local, mesh=mesh, in_specs=in_specs, out_specs=out_specs, check_vma=False)
```
